32 devices in a mesh: dp: 4 (over x, core), expert: 8 (over z, y).
Axes of the slice: x: 2, y: 2, z: 4, core: 2. Of those that a mesh axis runs over, the one named last changes fastest.
Arguments:
- hidden_in: bfloat16 [32, 512, 1024], P(('dp', 'expert')), may hold values from -6 to 6
- segment_ids: int32 [32, 512], P(('dp', 'expert')), may hold values from 0 to 15, never falling along the last dimension, each value on 1 to 256 neighbouring positions
- head_experts: int32 [32, 512, 4, 2], P(('dp', 'expert')), may hold values from 0 to 4, all different within a row
- token_experts: int32 [32, 512, 16], P(('dp', 'expert')), may hold values from 0 to 95, all different within a row; in each aligned block of 512 rows (0 to 511, 512 to 1023, ..., all dimensions but the last counted through in order) at most 96 rows name the same one
- attention_gain: float32 [1024], replicated, may hold values from 0.5 to 1.5
- query_weight: bfloat16 [1024, 512], replicated, may hold values from -0.1875 to 0.1875
- key_weight: bfloat16 [1024, 512], replicated, may hold values from -0.1875 to 0.1875
- value_weight: bfloat16 [1024, 2560], replicated, may hold values from -0.1875 to 0.1875
- value_selector: bfloat16 [1024, 20], replicated, may hold values from -0.09375 to 0.09375
- output_selector: bfloat16 [1024, 20], replicated, may hold values from -0.09375 to 0.09375
- output_weight: bfloat16 [2560, 1024], replicated, may hold values from -1.5 to 1.5
- mixture_gain: float32 [1024], replicated, may hold values from 0.5 to 1.5
- router_weight: bfloat16 [1024, 96], replicated, may hold values from -0.09375 to 0.09375
- up_weight: bfloat16 [96, 1024, 128], P(('dp', 'expert')), may hold values from -0.1875 to 0.1875
- down_weight: bfloat16 [96, 128, 1024], P(('dp', 'expert')), may hold values from -0.375 to 0.375
- expert_counts: int32 [96], replicated, may hold values from 0 to 999
- output_cotangent: bfloat16 [32, 512, 1024], P(('dp', 'expert')), may hold values from -6 to 6
Outputs:
- hidden_out: bfloat16 [32, 512, 1024], P(('dp', 'expert'))
- grad_input: float32 [32, 512, 1024], P(('dp', 'expert'))
- grad_attention_gain: float32 [1024], replicated
- grad_query_weight: float32 [1024, 512], replicated
- grad_key_weight: float32 [1024, 512], replicated
- grad_value_weight: float32 [1024, 2560], replicated
- grad_value_selector: float32 [1024, 20], replicated
- grad_output_selector: float32 [1024, 20], replicated
- grad_output_weight: float32 [2560, 1024], replicated
- grad_mixture_gain: float32 [1024], replicated
- grad_router_weight: float32 [1024, 96], replicated
- grad_up_weight: float32 [96, 1024, 128], P(('dp', 'expert'))
- grad_down_weight: float32 [96, 128, 1024], P(('dp', 'expert'))
- new_counts: int32 [96], replicated
The draws below stay inside these ranges and needn't reach their ends.
Inputs may be any that keep to these rules, and one draw needn't show every extreme that they name: `token_experts`: each token names 16 different experts; the 512 tokens of one row (one device) name no expert more than 96 times, a bound that some block reaches. `segment_ids`: within a row the numbers never fall; each of the 16 documents covers 1 to 256 tokens, one exactly 256. `head_experts`: the 2 experts of a token's head differ.
All inputs are finite; a program needn't handle non-finite values.
Results may differ from the reference program's by a relative error of at most 0.012.
Values may be sent and summed in bfloat16 or wider, within the bound.
No kernel may reach another device: no remote copies, remote signals or barrier semaphores. Data moves between devices by JAX's collectives and lax.ppermute only.
A program may use at most 320 MiB of HBM per device.

```python
import math
import jax
import jax.numpy as jnp
import numpy as np
from jax import lax

D = 1024
H = 4
DH = 128
NE = 5
FF = 128
ATOP = 2
TOPK = 16
TOK_DEV = 512
DOCS = 16
DOC_MOST = 256
ROWS = 32
EXPERTS = 96
MOST = 96


def set_ends(entries, stream_key, low, high):
    extent = entries.shape
    spot = [jax.random.randint(jax.random.fold_in(stream_key, axis), (), 0, extent[axis]) for axis in range(len(extent))]
    entries = entries.at[tuple(spot)].set(low)
    longest = extent.index(max(extent))
    spot[longest] = (spot[longest] + 1) % extent[longest]
    return entries.at[tuple(spot)].set(high)


def steps_of(stream_key, dims, cuts, smallest, largest):
    def one(axis_at, blocks):
        steps = jax.random.uniform(jax.random.fold_in(jax.random.fold_in(stream_key, 6), axis_at), (blocks,), jnp.float32, smallest / len(cuts), largest / len(cuts))
        return jnp.repeat(jnp.exp(steps), dims[axis_at] // blocks).reshape((-1,) + (1,) * (len(dims) - axis_at - 1))

    loudness = one(*cuts[0])
    for cut in cuts[1:]:
        loudness = loudness * one(*cut)
    return loudness


def choose_distinct(stream_key, rows, count, top, lift):
    sequence = jax.random.permutation(jax.random.fold_in(stream_key, 1), count)
    boost = sequence
    for power in range(3):
        boost = boost * boost // count
    boost = boost * lift // count
    chance = jax.random.randint(jax.random.fold_in(stream_key, 2), (rows, count), 0, 4096) + boost
    sure = jax.random.permutation(jax.random.fold_in(stream_key, 3), rows)[jnp.arange(count) % rows]
    chance = jnp.where(jnp.arange(rows)[:, None] == sure[None, :], 1 << 14, chance)
    merit = chance * count + jnp.arange(count)
    return lax.top_k(merit.astype(jnp.int32), top)[1].astype(jnp.int32)


def length_profile(number_of, total, limit, slope):
    portions = [(1 << 20) // math.isqrt(rank ** slope) + 1 for rank in range(2, number_of + 1)]
    rest, holding = total - limit - (number_of - 1), [1] * (number_of - 1)
    while rest > 0:
        free = [i for i in range(number_of - 1) if holding[i] < limit]
        pool, left = sum([portions[i] for i in free]), rest
        for i in free:
            addition = min(limit - holding[i], max(1, left * portions[i] // pool), rest)
            holding[i] = holding[i] + addition
            rest = rest - addition
    return np.array([limit] + holding)


def ragged_sizes(stream_key, amount, total, reach, lean):
    if amount == 2:
        one = jax.random.randint(stream_key, (), max(1, total - reach), min(reach, total - 1) + 1)
        return jnp.stack([one, total - one])
    lengths = jnp.asarray(length_profile(amount, total, reach, lean), jnp.int32)
    couples = (amount - 1) // 2
    source_of, sink = lengths[1:1 + 2 * couples:2], lengths[2:2 + 2 * couples:2]
    room = jnp.minimum(source_of - 1, reach - sink)
    passed = jax.random.randint(jax.random.fold_in(stream_key, 1), (couples,), 0, 1 << 20) % (room + 1)
    lengths = lengths.at[1:1 + 2 * couples:2].set(source_of - passed).at[2:2 + 2 * couples:2].set(sink + passed)
    return lengths[jax.random.permutation(jax.random.fold_in(stream_key, 2), amount)]


def deal_out(key, own, number, rows, count, top, most, lean):
    ranking = jax.random.permutation(key, count)
    packed, common = portions_of(count, rows * top, most, lean, True), portions_of(count, rows * top, most, lean, False)
    places = jnp.arange(count)

    def named(sizes, offset_by):
        used = int((sizes > 0).sum())
        fixed = max(1, used // 4)
        moved = fixed + (places - fixed + offset_by * (used - fixed)) % max(1, count - fixed)
        return jnp.zeros((count,), jnp.int32).at[ranking[jnp.where(places < fixed, places, moved)]].set(jnp.asarray(sizes, jnp.int32))

    sizes = jnp.where(number % 4 == 0, named(packed, number // 4), named(common, number - number // 4 - 1))
    mixed = jax.random.permutation(jax.random.fold_in(own, 3), count)
    source_of, receiver = mixed[0:count // 2 * 2:2], mixed[1:count // 2 * 2:2]
    margin = jnp.minimum(sizes[source_of] - 1, most - sizes[receiver]) // 2
    margin = jnp.where((source_of == ranking[0]) | (receiver == ranking[0]) | (sizes[receiver] == 0), 0, jnp.maximum(margin, 0))
    moved = jax.random.randint(jax.random.fold_in(own, 4), (count // 2,), 0, 1 << 20) % (margin + 1)
    sizes = sizes.at[source_of].add(-moved).at[receiver].add(moved)
    items = jnp.searchsorted(jnp.cumsum(sizes), jnp.arange(rows * top), side="right").astype(jnp.int32)
    table = items.reshape(top, rows).T
    table = table[jax.random.permutation(jax.random.fold_in(own, 1), rows)]
    offset_by = jax.random.randint(jax.random.fold_in(own, 2), (rows, 1), 0, top)
    return jnp.take_along_axis(table, (jnp.arange(top)[None, :] + offset_by) % top, axis=1)


def portions_of(amount, total, most, skew, full):
    loads = [(1 << 20) // math.isqrt(grade ** skew) + 1 for grade in range(1, amount + 1)]
    largest = most if full else min(most, max(-(-total // amount), total * loads[0] // sum(loads)))
    least = 1 if total - largest >= amount - 1 else 0
    holding, surplus = [largest] + [least] * (amount - 1), total - largest - least * (amount - 1)
    while surplus > 0:
        movable = [i for i in range(1, amount) if holding[i] < largest] or [i for i in range(1, amount) if holding[i] < most]
        whole, remaining = sum([loads[i] for i in movable]), surplus
        for i in movable:
            addition = min(most - holding[i], max(1, remaining * loads[i] // whole), surplus)
            holding[i] = holding[i] + addition
            surplus = surplus - addition
    return np.array(holding)


def normal_values(stream_key, shape, scale, reach, split=(), kind=jnp.bfloat16):
    drawn = jax.random.normal(stream_key, shape, jnp.float32) * scale
    if len(split) > 0:
        drawn = steps_of(stream_key, shape, split, -0.22, 0.18) * drawn
    return jnp.clip(drawn, min=-reach, max=reach).astype(kind)


def setup_inputs(seed: int = 0) -> dict:
    key_list = jax.random.split(jax.random.key(seed), 18)
    hidden_in = normal_values(key_list[0], (ROWS, TOK_DEV, D), 1.0, 6.0, ((0, 32),))
    segment_ids = jax.vmap(lambda own: jnp.searchsorted(jnp.cumsum(ragged_sizes(own, DOCS, TOK_DEV, DOC_MOST, 2)), jnp.arange(TOK_DEV), side="right"))(jax.random.split(key_list[1], ROWS)).reshape((ROWS, TOK_DEV)).astype(jnp.int32)
    head_experts = choose_distinct(key_list[2], ROWS * TOK_DEV * H, NE, ATOP, 0).reshape((ROWS, TOK_DEV, H, ATOP))
    token_experts_keys = jax.random.split(jax.random.fold_in(key_list[3], 1), ROWS * TOK_DEV // TOK_DEV)
    token_experts_turns = jax.random.permutation(jax.random.fold_in(key_list[3], 3), ROWS * TOK_DEV // TOK_DEV)
    token_experts = jax.vmap(lambda own, number: deal_out(jax.random.fold_in(key_list[3], 2), own, number, TOK_DEV, EXPERTS, TOPK, MOST, 1))(token_experts_keys, token_experts_turns).reshape((ROWS, TOK_DEV, TOPK))
    attention_gain = jnp.clip(1.0 + 0.1 * jax.random.normal(key_list[4], (D,), jnp.float32), 0.5, 1.5)
    query_weight = normal_values(key_list[5], (D, H * DH), D ** -0.5, 0.1875)
    key_weight = normal_values(key_list[6], (D, H * DH), D ** -0.5, 0.1875)
    value_weight = normal_values(key_list[7], (D, H * NE * DH), D ** -0.5, 0.1875)
    value_selector = normal_values(key_list[8], (D, H * NE), (4 * D) ** -0.5, 0.09375)
    output_selector = normal_values(key_list[9], (D, H * NE), (4 * D) ** -0.5, 0.09375)
    output_weight = normal_values(key_list[10], (H * NE * DH, D), (DH // 8) ** -0.5, 1.5)
    mixture_gain = jnp.clip(1.0 + 0.1 * jax.random.normal(key_list[11], (D,), jnp.float32), 0.5, 1.5)
    router_weight = normal_values(key_list[12], (D, EXPERTS), (4 * D) ** -0.5, 0.09375)
    up_weight = normal_values(key_list[13], (EXPERTS, D, FF), D ** -0.5, 0.1875, ((0, 32),))
    down_weight = normal_values(key_list[14], (EXPERTS, FF, D), (2 * FF) ** -0.5, 0.375, ((0, 32),))
    expert_counts = set_ends(jax.random.randint(key_list[15], (EXPERTS,), 0, 1000), jax.random.fold_in(key_list[15], 1), 0, 999).astype(jnp.int32)
    output_cotangent = normal_values(key_list[16], (ROWS, TOK_DEV, D), 1.0, 6.0, ((0, 32),))
    return dict(hidden_in=hidden_in, segment_ids=segment_ids, head_experts=head_experts, token_experts=token_experts, attention_gain=attention_gain, query_weight=query_weight, key_weight=key_weight, value_weight=value_weight, value_selector=value_selector, output_selector=output_selector, output_weight=output_weight, mixture_gain=mixture_gain, router_weight=router_weight, up_weight=up_weight, down_weight=down_weight, expert_counts=expert_counts, output_cotangent=output_cotangent)


epsilon = 1e-06
masked_value = -1e+30
highest = lax.Precision.HIGHEST

@jax.custom_vjp
def low(v):
    return lax.optimization_barrier(v.astype(jnp.bfloat16)).astype(jnp.float32)

@jax.custom_vjp
def low_back(v):
    return v

def low_keep(v):
    return (low(v), None)

def low_pass(kept, grad):
    return (grad,)

def back_keep(v):
    return (v, None)

def back_low(kept, grad):
    return (low(grad),)
low.defvjp(low_keep, low_pass)
low_back.defvjp(back_keep, back_low)

def rms_norm(values, gain):
    return values * lax.rsqrt(lax.optimization_barrier(jnp.mean(values * values, axis=-1, keepdims=True)) + epsilon) * gain

def attend_row(normed_low, segments, choices_row, query_weight, key_weight, value_weight, value_selector, output_selector):
    length = normed_low.shape[0]
    query = low(low_back(jnp.dot(normed_low, query_weight, precision=highest))).reshape(length, H, DH)
    keys = low(low_back(jnp.dot(normed_low, key_weight, precision=highest))).reshape(length, H, DH)
    values_all = low_back(jnp.dot(normed_low, value_weight, precision=highest)).reshape(length, H, NE, DH)
    chosen_mask = lax.optimization_barrier(jnp.sum((choices_row[:, :, :, None] == jnp.arange(NE, dtype=jnp.int32)).astype(jnp.float32), axis=2))
    value_gate = jax.nn.sigmoid(low_back(jnp.dot(normed_low, value_selector, precision=highest))).reshape(length, H, NE) * chosen_mask
    output_gate = jax.nn.sigmoid(low_back(jnp.dot(normed_low, output_selector, precision=highest))).reshape(length, H, NE) * chosen_mask
    value_low = low(lax.optimization_barrier(jnp.sum(value_gate[..., None] * values_all, axis=2)))
    positions = jnp.arange(length, dtype=jnp.int32)
    allowed = (positions[None, :] <= positions[:, None]) & (segments[None, :] == segments[:, None])
    scores = low_back(jnp.einsum('qhd,khd->hqk', query, keys, precision=highest) * DH ** (-0.5))
    scores = jnp.where(allowed[None], scores, masked_value)
    probs_low = low(jax.nn.softmax(scores, axis=-1))
    mixed = low_back(jnp.einsum('hqk,khd->qhd', probs_low, value_low, precision=highest))
    return low(output_gate[..., None] * mixed[:, :, None, :]).reshape(length, H * NE * DH)

def experts_row(moe_low, chosen, gate_values, up_weight, down_weight):
    length = moe_low.shape[0]
    experts = up_weight.shape[0]
    pair_ids = chosen.reshape(-1)
    one_hot = (pair_ids[:, None] == jnp.arange(experts, dtype=jnp.int32)[None, :]).astype(jnp.int32)
    rank_in = lax.optimization_barrier(jnp.sum((jnp.cumsum(one_hot, axis=0, dtype=jnp.int32) - one_hot) * one_hot, axis=1, dtype=jnp.int32))
    slot_index = pair_ids * MOST + rank_in
    pair_count = length * TOPK
    slot_token = jnp.full((experts * MOST,), length, jnp.int32).at[slot_index].set(jnp.arange(pair_count, dtype=jnp.int32) // TOPK)
    padded_rows = jnp.concatenate([moe_low, jnp.zeros((1, moe_low.shape[1]), jnp.float32)], axis=0)
    rows_in = low_back(padded_rows[slot_token]).reshape(experts, MOST, moe_low.shape[1])
    hidden = low(jax.nn.gelu(low_back(jnp.einsum('emd,edf->emf', rows_in, up_weight, precision=highest)), approximate=True))
    produced = low_back(low(jnp.einsum('emf,efd->emd', hidden, down_weight, precision=highest))).reshape(experts * MOST, moe_low.shape[1])
    picked = produced[slot_index].reshape(length, TOPK, moe_low.shape[1])
    return lax.optimization_barrier(jnp.sum(gate_values[:, :, None] * picked, axis=1))

def forward(params, segment_ids, head_experts, token_experts):
    inputs, attention_gain, query_weight, key_weight, value_weight, value_selector, output_selector, output_weight, mixture_gain, router_weight, up_weight, down_weight = params
    normed_low = low(rms_norm(inputs, attention_gain))

    def attend_one(item):
        return attend_row(item[0], item[1], item[2], query_weight, key_weight, value_weight, value_selector, output_selector)
    spread = lax.map(jax.checkpoint(attend_one), (normed_low, segment_ids, head_experts))
    middle = inputs + low_back(jnp.einsum('rtc,cd->rtd', spread, output_weight, precision=highest))
    moe_low = low(rms_norm(middle, mixture_gain))
    logits = low_back(jnp.einsum('rtd,de->rte', moe_low, router_weight, precision=highest))
    gate_values = jax.nn.sigmoid(jnp.take_along_axis(logits, token_experts, axis=2))

    def experts_one(item):
        return experts_row(item[0], item[1], item[2], up_weight, down_weight)
    moe_out = lax.map(jax.checkpoint(experts_one), (moe_low, token_experts, gate_values))
    return middle + moe_out

def row_counts(chosen):
    hits = (chosen.reshape(-1)[:, None] == jnp.arange(EXPERTS, dtype=jnp.int32)[None, :]).astype(jnp.int32)
    return lax.optimization_barrier(jnp.sum(hits, axis=0, dtype=jnp.int32))

def reference(hidden_in, segment_ids, head_experts, token_experts, attention_gain, query_weight, key_weight, value_weight, value_selector, output_selector, output_weight, mixture_gain, router_weight, up_weight, down_weight, expert_counts, output_cotangent):
    floats = (hidden_in, attention_gain, query_weight, key_weight, value_weight, value_selector, output_selector, output_weight, mixture_gain, router_weight, up_weight, down_weight)
    floats = tuple((item.astype(jnp.float32) for item in floats))

    def run(*params):
        return forward(params, segment_ids, head_experts, token_experts)
    output, pullback = jax.vjp(run, *floats)
    grads = pullback(output_cotangent.astype(jnp.float32))
    counted = lax.optimization_barrier(jnp.sum(lax.map(row_counts, token_experts), axis=0, dtype=jnp.int32))
    return (output.astype(jnp.bfloat16), grads[0], grads[1], grads[2], grads[3], grads[4], grads[5], grads[6], grads[7], grads[8], grads[9], grads[10], grads[11], expert_counts + counted)
```

```python
import functools

import jax
import jax.numpy as jnp
from jax import lax
from jax.experimental import pallas as pl
from jax.experimental.pallas import tpu as pltpu
from jax.sharding import PartitionSpec as P

D = 1024
H = 4
DH = 128
NE = 5
FF = 128
TOPK = 16
GATE_LANES = 16

epsilon = 1e-06
masked_value = -1e30
bf16 = jnp.bfloat16
f32 = jnp.float32
tanh_scale = 0.7978845608028654
cubic = 0.044715


def inverse_rms(values):
    return lax.rsqrt(jnp.mean(values * values, axis=-1, keepdims=True) + epsilon)


def norm_back(values, scaling, gain, upstream):
    weighted = upstream * gain
    middle = jnp.mean(values * weighted, axis=-1, keepdims=True)
    return scaling * weighted - values * scaling * scaling * scaling * middle


def masked_scores(query_low, key_low, allowed):
    raw = jnp.einsum(
        "qhd,khd->hqk", query_low, key_low, preferred_element_type=f32
    ) * DH ** (-0.5)
    return jnp.where(allowed[None], raw, masked_value)


def weight_grad(left, right):
    return jnp.einsum("td,tc->dc", left, right, preferred_element_type=f32)


def input_term(delta, weight):
    return jnp.einsum("tc,dc->td", delta, weight, preferred_element_type=f32)


def contract(left, right, left_dim, right_dim):
    return lax.dot_general(
        left, right, (((left_dim,), (right_dim,)), ((), ())), preferred_element_type=f32
    )


def experts_kernel(blocks, pairs, chained, opened, closed, *refs):
    refs = list(refs)

    def take(count):
        taken = refs[:count]
        del refs[:count]
        return taken

    x_hbm, u_hbm, m_hbm = take(blocks), take(blocks), take(blocks)
    select_ref, router_ref = take(2)
    weights = (take(4), take(4))
    y_prev, dx_prev = take(2) if chained else (None, None)
    gu_prev, gd_prev, gr_prev = take(3) if opened else (None, None, None)
    y_ref, dx_ref = take(2)
    grads = take(4) if closed else take(2)
    (gr_ref,) = take(1)
    (x_buf, u_buf, m_buf, sems, w_up, w_down, w_sems) = take(7)
    (y_acc, dx_acc, gup, gdown, x_turned, gate, delta, gr_acc) = refs
    step = pl.program_id(0)
    pair = pl.program_id(1)
    slot = lax.rem(step, 2)
    local = pairs // 2

    def copies(index, place):
        return (
            pltpu.make_async_copy(x_hbm[index], x_buf.at[place], sems.at[place, 0]),
            pltpu.make_async_copy(u_hbm[index], u_buf.at[place], sems.at[place, 1]),
            pltpu.make_async_copy(m_hbm[index], m_buf.at[place], sems.at[place, 2]),
        )

    def weight_copies(index):
        place = index % 2
        k = index % local
        up_a, up_b, down_a, down_b = weights[index // local]
        return (
            pltpu.make_async_copy(up_a.at[k], w_up.at[place, 0], w_sems.at[place, 0]),
            pltpu.make_async_copy(up_b.at[k], w_up.at[place, 1], w_sems.at[place, 1]),
            pltpu.make_async_copy(
                down_a.at[k], w_down.at[place, pl.ds(0, FF)], w_sems.at[place, 2]
            ),
            pltpu.make_async_copy(
                down_b.at[k], w_down.at[place, pl.ds(FF, FF)], w_sems.at[place, 3]
            ),
        )

    @pl.when(jnp.logical_and(step == 0, pair == 0))
    def _():
        for copy in (*copies(0, 0), *weight_copies(0)):
            copy.start()

    for index in range(pairs):

        @pl.when(pair == index)
        def _():
            for copy in weight_copies(index):
                copy.wait()
            if index + 1 < pairs:
                for copy in weight_copies(index + 1):
                    copy.start()
            elif blocks > 1:

                @pl.when(step < blocks - 1)
                def _():
                    for copy in weight_copies(0):
                        copy.start()

    @pl.when(pair == 0)
    def _():
        for number in range(blocks):
            place = number % 2

            @pl.when(step == number)
            def _():
                for copy in copies(number, place):
                    copy.wait()
                if number + 1 < blocks:
                    for copy in copies(number + 1, 1 - place):
                        copy.start()

        x = x_buf[slot]
        x_turned[...] = x.T
        logits = jnp.dot(x, router_ref[...], preferred_element_type=f32)
        chosen = jnp.dot(m_buf[slot], select_ref[...], preferred_element_type=f32)
        gate[...] = jax.nn.sigmoid(logits) * chosen
        delta[...] = jnp.zeros_like(delta)

    x = x_buf[slot]
    u = u_buf[slot]
    tokens = x.shape[0]
    which = lax.rem(pair, 2)
    up = jnp.concatenate([w_up[which, 0], w_up[which, 1]], axis=1)
    down = w_down[which]
    pre_act = jnp.dot(x, up, preferred_element_type=f32)
    pulled = contract(u, down, 1, 1)
    lanes = lax.broadcasted_iota(jnp.int32, gate.shape, 1)
    gates = gate[...]
    gate_a = jnp.sum(jnp.where(lanes == pair, gates, 0.0), axis=1, keepdims=True)
    gate_b = jnp.sum(jnp.where(lanes == pairs + pair, gates, 0.0), axis=1, keepdims=True)
    spread_gate = jnp.concatenate(
        [jnp.broadcast_to(gate_a, (tokens, FF)), jnp.broadcast_to(gate_b, (tokens, FF))], axis=1
    )
    square = pre_act * pre_act
    bent = jnp.tanh(tanh_scale * pre_act * (1.0 + cubic * square))
    hidden = (0.5 * pre_act * (1.0 + bent)).astype(bf16).astype(f32)
    slope = 0.5 * (1.0 + bent) + 0.5 * pre_act * (1.0 - bent * bent) * (
        tanh_scale * (1.0 + 3.0 * cubic * square)
    )
    felt = hidden * pulled
    felt_a = jnp.sum(felt[:, :FF], axis=1, keepdims=True)
    felt_b = jnp.sum(felt[:, FF:], axis=1, keepdims=True)
    kept = jnp.where(lanes == pair, felt_a, delta[...])
    delta[...] = jnp.where(lanes == pairs + pair, felt_b, kept)
    gated = (spread_gate * hidden).astype(bf16)
    hidden_delta = (spread_gate * pulled * slope).astype(bf16)
    y_new = jnp.dot(gated, down, preferred_element_type=f32)
    dx_new = contract(hidden_delta, up, 1, 1)
    gd_new = contract(gated, u, 0, 0)
    gu_new = jnp.dot(x_turned[...], hidden_delta, preferred_element_type=f32)

    @pl.when(pair == 0)
    def _():
        if chained:
            y_acc[...] = y_prev[...].astype(f32) + y_new
            dx_acc[...] = dx_prev[...].astype(f32) + dx_new
        else:
            y_acc[...] = y_new
            dx_acc[...] = dx_new

    @pl.when(pair > 0)
    def _():
        y_acc[...] += y_new
        dx_acc[...] += dx_new

    if blocks == 1:
        if opened:
            gd_new = gd_prev[0] + gd_new
            gu_new = gu_prev[0] + gu_new
        gd_now, gu_now = gd_new, gu_new
    else:

        @pl.when(step == 0)
        def _():
            if opened:
                gdown[pair] = gd_prev[0] + gd_new
                gup[pair] = gu_prev[0] + gu_new
            else:
                gdown[pair] = gd_new
                gup[pair] = gu_new

        @pl.when(step > 0)
        def _():
            gdown[pair] += gd_new
            gup[pair] += gu_new

        gd_now, gu_now = None, None

    @pl.when(step == blocks - 1)
    def _():
        gu_out = gup[pair] if gu_now is None else gu_now
        gd_out = gdown[pair] if gd_now is None else gd_now
        if closed:
            grads[0][0] = gu_out[:, :FF].astype(bf16)
            grads[1][0] = gu_out[:, FF:].astype(bf16)
            grads[2][0] = gd_out[:FF].astype(bf16)
            grads[3][0] = gd_out[FF:].astype(bf16)
        else:
            grads[0][0] = gu_out
            grads[1][0] = gd_out

    @pl.when(pair == pairs - 1)
    def _():
        gates_now = gate[...]
        logit_delta = (delta[...] * gates_now * (1.0 - gates_now)).astype(bf16)
        y_ref[...] = y_acc[...].astype(bf16)
        dx_ref[...] = (dx_acc[...] + contract(logit_delta, router_ref[...], 1, 1)).astype(bf16)
        gr_new = jnp.dot(x_turned[...], logit_delta, preferred_element_type=f32)

        @pl.when(step == 0)
        def _():
            if opened:
                gr_acc[...] = gr_prev[...] + gr_new
            else:
                gr_acc[...] = gr_new

        @pl.when(step > 0)
        def _():
            gr_acc[...] += gr_new

        @pl.when(step == blocks - 1)
        def _():
            gr_ref[...] = gr_acc[...]


def run_experts(xs, us, ms, select, router, first, second, previous, carried, finish):
    blocks = len(xs)
    local = first[0].shape[0]
    pairs = 2 * local
    tokens = xs[0].shape[0]
    experts = select.shape[0]

    def block(i, j):
        return (i, 0)

    def whole(i, j):
        return (0, 0)

    def opening(i, j):
        return (jnp.where(i == 0, j, pairs - 1), 0, 0)

    def closing(i, j):
        return (jnp.where(i == blocks - 1, j, 0), 0, 0)

    anywhere = pl.BlockSpec(memory_space=pl.ANY)
    in_specs = [anywhere] * (3 * blocks) + [
        pl.BlockSpec((experts, GATE_LANES), whole),
        pl.BlockSpec((D, GATE_LANES), whole),
        *[anywhere] * 8,
    ]
    operands = [*xs, *us, *ms, select, router, *first, *second]
    if previous is not None:
        in_specs += [pl.BlockSpec((tokens, D), block)] * 2
        operands += list(previous)
    if carried is not None:
        in_specs += [
            pl.BlockSpec((1, D, 2 * FF), opening),
            pl.BlockSpec((1, 2 * FF, D), opening),
            pl.BlockSpec((D, GATE_LANES), whole),
        ]
        operands += list(carried)
    out_shape = [jax.ShapeDtypeStruct((blocks * tokens, D), bf16)] * 2
    out_specs = [pl.BlockSpec((tokens, D), block)] * 2
    if finish:
        out_shape += [jax.ShapeDtypeStruct((pairs, D, FF), bf16)] * 2
        out_shape += [jax.ShapeDtypeStruct((pairs, FF, D), bf16)] * 2
        out_specs += [pl.BlockSpec((1, D, FF), closing)] * 2
        out_specs += [pl.BlockSpec((1, FF, D), closing)] * 2
    else:
        out_shape += [jax.ShapeDtypeStruct((pairs, D, 2 * FF), f32)]
        out_shape += [jax.ShapeDtypeStruct((pairs, 2 * FF, D), f32)]
        out_specs += [pl.BlockSpec((1, D, 2 * FF), closing), pl.BlockSpec((1, 2 * FF, D), closing)]
    out_shape.append(jax.ShapeDtypeStruct((D, GATE_LANES), f32))
    out_specs.append(pl.BlockSpec((D, GATE_LANES), whole))
    kept = pairs if blocks > 1 else 1
    return pl.pallas_call(
        functools.partial(
            experts_kernel, blocks, pairs, previous is not None, carried is not None, finish
        ),
        grid=(blocks, pairs),
        in_specs=in_specs,
        out_specs=out_specs,
        out_shape=out_shape,
        scratch_shapes=[
            pltpu.VMEM((2, tokens, D), bf16),
            pltpu.VMEM((2, tokens, D), bf16),
            pltpu.VMEM((2, tokens, experts), bf16),
            pltpu.SemaphoreType.DMA((2, 3)),
            pltpu.VMEM((2, 2, D, FF), bf16),
            pltpu.VMEM((2, 2 * FF, D), bf16),
            pltpu.SemaphoreType.DMA((2, 4)),
            pltpu.VMEM((tokens, D), f32),
            pltpu.VMEM((tokens, D), f32),
            pltpu.VMEM((kept, D, 2 * FF), f32),
            pltpu.VMEM((kept, 2 * FF, D), f32),
            pltpu.VMEM((D, tokens), bf16),
            pltpu.VMEM((tokens, GATE_LANES), f32),
            pltpu.VMEM((tokens, GATE_LANES), f32),
            pltpu.VMEM((D, GATE_LANES), f32),
        ],
        compiler_params=pltpu.CompilerParams(
            dimension_semantics=("arbitrary", "arbitrary"),
            vmem_limit_bytes=56 * 1024 * 1024,
        ),
        cost_estimate=pl.CostEstimate(
            flops=24 * blocks * tokens * D * FF * pairs,
            bytes_accessed=blocks * tokens * D * 12 + pairs * D * FF * 24,
            transcendentals=blocks * tokens * 2 * FF * pairs,
        ),
        name="experts",
    )(*operands)


class Moves:
    def __init__(self):
        self.dp = lax.axis_size("dp")
        self.ex = lax.axis_size("expert")
        self.nx = self.dp // 2
        self.nh = self.ex // 2
        self.dp_index = lax.axis_index("dp")
        self.ex_index = lax.axis_index("expert")
        self.core = self.dp_index % 2
        self.x = self.dp_index // 2
        self.lo = self.ex_index % 2
        self.hi = self.ex_index // 2
        steps = [(a, b) for a in range(self.nx) for b in range(2)]
        self.plane = sorted(steps, key=lambda s: ((s[0] > 0) + (s[1] > 0), s))

    def over_core(self, value):
        return lax.ppermute(value, "dp", [(i, i ^ 1) for i in range(self.dp)])

    def over_hi(self, value, by=1):
        pairs = [(i, (i // 2 + by) % self.nh * 2 + i % 2) for i in range(self.ex)]
        return lax.ppermute(value, "expert", pairs)

    def over_plane(self, value, offset, back=False):
        a, b = offset
        if back:
            a = (self.nx - a) % self.nx
        if a == 0:
            return lax.ppermute(value, "expert", [(i, i ^ b) for i in range(self.ex)])
        dp_to = [(i // 2 + a) % self.nx * 2 + i % 2 for i in range(self.dp)]
        if b == 0:
            return lax.ppermute(value, "dp", list(enumerate(dp_to)))
        pairs = [
            (i * self.ex + j, dp_to[i] * self.ex + (j ^ 1))
            for i in range(self.dp)
            for j in range(self.ex)
        ]
        return lax.ppermute(value, ("dp", "expert"), pairs)


def add_low(*terms):
    total = terms[0].astype(f32)
    for term in terms[1:]:
        total = total + term.astype(f32)
    return total.astype(bf16)


def tie(*values):
    return lax.optimization_barrier(values)


def copy_two(order_ref, value_a, value_b, out_a, out_b):
    out_a[...] = value_a[...]
    out_b[...] = value_b[...]


def in_relative_order(moves, value):
    nx, nh = moves.nx, moves.nh
    count = nx * 2 * nh
    rows = value.shape[0] // (2 * count)
    columns = value.shape[1]
    order = []
    for core in (moves.core, 1 - moves.core):
        for a, b in moves.plane:
            for h in range(nh):
                place = (moves.x + a) % nx * 2 + (moves.lo ^ b)
                order.append((core * nx * 2 + place) * nh + (moves.hi + h) % nh)
    order = jnp.stack(order).astype(jnp.int32)
    shape = jax.ShapeDtypeStruct((count, rows, columns), value.dtype)
    value = value.reshape(2 * count, rows, columns)
    outs = pl.pallas_call(
        copy_two,
        grid_spec=pltpu.PrefetchScalarGridSpec(
            num_scalar_prefetch=1,
            grid=(count,),
            in_specs=[
                pl.BlockSpec((1, rows, columns), lambda i, o: (o[i], 0, 0)),
                pl.BlockSpec((1, rows, columns), lambda i, o: (o[count + i], 0, 0)),
            ],
            out_specs=[pl.BlockSpec((1, rows, columns), lambda i, o: (i, 0, 0))] * 2,
        ),
        out_shape=[shape, shape],
        name="relative",
    )(order, value, value)
    return [out.reshape(count * rows, columns) for out in outs]


def in_place_order(moves, mine, theirs, widths):
    nx, nh = moves.nx, moves.nh
    count = nx * 2 * nh
    rows = mine[0].shape[0] // nh
    columns = mine[0].shape[1]
    order = []
    for core in (moves.core, 1 - moves.core):
        for a, b in moves.plane:
            for h in range(nh):
                place = (moves.x - a) % nx * 2 + (moves.lo ^ b)
                order.append((core * nx * 2 + place) * nh + (moves.hi - h) % nh)
    order = jnp.stack(order).astype(jnp.int32)

    def piece(index):
        return pl.BlockSpec(
            (1, rows, columns), lambda i, o: (jnp.clip(i - index * nh, 0, nh - 1), 0, 0)
        )

    pieces = [p.reshape(nh, rows, columns) for p in (*mine, *theirs)]
    outs = pl.pallas_call(
        functools.partial(place_pieces, nx * 4, nh, widths),
        grid_spec=pltpu.PrefetchScalarGridSpec(
            num_scalar_prefetch=1,
            grid=(2 * count,),
            in_specs=[piece(index) for index in range(nx * 4)],
            out_specs=[
                pl.BlockSpec((1, rows, width), lambda i, o: (o[i], 0, 0)) for width in widths
            ],
        ),
        out_shape=[jax.ShapeDtypeStruct((2 * count, rows, width), f32) for width in widths],
        name="assemble",
    )(order, *pieces)
    return [out.reshape(2 * count * rows, width) for out, width in zip(outs, widths)]


def place_pieces(pieces, nh, widths, order_ref, *refs):
    outs = refs[pieces:]
    step = pl.program_id(0)
    for index in range(pieces):

        @pl.when(step // nh == index)
        def _():
            start = 0
            for out, width in zip(outs, widths):
                out[...] = refs[index][:, :, start : start + width].astype(f32)
                start += width


class Sum:
    def __init__(self, moves, value, widths):
        self.moves = moves
        self.widths = widths
        self.held, self.away = in_relative_order(moves, value)

    def core(self):
        moves = self.moves
        got = moves.over_core(self.away)
        count = len(moves.plane)
        rows = got.shape[0] // count
        self.parts = [
            add_low(self.held[k * rows : (k + 1) * rows], got[k * rows : (k + 1) * rows])
            for k in range(count)
        ]

    def plane(self):
        moves = self.moves
        got = [moves.over_plane(p, s) for p, s in zip(self.parts[1:], moves.plane[1:])]
        nh = moves.nh
        rows = self.parts[0].shape[0] // nh
        terms = [self.parts[0], *got]
        self.parts = [
            add_low(*[term[h * rows : (h + 1) * rows] for term in terms]) for h in range(nh)
        ]

    def line(self):
        moves = self.moves
        got = [moves.over_hi(self.parts[h], h) for h in range(1, moves.nh)]
        self.total = add_low(self.parts[0], *got)

    def line_back(self):
        moves = self.moves
        got = [moves.over_hi(self.total, h) for h in range(1, moves.nh)]
        self.rows = jnp.concatenate([self.total, *got], axis=0)

    def plane_back(self):
        moves = self.moves
        self.mine = [self.rows] + [moves.over_plane(self.rows, s) for s in moves.plane[1:]]

    def core_back(self):
        moves = self.moves
        theirs = [moves.over_core(piece) for piece in self.mine]
        return in_place_order(moves, self.mine, theirs, self.widths)


def sum_small(moves, value):
    for axis, size in (("dp", moves.dp), ("expert", moves.ex)):
        span = 1
        while span < size:
            value = value + lax.ppermute(value, axis, [(i, i ^ span) for i in range(size)])
            span *= 2
    return value


def select_back(select):
    return select.T


def on_device(
    hidden_in,
    segment_ids,
    head_experts,
    token_experts,
    attention_gain,
    query_weight,
    key_weight,
    value_weight,
    value_selector,
    output_selector,
    output_weight,
    mixture_gain,
    router_weight,
    up_weight,
    down_weight,
    expert_counts,
    output_cotangent,
):
    moves = Moves()
    nx, nh = moves.nx, moves.nh
    length = hidden_in.shape[1]
    experts = router_weight.shape[1]
    local = up_weight.shape[0]
    expert_range = jnp.arange(experts, dtype=jnp.int32)

    chosen = token_experts[0]
    routed = jnp.sum((chosen[:, :, None] == expert_range[None, None, :]).astype(f32), axis=1)
    local_counts = jnp.sum(routed, axis=0)
    upstream_low = output_cotangent[0]
    near = [s for s in moves.plane[1:] if 0 in s]
    far = [s for s in moves.plane[1:] if 0 not in s]
    routed_low = routed.astype(bf16)

    ups, downs = [up_weight], [down_weight]
    ups.append(moves.over_hi(up_weight))
    downs.append(moves.over_hi(down_weight))
    us = {s: moves.over_plane(upstream_low, s) for s in near}
    ms = {s: moves.over_plane(routed_low, s) for s in moves.plane[1:]}

    inputs = hidden_in[0].astype(f32)
    att_rms = inverse_rms(inputs)
    normed_low = (inputs * att_rms * attention_gain).astype(bf16)
    query_low = (
        jnp.dot(normed_low, query_weight, preferred_element_type=f32)
        .astype(bf16)
        .reshape(length, H, DH)
    )
    key_low = (
        jnp.dot(normed_low, key_weight, preferred_element_type=f32)
        .astype(bf16)
        .reshape(length, H, DH)
    )
    values_all = jnp.dot(normed_low, value_weight, preferred_element_type=f32).reshape(
        length, H, NE, DH
    )
    value_sigmoid = jax.nn.sigmoid(
        jnp.dot(normed_low, value_selector, preferred_element_type=f32)
    ).reshape(length, H, NE)
    output_sigmoid = jax.nn.sigmoid(
        jnp.dot(normed_low, output_selector, preferred_element_type=f32)
    ).reshape(length, H, NE)
    chosen_mask = jnp.sum(
        (head_experts[0][:, :, :, None] == jnp.arange(NE, dtype=jnp.int32)).astype(f32),
        axis=2,
    )
    value_gate = value_sigmoid * chosen_mask
    output_gate = output_sigmoid * chosen_mask
    value_low = jnp.sum(value_gate[..., None] * values_all, axis=2).astype(bf16)
    positions = jnp.arange(length, dtype=jnp.int32)
    segments = segment_ids[0]
    allowed = (positions[None, :] <= positions[:, None]) & (segments[None, :] == segments[:, None])
    scores = masked_scores(query_low, key_low, allowed)
    log_total = jax.nn.logsumexp(scores, axis=-1, keepdims=True)
    probs_low = jnp.exp(scores - log_total).astype(bf16)
    mixed_heads = jnp.einsum("hqk,khd->qhd", probs_low, value_low, preferred_element_type=f32)
    spread_low = (
        (output_gate[..., None] * mixed_heads[:, :, None, :])
        .astype(bf16)
        .reshape(length, H * NE * DH)
    )
    middle_rows = inputs + jnp.dot(spread_low, output_weight, preferred_element_type=f32)
    moe_rms = inverse_rms(middle_rows)
    moe_low = (middle_rows * moe_rms * mixture_gain).astype(bf16)

    moe_low, ups[1], downs[1] = tie(moe_low, ups[1], downs[1])
    home = moves.plane[0]
    xs = {home: moe_low}
    us[home] = upstream_low
    ms[home] = routed_low
    for s in near:
        xs[s] = moves.over_plane(moe_low, s)
    core_ups = [moves.over_core(u) for u in ups[:2]]
    core_downs = [moves.over_core(d) for d in downs[:2]]
    ups.append(moves.over_hi(ups[1]))
    downs.append(moves.over_hi(downs[1]))

    def slot_weights(s):
        return (ups[s], core_ups[s], downs[s], core_downs[s])

    def selection(slots):
        columns = []
        for core in (0, 1):
            for s in slots:
                owner = (moves.dp_index ^ core) * moves.ex + (moves.hi - s) % nh * 2 + moves.lo
                columns += [owner * local + k for k in range(local)]
        columns += [jnp.int32(-1)] * (GATE_LANES - len(columns))
        select = (expert_range[:, None] == jnp.stack(columns)[None, :]).astype(bf16)
        return select, jnp.dot(router_weight, select, preferred_element_type=f32).astype(bf16)

    sums = {}
    router_sum = jnp.zeros((D, experts), f32)
    mine_slots, theirs_slots = [None] * nh, [None] * nh

    def visit(offsets, phase, carried, finish):
        slots = (2 * phase, 2 * phase + 1)
        select, router = chosen_by[phase]
        previous = None
        if offsets[0] in sums:
            joined = [sums[s] for s in offsets]
            previous = joined[0] if len(joined) == 1 else tuple(
                jnp.concatenate([j[w] for j in joined], axis=0) for w in (0, 1)
            )
        y, dx, *grads = run_experts(
            [xs[s] for s in offsets],
            [us[s] for s in offsets],
            [ms[s] for s in offsets],
            select,
            router,
            slot_weights(slots[0]),
            slot_weights(slots[1]),
            previous,
            carried,
            finish,
        )
        for k, s in enumerate(offsets):
            sums[s] = (y[k * length : (k + 1) * length], dx[k * length : (k + 1) * length])
        return grads

    phases = nh // 2
    chosen_by = [selection((2 * p, 2 * p + 1)) for p in range(phases)]
    held = None
    sent_back = {}
    for phase in range(phases):
        last = phase == phases - 1
        if phase == 0:
            calls = [[home], *[[s] for s in near], far]
        elif last:
            calls = [[s] for s in far] + [[s] for s in near] + [[home]]
        else:
            calls = [[home], *[[s] for s in near], far]
        grads = None
        for turn, offsets in enumerate(calls):
            grads = visit(offsets, phase, grads, turn == len(calls) - 1)
            if phase == 0 and turn == 0:
                values = tie(grads[0], moe_low, upstream_low, *[xs[s] for s in near])
                grads[0], far_x, far_u = values[:3]
                for s, value in zip(near, values[3:]):
                    xs[s] = value
                for s in far:
                    xs[s] = moves.over_plane(far_x, s)
                    us[s] = moves.over_plane(far_u, s)
            if phase == 0 and turn == 1 and nh > 2:
                grads[0], ups[2], downs[2] = tie(grads[0], ups[2], downs[2])
                for s in range(3, nh):
                    ups.append(moves.over_hi(ups[-1]))
                    downs.append(moves.over_hi(downs[-1]))
                core_ups.append(moves.over_core(ups[2]))
                core_downs.append(moves.over_core(downs[2]))
            if phase == 0 and turn == len(calls) - 2 and nh > 2:
                values = tie(grads[0], *ups[3:], *downs[3:])
                grads[0] = values[0]
                ups[3:] = values[1 : nh - 2]
                downs[3:] = values[nh - 2 :]
                core_ups += [moves.over_core(u) for u in ups[3:]]
                core_downs += [moves.over_core(d) for d in downs[3:]]
            if last and offsets != [home]:
                for s in offsets:
                    sent_back[s] = [moves.over_plane(v, s, back=True) for v in sums[s][::-1]]
        router_sum = router_sum + jnp.dot(
            grads[4].astype(bf16), select_back(chosen_by[phase][0]), preferred_element_type=f32
        )
        gu_mine, gu_theirs, gd_mine, gd_theirs = grads[:4]
        gu_got, gd_got = moves.over_core(gu_theirs), moves.over_core(gd_theirs)
        for k in range(2):
            s = 2 * phase + k
            cut = slice(k * local, (k + 1) * local)
            parts = [(gu_mine[cut], gu_got[cut]), (gd_mine[cut], gd_got[cut])]
            if s == 0:
                first_parts = parts
                continue
            if held is not None:
                parts = [(*p, moves.over_hi(h)) for p, h in zip(parts, held)]
            held = [add_low(*p) for p in parts]

    def token_sum(which):
        total = sums[home][1 - which].astype(f32)
        for s in moves.plane[1:]:
            total = total + sent_back[s][which].astype(f32)
        return total

    expert_delta = token_sum(0)

    upstream = upstream_low.astype(f32)
    middle_delta = upstream + norm_back(middle_rows, moe_rms, mixture_gain, expert_delta)
    grad_mixture = jnp.sum(expert_delta * middle_rows * moe_rms, axis=0)
    middle_low = middle_delta.astype(bf16)
    grad_output = jnp.einsum(
        "tc,td->cd", spread_low, middle_low, preferred_element_type=f32
    ).astype(bf16)
    spread_delta = jnp.einsum(
        "td,cd->tc", middle_low, output_weight, preferred_element_type=f32
    ).reshape(length, H, NE, DH)
    mixed_delta = jnp.sum(output_gate[..., None] * spread_delta, axis=2).astype(bf16)
    oselect_delta = (
        (
            jnp.sum(spread_delta * mixed_heads[:, :, None, :], axis=3)
            * chosen_mask
            * output_sigmoid
            * (1.0 - output_sigmoid)
        )
        .astype(bf16)
        .reshape(length, H * NE)
    )
    scores = masked_scores(query_low, key_low, allowed)
    probs_full = jnp.exp(scores - log_total)
    probs_again = probs_full.astype(bf16)
    weight_delta = jnp.einsum("qhd,khd->hqk", mixed_delta, value_low, preferred_element_type=f32)
    score_delta = (
        probs_full * (weight_delta - jnp.sum(probs_full * weight_delta, axis=-1, keepdims=True))
    ).astype(bf16)
    query_delta = (
        (
            jnp.einsum("hqk,khd->qhd", score_delta, key_low, preferred_element_type=f32)
            * DH ** (-0.5)
        )
        .astype(bf16)
        .reshape(length, H * DH)
    )
    key_delta = (
        (
            jnp.einsum("hqk,qhd->khd", score_delta, query_low, preferred_element_type=f32)
            * DH ** (-0.5)
        )
        .astype(bf16)
        .reshape(length, H * DH)
    )
    value_delta = jnp.einsum("hqk,qhd->khd", probs_again, mixed_delta, preferred_element_type=f32)
    values_delta = (
        (value_gate[..., None] * value_delta[:, :, None, :])
        .astype(bf16)
        .reshape(length, H * NE * DH)
    )
    vselect_delta = (
        (
            jnp.sum(value_delta[:, :, None, :] * values_all, axis=3)
            * chosen_mask
            * value_sigmoid
            * (1.0 - value_sigmoid)
        )
        .astype(bf16)
        .reshape(length, H * NE)
    )
    grad_value = weight_grad(normed_low, values_delta).astype(bf16)
    narrow = 2 * H * NE + experts
    padding = -narrow % 128
    grad_rest = jnp.concatenate(
        [
            weight_grad(normed_low, query_delta).astype(bf16),
            weight_grad(normed_low, key_delta).astype(bf16),
            jnp.concatenate(
                [
                    weight_grad(normed_low, vselect_delta),
                    weight_grad(normed_low, oselect_delta),
                    router_sum,
                    jnp.zeros((D, padding), f32),
                ],
                axis=1,
            ).astype(bf16),
        ],
        axis=1,
    )
    normed_delta = (
        input_term(query_delta, query_weight)
        + input_term(key_delta, key_weight)
        + input_term(values_delta, value_weight)
    )
    normed_delta = (
        normed_delta
        + input_term(vselect_delta, value_selector)
        + input_term(oselect_delta, output_selector)
    )
    input_delta = middle_delta + norm_back(inputs, att_rms, attention_gain, normed_delta)
    grad_attention = jnp.sum(normed_delta * inputs * att_rms, axis=0)
    out_sum = Sum(moves, grad_output, [D])
    value_sum = Sum(moves, grad_value, [H * NE * DH])
    rest_sum = Sum(moves, grad_rest, [H * DH, H * DH, narrow + padding])
    out_sum.core()
    out_sum.plane()
    value_sum.core()
    out_sum.line()
    value_sum.plane()
    out_sum.line_back()
    rest_sum.core()
    value_sum.line()
    rest_sum.plane()
    value_sum.line_back()
    rest_sum.line()
    out_sum.plane_back()
    rest_sum.line_back()
    (grad_output,) = out_sum.core_back()
    value_sum.plane_back()
    (grad_value,) = value_sum.core_back()
    rest_sum.plane_back()
    grad_query, grad_key, narrow_sum = rest_sum.core_back()
    grad_vselect = narrow_sum[:, : H * NE]
    grad_oselect = narrow_sum[:, H * NE : 2 * H * NE]
    grad_router = narrow_sum[:, 2 * H * NE : narrow]

    output_rows = middle_rows + token_sum(1)
    grad_up, grad_down = (
        moves.over_hi(h).astype(f32) + a.astype(f32) + b.astype(f32)
        for h, (a, b) in zip(held, first_parts)
    )
    small = sum_small(
        moves,
        jnp.stack([grad_attention, grad_mixture, jnp.pad(local_counts, (0, D - experts))]),
    )
    new_counts = expert_counts + small[2, :experts].astype(jnp.int32)
    return (
        output_rows.astype(bf16)[None],
        input_delta[None],
        small[0],
        grad_query,
        grad_key,
        grad_value,
        grad_vselect,
        grad_oselect,
        grad_output,
        small[1],
        grad_router,
        grad_up,
        grad_down,
        new_counts,
    )


def solution(mesh):
    rows3 = P(("dp", "expert"), None, None)
    placed = (
        rows3,
        P(("dp", "expert"), None),
        P(("dp", "expert"), None, None, None),
        rows3,
        *[P()] * 9,
        rows3,
        rows3,
        P(),
        rows3,
    )
    return jax.shard_map(
        on_device,
        mesh=mesh,
        in_specs=placed,
        out_specs=(rows3, rows3, *[P()] * 9, rows3, rows3, P()),
        check_vma=False,
    )
```

```python
import functools

import jax
import jax.numpy as jnp
from jax import lax
from jax.experimental import pallas as pl
from jax.experimental.pallas import tpu as pltpu
from jax.sharding import PartitionSpec as P

D = 1024
H = 4
DH = 128
NE = 5
FF = 128
TOPK = 16
GATE_LANES = 16

epsilon = 1e-06
masked_value = -1e30
bf16 = jnp.bfloat16
f32 = jnp.float32
tanh_scale = 0.7978845608028654
cubic = 0.044715


def inverse_rms(values):
    return lax.rsqrt(jnp.mean(values * values, axis=-1, keepdims=True) + epsilon)


def norm_back(values, scaling, gain, upstream):
    weighted = upstream * gain
    middle = jnp.mean(values * weighted, axis=-1, keepdims=True)
    return scaling * weighted - values * scaling * scaling * scaling * middle


def masked_scores(query_low, key_low, allowed):
    raw = jnp.einsum(
        "qhd,khd->hqk", query_low, key_low, preferred_element_type=f32
    ) * DH ** (-0.5)
    return jnp.where(allowed[None], raw, masked_value)


def weight_grad(left, right):
    return jnp.einsum("td,tc->dc", left, right, preferred_element_type=f32)


def input_term(delta, weight):
    return jnp.einsum("tc,dc->td", delta, weight, preferred_element_type=f32)


def contract(left, right, left_dim, right_dim):
    return lax.dot_general(
        left, right, (((left_dim,), (right_dim,)), ((), ())), preferred_element_type=f32
    )


def experts_kernel(blocks, pairs, chained, opened, closed, *refs):
    refs = list(refs)

    def take(count):
        taken = refs[:count]
        del refs[:count]
        return taken

    x_hbm, u_hbm, m_hbm = take(blocks), take(blocks), take(blocks)
    select_ref, router_ref = take(2)
    weights = (take(4), take(4))
    y_prev, dx_prev = take(2) if chained else (None, None)
    gu_prev, gd_prev, gr_prev = take(3) if opened else (None, None, None)
    y_ref, dx_ref = take(2)
    grads = take(4) if closed else take(2)
    (gr_ref,) = take(1)
    (x_buf, u_buf, m_buf, sems, w_up, w_down, w_sems) = take(7)
    (y_acc, dx_acc, gup, gdown, x_turned, gate, delta, gr_acc) = refs
    step = pl.program_id(0)
    pair = pl.program_id(1)
    slot = lax.rem(step, 2)
    local = pairs // 2

    def copies(index, place):
        return (
            pltpu.make_async_copy(x_hbm[index], x_buf.at[place], sems.at[place, 0]),
            pltpu.make_async_copy(u_hbm[index], u_buf.at[place], sems.at[place, 1]),
            pltpu.make_async_copy(m_hbm[index], m_buf.at[place], sems.at[place, 2]),
        )

    def weight_copies(index):
        place = index % 2
        k = index % local
        up_a, up_b, down_a, down_b = weights[index // local]
        return (
            pltpu.make_async_copy(up_a.at[k], w_up.at[place, 0], w_sems.at[place, 0]),
            pltpu.make_async_copy(up_b.at[k], w_up.at[place, 1], w_sems.at[place, 1]),
            pltpu.make_async_copy(
                down_a.at[k], w_down.at[place, pl.ds(0, FF)], w_sems.at[place, 2]
            ),
            pltpu.make_async_copy(
                down_b.at[k], w_down.at[place, pl.ds(FF, FF)], w_sems.at[place, 3]
            ),
        )

    @pl.when(jnp.logical_and(step == 0, pair == 0))
    def _():
        for copy in (*copies(0, 0), *weight_copies(0)):
            copy.start()

    for index in range(pairs):

        @pl.when(pair == index)
        def _():
            for copy in weight_copies(index):
                copy.wait()
            if index + 1 < pairs:
                for copy in weight_copies(index + 1):
                    copy.start()
            elif blocks > 1:

                @pl.when(step < blocks - 1)
                def _():
                    for copy in weight_copies(0):
                        copy.start()

    @pl.when(pair == 0)
    def _():
        for number in range(blocks):
            place = number % 2

            @pl.when(step == number)
            def _():
                for copy in copies(number, place):
                    copy.wait()
                if number + 1 < blocks:
                    for copy in copies(number + 1, 1 - place):
                        copy.start()

        x = x_buf[slot]
        x_turned[...] = x.T
        logits = jnp.dot(x, router_ref[...], preferred_element_type=f32)
        chosen = jnp.dot(m_buf[slot], select_ref[...], preferred_element_type=f32)
        gate[...] = jax.nn.sigmoid(logits) * chosen
        delta[...] = jnp.zeros_like(delta)

    x = x_buf[slot]
    u = u_buf[slot]
    tokens = x.shape[0]
    which = lax.rem(pair, 2)
    up = jnp.concatenate([w_up[which, 0], w_up[which, 1]], axis=1)
    down = w_down[which]
    pre_act = jnp.dot(x, up, preferred_element_type=f32)
    pulled = contract(u, down, 1, 1)
    lanes = lax.broadcasted_iota(jnp.int32, gate.shape, 1)
    gates = gate[...]
    gate_a = jnp.sum(jnp.where(lanes == pair, gates, 0.0), axis=1, keepdims=True)
    gate_b = jnp.sum(jnp.where(lanes == pairs + pair, gates, 0.0), axis=1, keepdims=True)
    spread_gate = jnp.concatenate(
        [jnp.broadcast_to(gate_a, (tokens, FF)), jnp.broadcast_to(gate_b, (tokens, FF))], axis=1
    )
    square = pre_act * pre_act
    bent = jnp.tanh(tanh_scale * pre_act * (1.0 + cubic * square))
    hidden = (0.5 * pre_act * (1.0 + bent)).astype(bf16).astype(f32)
    slope = 0.5 * (1.0 + bent) + 0.5 * pre_act * (1.0 - bent * bent) * (
        tanh_scale * (1.0 + 3.0 * cubic * square)
    )
    felt = hidden * pulled
    felt_a = jnp.sum(felt[:, :FF], axis=1, keepdims=True)
    felt_b = jnp.sum(felt[:, FF:], axis=1, keepdims=True)
    kept = jnp.where(lanes == pair, felt_a, delta[...])
    delta[...] = jnp.where(lanes == pairs + pair, felt_b, kept)
    gated = (spread_gate * hidden).astype(bf16)
    hidden_delta = (spread_gate * pulled * slope).astype(bf16)
    y_new = jnp.dot(gated, down, preferred_element_type=f32)
    dx_new = contract(hidden_delta, up, 1, 1)
    gd_new = contract(gated, u, 0, 0)
    gu_new = jnp.dot(x_turned[...], hidden_delta, preferred_element_type=f32)

    @pl.when(pair == 0)
    def _():
        if chained:
            y_acc[...] = y_prev[...].astype(f32) + y_new
            dx_acc[...] = dx_prev[...].astype(f32) + dx_new
        else:
            y_acc[...] = y_new
            dx_acc[...] = dx_new

    @pl.when(pair > 0)
    def _():
        y_acc[...] += y_new
        dx_acc[...] += dx_new

    if blocks == 1:
        if opened:
            gd_new = gd_prev[0] + gd_new
            gu_new = gu_prev[0] + gu_new
        gd_now, gu_now = gd_new, gu_new
    else:

        @pl.when(step == 0)
        def _():
            if opened:
                gdown[pair] = gd_prev[0] + gd_new
                gup[pair] = gu_prev[0] + gu_new
            else:
                gdown[pair] = gd_new
                gup[pair] = gu_new

        @pl.when(step > 0)
        def _():
            gdown[pair] += gd_new
            gup[pair] += gu_new

        gd_now, gu_now = None, None

    @pl.when(step == blocks - 1)
    def _():
        gu_out = gup[pair] if gu_now is None else gu_now
        gd_out = gdown[pair] if gd_now is None else gd_now
        if closed:
            grads[0][0] = gu_out[:, :FF].astype(bf16)
            grads[1][0] = gu_out[:, FF:].astype(bf16)
            grads[2][0] = gd_out[:FF].astype(bf16)
            grads[3][0] = gd_out[FF:].astype(bf16)
        else:
            grads[0][0] = gu_out
            grads[1][0] = gd_out

    @pl.when(pair == pairs - 1)
    def _():
        gates_now = gate[...]
        logit_delta = (delta[...] * gates_now * (1.0 - gates_now)).astype(bf16)
        y_ref[...] = y_acc[...].astype(bf16)
        dx_ref[...] = (dx_acc[...] + contract(logit_delta, router_ref[...], 1, 1)).astype(bf16)
        gr_new = jnp.dot(x_turned[...], logit_delta, preferred_element_type=f32)

        @pl.when(step == 0)
        def _():
            if opened:
                gr_acc[...] = gr_prev[...] + gr_new
            else:
                gr_acc[...] = gr_new

        @pl.when(step > 0)
        def _():
            gr_acc[...] += gr_new

        @pl.when(step == blocks - 1)
        def _():
            gr_ref[...] = gr_acc[...]


def run_experts(xs, us, ms, select, router, first, second, previous, carried, finish):
    blocks = len(xs)
    local = first[0].shape[0]
    pairs = 2 * local
    tokens = xs[0].shape[0]
    experts = select.shape[0]

    def block(i, j):
        return (i, 0)

    def whole(i, j):
        return (0, 0)

    def opening(i, j):
        return (jnp.where(i == 0, j, pairs - 1), 0, 0)

    def closing(i, j):
        return (jnp.where(i == blocks - 1, j, 0), 0, 0)

    anywhere = pl.BlockSpec(memory_space=pl.ANY)
    in_specs = [anywhere] * (3 * blocks) + [
        pl.BlockSpec((experts, GATE_LANES), whole),
        pl.BlockSpec((D, GATE_LANES), whole),
        *[anywhere] * 8,
    ]
    operands = [*xs, *us, *ms, select, router, *first, *second]
    if previous is not None:
        in_specs += [pl.BlockSpec((tokens, D), block)] * 2
        operands += list(previous)
    if carried is not None:
        in_specs += [
            pl.BlockSpec((1, D, 2 * FF), opening),
            pl.BlockSpec((1, 2 * FF, D), opening),
            pl.BlockSpec((D, GATE_LANES), whole),
        ]
        operands += list(carried)
    out_shape = [jax.ShapeDtypeStruct((blocks * tokens, D), bf16)] * 2
    out_specs = [pl.BlockSpec((tokens, D), block)] * 2
    if finish:
        out_shape += [jax.ShapeDtypeStruct((pairs, D, FF), bf16)] * 2
        out_shape += [jax.ShapeDtypeStruct((pairs, FF, D), bf16)] * 2
        out_specs += [pl.BlockSpec((1, D, FF), closing)] * 2
        out_specs += [pl.BlockSpec((1, FF, D), closing)] * 2
    else:
        out_shape += [jax.ShapeDtypeStruct((pairs, D, 2 * FF), f32)]
        out_shape += [jax.ShapeDtypeStruct((pairs, 2 * FF, D), f32)]
        out_specs += [pl.BlockSpec((1, D, 2 * FF), closing), pl.BlockSpec((1, 2 * FF, D), closing)]
    out_shape.append(jax.ShapeDtypeStruct((D, GATE_LANES), f32))
    out_specs.append(pl.BlockSpec((D, GATE_LANES), whole))
    kept = pairs if blocks > 1 else 1
    return pl.pallas_call(
        functools.partial(
            experts_kernel, blocks, pairs, previous is not None, carried is not None, finish
        ),
        grid=(blocks, pairs),
        in_specs=in_specs,
        out_specs=out_specs,
        out_shape=out_shape,
        scratch_shapes=[
            pltpu.VMEM((2, tokens, D), bf16),
            pltpu.VMEM((2, tokens, D), bf16),
            pltpu.VMEM((2, tokens, experts), bf16),
            pltpu.SemaphoreType.DMA((2, 3)),
            pltpu.VMEM((2, 2, D, FF), bf16),
            pltpu.VMEM((2, 2 * FF, D), bf16),
            pltpu.SemaphoreType.DMA((2, 4)),
            pltpu.VMEM((tokens, D), f32),
            pltpu.VMEM((tokens, D), f32),
            pltpu.VMEM((kept, D, 2 * FF), f32),
            pltpu.VMEM((kept, 2 * FF, D), f32),
            pltpu.VMEM((D, tokens), bf16),
            pltpu.VMEM((tokens, GATE_LANES), f32),
            pltpu.VMEM((tokens, GATE_LANES), f32),
            pltpu.VMEM((D, GATE_LANES), f32),
        ],
        compiler_params=pltpu.CompilerParams(
            dimension_semantics=("arbitrary", "arbitrary"),
            vmem_limit_bytes=56 * 1024 * 1024,
        ),
        cost_estimate=pl.CostEstimate(
            flops=blocks * tokens * D, bytes_accessed=0, transcendentals=0
        ),
        name="experts",
    )(*operands)


class Moves:
    def __init__(self):
        self.dp = lax.axis_size("dp")
        self.ex = lax.axis_size("expert")
        self.nx = self.dp // 2
        self.nh = self.ex // 2
        self.dp_index = lax.axis_index("dp")
        self.ex_index = lax.axis_index("expert")
        self.core = self.dp_index % 2
        self.x = self.dp_index // 2
        self.lo = self.ex_index % 2
        self.hi = self.ex_index // 2
        steps = [(a, b) for a in range(self.nx) for b in range(2)]
        self.plane = sorted(steps, key=lambda s: ((s[0] > 0) + (s[1] > 0), s))

    def over_core(self, value):
        return lax.ppermute(value, "dp", [(i, i ^ 1) for i in range(self.dp)])

    def over_hi(self, value, by=1):
        pairs = [(i, (i // 2 + by) % self.nh * 2 + i % 2) for i in range(self.ex)]
        return lax.ppermute(value, "expert", pairs)

    def over_plane(self, value, offset, back=False):
        a, b = offset
        if back:
            a = (self.nx - a) % self.nx
        if a == 0:
            return lax.ppermute(value, "expert", [(i, i ^ b) for i in range(self.ex)])
        dp_to = [(i // 2 + a) % self.nx * 2 + i % 2 for i in range(self.dp)]
        if b == 0:
            return lax.ppermute(value, "dp", list(enumerate(dp_to)))
        pairs = [
            (i * self.ex + j, dp_to[i] * self.ex + (j ^ 1))
            for i in range(self.dp)
            for j in range(self.ex)
        ]
        return lax.ppermute(value, ("dp", "expert"), pairs)


def add_low(*terms):
    total = terms[0].astype(f32)
    for term in terms[1:]:
        total = total + term.astype(f32)
    return total.astype(bf16)


def tie(*values):
    return lax.optimization_barrier(values)


class Cube:
    def __init__(self, moves):
        self.moves = moves
        ex = moves.ex
        across = [1 << i for i in range(1, moves.dp.bit_length() - 1)]
        along = [1 << i for i in range(ex.bit_length() - 1)]
        across = [mask * ex for mask in across]
        self.flips = (across + along, along[:1] + across + along[1:])
        self.core_flip = ex
        self.count = moves.dp * ex
        self.bits = len(along) + len(across)
        place = moves.dp_index * ex + moves.ex_index
        corners = []
        for flips in self.flips:
            corner = jnp.int32(0)
            for flip in flips:
                corner = corner * 2 + (place // flip) % 2
            corners.append(corner)
        mine = moves.core == 0
        self.corner = jnp.where(mine, corners[0], corners[1])
        self.partner_corner = jnp.where(mine, corners[1], corners[0])

    def exchange(self, value, stage):
        ex = self.moves.ex
        pairs = [
            (i, i ^ self.flips[i // ex % 2][stage]) for i in range(self.count)
        ]
        return lax.ppermute(value, ("dp", "expert"), pairs)

    def over_core(self, value):
        return self.moves.over_core(value)


def small_cost(flops, moved):
    return pl.CostEstimate(flops=flops, bytes_accessed=moved, transcendentals=0)


def grad_blocks_kernel(steps, group, rows, count, order_ref, left_a, left_b, *refs):
    rights, refs = refs[:count], refs[count:]
    out_a, out_b = refs[-2:]
    added = refs[:-2]
    for which, (left, out) in enumerate(((left_a, out_a), (left_b, out_b))):
        low = order_ref[2 * steps + which]
        turned = left[...]
        start = 0
        for right in rights:
            width = right.shape[1]
            product = contract(turned, right[...], 0, 0)
            for h in range(group):
                out[lax.bitwise_xor(low, h), :, start : start + width] = product[
                    h * rows : (h + 1) * rows
                ].astype(bf16)
            start += width
        if added:
            block = added[which][...]
            width = block.shape[1]
            for h in range(group):
                out[lax.bitwise_xor(low, h), :, start : start + width] = block[
                    h * rows : (h + 1) * rows
                ].astype(bf16)


def grad_blocks(cube, left, rights, added=None):
    n = cube.count
    total = left.shape[1]
    tokens = left.shape[0]
    rows = total // n
    group = 1
    while rows * group % 128:
        group *= 2
    wide = rows * group
    steps = n // 2 // group
    core = cube.moves.core
    order = [core * steps + lax.bitwise_xor(cube.corner // group, i) for i in range(steps)]
    order += [
        (1 - core) * steps + lax.bitwise_xor(cube.partner_corner // group, i) for i in range(steps)
    ]
    order += [cube.corner % group, cube.partner_corner % group]
    order = jnp.stack(order).astype(jnp.int32)
    columns = sum(r.shape[1] for r in rights) + (0 if added is None else added.shape[1])
    in_specs = [
        pl.BlockSpec((tokens, wide), lambda i, o: (0, o[i])),
        pl.BlockSpec((tokens, wide), lambda i, o: (0, o[steps + i])),
        *[pl.BlockSpec(r.shape, lambda i, o: (0, 0)) for r in rights],
    ]
    operands = [left, left, *rights]
    if added is not None:
        in_specs += [
            pl.BlockSpec((wide, added.shape[1]), lambda i, o: (o[i], 0)),
            pl.BlockSpec((wide, added.shape[1]), lambda i, o: (o[steps + i], 0)),
        ]
        operands += [added, added]
    shape = jax.ShapeDtypeStruct((n // 2, rows, columns), bf16)
    return pl.pallas_call(
        functools.partial(grad_blocks_kernel, steps, group, rows, len(rights)),
        grid_spec=pltpu.PrefetchScalarGridSpec(
            num_scalar_prefetch=1,
            grid=(steps,),
            in_specs=in_specs,
            out_specs=[pl.BlockSpec((group, rows, columns), lambda i, o: (i, 0, 0))] * 2,
        ),
        out_shape=[shape, shape],
        compiler_params=pltpu.CompilerParams(vmem_limit_bytes=40 * 1024 * 1024),
        cost_estimate=small_cost(tokens * total * columns, total * columns * 2),
        name="grad_blocks",
    )(order, *operands)


def assemble_kernel(count, cuts, order_ref, *refs):
    pieces, outs = refs[:4], refs[4:]
    step = pl.program_id(0)
    for index, piece in enumerate(pieces):

        @pl.when(step // 2 == index)
        def _():
            low = order_ref[8 + index // 2]
            for r in range(count):
                for out, (start, width) in zip(outs, cuts):
                    out[lax.bitwise_xor(low, r)] = piece[r, :, start : start + width].astype(f32)


def assemble(cube, pieces, cuts):
    n = cube.count
    count = n // 8
    rows, columns = pieces[0].shape[1:]
    order = []
    for core, corner in (
        (cube.moves.core, cube.corner),
        (1 - cube.moves.core, cube.partner_corner),
    ):
        order += [core * 4 + lax.bitwise_xor(corner // count, i) for i in range(4)]
    order += [cube.corner % count, cube.partner_corner % count]
    order = jnp.stack(order).astype(jnp.int32)

    def piece(index):
        return pl.BlockSpec(
            (count, rows, columns), lambda i, o: (jnp.clip(i - 2 * index, 0, 1), 0, 0)
        )

    outs = pl.pallas_call(
        functools.partial(assemble_kernel, count, cuts),
        grid_spec=pltpu.PrefetchScalarGridSpec(
            num_scalar_prefetch=1,
            grid=(8,),
            in_specs=[piece(index) for index in range(4)],
            out_specs=[
                pl.BlockSpec((count, rows, width), lambda i, o: (o[i], 0, 0))
                for _, width in cuts
            ],
        ),
        out_shape=[jax.ShapeDtypeStruct((n, rows, width), f32) for _, width in cuts],
        compiler_params=pltpu.CompilerParams(vmem_limit_bytes=40 * 1024 * 1024),
        cost_estimate=small_cost(0, n * rows * columns * 2),
        name="assemble",
    )(order, *pieces)
    return [out.reshape(n * rows, width) for out, (_, width) in zip(outs, cuts)]


def add_halves(kept, got):
    half = kept.shape[0] // 2
    return add_low(kept[:half], got[:half]), add_low(kept[half:], got[half:])


class Sum:
    def __init__(self, cube, blocks, cuts):
        self.cube = cube
        self.cuts = cuts
        self.kept, self.sent = blocks
        self.stage = -1

    def step(self):
        cube = self.cube
        stage = self.stage
        self.stage += 1
        if stage < cube.bits:
            got = cube.over_core(self.sent) if stage < 0 else cube.exchange(self.sent, stage)
            if stage == cube.bits - 1:
                self.total = add_low(self.kept, got)
            else:
                self.kept, self.sent = add_halves(self.kept, got)
            return
        back = 2 * cube.bits - 1 - stage
        if back > 0:
            self.total = jnp.concatenate([self.total, cube.exchange(self.total, back)], axis=0)
        elif back == 0:
            self.halves = [self.total, cube.exchange(self.total, 0)]
        else:
            theirs = [cube.over_core(half) for half in self.halves]
            self.out = assemble(cube, [*self.halves, *theirs], self.cuts)

    def tied(self, value):
        if hasattr(self, "total"):
            self.total, value = tie(self.total, value)
        else:
            self.kept, self.sent, value = tie(self.kept, self.sent, value)
        return value

    @property
    def done(self):
        return self.stage + 1

    def run(self, steps):
        for _ in range(steps):
            self.step()

    @property
    def steps(self):
        return 2 * self.cube.bits + 2


def sum_small(moves, value):
    for axis, size in (("dp", moves.dp), ("expert", moves.ex)):
        span = 1
        while span < size:
            value = value + lax.ppermute(value, axis, [(i, i ^ span) for i in range(size)])
            span *= 2
    return value


def on_device(
    hidden_in,
    segment_ids,
    head_experts,
    token_experts,
    attention_gain,
    query_weight,
    key_weight,
    value_weight,
    value_selector,
    output_selector,
    output_weight,
    mixture_gain,
    router_weight,
    up_weight,
    down_weight,
    expert_counts,
    output_cotangent,
):
    moves = Moves()
    nx, nh = moves.nx, moves.nh
    length = hidden_in.shape[1]
    experts = router_weight.shape[1]
    local = up_weight.shape[0]
    expert_range = jnp.arange(experts, dtype=jnp.int32)

    chosen = token_experts[0]
    routed = jnp.sum((chosen[:, :, None] == expert_range[None, None, :]).astype(f32), axis=1)
    local_counts = jnp.sum(routed, axis=0)
    upstream_low = output_cotangent[0]
    near = [s for s in moves.plane[1:] if 0 in s]
    far = [s for s in moves.plane[1:] if 0 not in s]
    routed_low = routed.astype(bf16)

    ups, downs = [up_weight], [down_weight]
    ups.append(moves.over_hi(up_weight))
    downs.append(moves.over_hi(down_weight))
    us = {s: moves.over_plane(upstream_low, s) for s in near}
    ms = {s: moves.over_plane(routed_low, s) for s in moves.plane[1:]}

    inputs = hidden_in[0].astype(f32)
    att_rms = inverse_rms(inputs)
    normed_low = (inputs * att_rms * attention_gain).astype(bf16)
    query_low = (
        jnp.dot(normed_low, query_weight, preferred_element_type=f32)
        .astype(bf16)
        .reshape(length, H, DH)
    )
    key_low = (
        jnp.dot(normed_low, key_weight, preferred_element_type=f32)
        .astype(bf16)
        .reshape(length, H, DH)
    )
    values_all = jnp.dot(normed_low, value_weight, preferred_element_type=f32).reshape(
        length, H, NE, DH
    )
    value_sigmoid = jax.nn.sigmoid(
        jnp.dot(normed_low, value_selector, preferred_element_type=f32)
    ).reshape(length, H, NE)
    output_sigmoid = jax.nn.sigmoid(
        jnp.dot(normed_low, output_selector, preferred_element_type=f32)
    ).reshape(length, H, NE)
    chosen_mask = jnp.sum(
        (head_experts[0][:, :, :, None] == jnp.arange(NE, dtype=jnp.int32)).astype(f32),
        axis=2,
    )
    value_gate = value_sigmoid * chosen_mask
    output_gate = output_sigmoid * chosen_mask
    value_low = jnp.sum(value_gate[..., None] * values_all, axis=2).astype(bf16)
    positions = jnp.arange(length, dtype=jnp.int32)
    segments = segment_ids[0]
    allowed = (positions[None, :] <= positions[:, None]) & (segments[None, :] == segments[:, None])
    scores = masked_scores(query_low, key_low, allowed)
    log_total = jax.nn.logsumexp(scores, axis=-1, keepdims=True)
    probs_low = jnp.exp(scores - log_total).astype(bf16)
    mixed_heads = jnp.einsum("hqk,khd->qhd", probs_low, value_low, preferred_element_type=f32)
    spread_low = (
        (output_gate[..., None] * mixed_heads[:, :, None, :])
        .astype(bf16)
        .reshape(length, H * NE * DH)
    )
    middle_rows = inputs + jnp.dot(spread_low, output_weight, preferred_element_type=f32)
    moe_rms = inverse_rms(middle_rows)
    moe_low = (middle_rows * moe_rms * mixture_gain).astype(bf16)

    moe_low, ups[1], downs[1] = tie(moe_low, ups[1], downs[1])
    home = moves.plane[0]
    xs = {home: moe_low}
    us[home] = upstream_low
    ms[home] = routed_low
    for s in near:
        xs[s] = moves.over_plane(moe_low, s)
    core_ups = [moves.over_core(u) for u in ups[:2]]
    core_downs = [moves.over_core(d) for d in downs[:2]]
    ups.append(moves.over_hi(ups[1]))
    downs.append(moves.over_hi(downs[1]))

    def slot_weights(s):
        return (ups[s], core_ups[s], downs[s], core_downs[s])

    def selection(slots):
        columns = []
        for core in (0, 1):
            for s in slots:
                owner = (moves.dp_index ^ core) * moves.ex + (moves.hi - s) % nh * 2 + moves.lo
                columns += [owner * local + k for k in range(local)]
        columns += [jnp.int32(-1)] * (GATE_LANES - len(columns))
        select = (expert_range[:, None] == jnp.stack(columns)[None, :]).astype(bf16)
        return select, jnp.dot(router_weight, select, preferred_element_type=f32).astype(bf16)

    sums = {}
    router_width = experts + -experts % 128
    router_sum = jnp.zeros((D, router_width), f32)
    mine_slots, theirs_slots = [None] * nh, [None] * nh

    def visit(offsets, phase, carried, finish):
        slots = (2 * phase, 2 * phase + 1)
        select, router = chosen_by[phase]
        previous = None
        if offsets[0] in sums:
            joined = [sums[s] for s in offsets]
            previous = joined[0] if len(joined) == 1 else tuple(
                jnp.concatenate([j[w] for j in joined], axis=0) for w in (0, 1)
            )
        y, dx, *grads = run_experts(
            [xs[s] for s in offsets],
            [us[s] for s in offsets],
            [ms[s] for s in offsets],
            select,
            router,
            slot_weights(slots[0]),
            slot_weights(slots[1]),
            previous,
            carried,
            finish,
        )
        for k, s in enumerate(offsets):
            sums[s] = (y[k * length : (k + 1) * length], dx[k * length : (k + 1) * length])
        return grads

    phases = nh // 2
    chosen_by = [selection((2 * p, 2 * p + 1)) for p in range(phases)]
    held = None
    sent_back, later = {}, []
    for phase in range(phases):
        last = phase == phases - 1
        if phase == 0:
            calls = [[home], *[[s] for s in near], far]
        elif last:
            calls = [[s] for s in far] + [[s] for s in near] + [[home]]
        else:
            calls = [[home], *[[s] for s in near], far]
        grads = None
        for turn, offsets in enumerate(calls):
            grads = visit(offsets, phase, grads, turn == len(calls) - 1)
            if phase == 0 and turn == 0:
                values = tie(grads[0], moe_low, upstream_low, *[xs[s] for s in near])
                grads[0], far_x, far_u = values[:3]
                for s, value in zip(near, values[3:]):
                    xs[s] = value
                for s in far:
                    xs[s] = moves.over_plane(far_x, s)
                    us[s] = moves.over_plane(far_u, s)
            if phase == 0 and turn == 1 and nh > 2:
                grads[0], ups[2], downs[2] = tie(grads[0], ups[2], downs[2])
                for s in range(3, nh):
                    ups.append(moves.over_hi(ups[-1]))
                    downs.append(moves.over_hi(downs[-1]))
                core_ups.append(moves.over_core(ups[2]))
                core_downs.append(moves.over_core(downs[2]))
            if phase == 0 and turn == len(calls) - 2 and nh > 2:
                values = tie(grads[0], *ups[3:], *downs[3:])
                grads[0] = values[0]
                ups[3:] = values[1 : nh - 2]
                downs[3:] = values[nh - 2 :]
                core_ups += [moves.over_core(u) for u in ups[3:]]
                core_downs += [moves.over_core(d) for d in downs[3:]]
            if phase > 0 and turn == 0:
                grads[0], *held = tie(grads[0], *held)
                held = [moves.over_hi(h) for h in held]
            if phase > 0 and turn == len(calls) - 2:
                grads[0], *held = tie(grads[0], *held)
            if last:
                if later:
                    grads[0], *late = tie(grads[0], *[sums[s][0] for s in later])
                    for s, value in zip(later, late):
                        sent_back[s].append(moves.over_plane(value, s, back=True))
                later = [s for s in offsets if s != home]
                for s in later:
                    sent_back[s] = [moves.over_plane(sums[s][1], s, back=True)]
        router_sum = router_sum + jnp.dot(
            grads[4].astype(bf16),
            jnp.pad(chosen_by[phase][0].T, ((0, 0), (0, router_width - experts))),
            preferred_element_type=f32,
        )
        gu_mine, gu_theirs, gd_mine, gd_theirs = grads[:4]
        gu_got, gd_got = moves.over_core(gu_theirs), moves.over_core(gd_theirs)
        for k in range(2):
            s = 2 * phase + k
            cut = slice(k * local, (k + 1) * local)
            parts = [(gu_mine[cut], gu_got[cut]), (gd_mine[cut], gd_got[cut])]
            if s == 0:
                first_parts = parts
                continue
            if held is not None:
                arrived = held if k == 0 else [moves.over_hi(h) for h in held]
                parts = [(*p, h) for p, h in zip(parts, arrived)]
            held = [add_low(*p) for p in parts]

    expert_delta = sums[home][1].astype(f32)
    for s in moves.plane[1:]:
        expert_delta = expert_delta + sent_back[s][0].astype(f32)

    upstream = upstream_low.astype(f32)
    middle_delta = upstream + norm_back(middle_rows, moe_rms, mixture_gain, expert_delta)
    grad_mixture = jnp.sum(expert_delta * middle_rows * moe_rms, axis=0)
    middle_low = middle_delta.astype(bf16)
    cube = Cube(moves)
    out_sum = Sum(cube, grad_blocks(cube, spread_low, [middle_low]), [(0, D)])
    middle_sent = out_sum.tied(middle_low)
    out_sum.step()
    spread_delta = jnp.einsum(
        "td,cd->tc", middle_sent, output_weight, preferred_element_type=f32
    ).reshape(length, H, NE, DH)
    mixed_delta = jnp.sum(output_gate[..., None] * spread_delta, axis=2).astype(bf16)
    oselect_delta = (
        (
            jnp.sum(spread_delta * mixed_heads[:, :, None, :], axis=3)
            * chosen_mask
            * output_sigmoid
            * (1.0 - output_sigmoid)
        )
        .astype(bf16)
        .reshape(length, H * NE)
    )
    mixed_delta = out_sum.tied(mixed_delta)
    out_sum.step()
    scores = masked_scores(query_low, key_low, allowed)
    probs_full = jnp.exp(scores - log_total)
    probs_again = probs_full.astype(bf16)
    weight_delta = jnp.einsum("qhd,khd->hqk", mixed_delta, value_low, preferred_element_type=f32)
    score_delta = (
        probs_full * (weight_delta - jnp.sum(probs_full * weight_delta, axis=-1, keepdims=True))
    ).astype(bf16)
    value_delta = jnp.einsum("hqk,qhd->khd", probs_again, mixed_delta, preferred_element_type=f32)
    values_delta = (
        (value_gate[..., None] * value_delta[:, :, None, :])
        .astype(bf16)
        .reshape(length, H * NE * DH)
    )
    value_sum = Sum(cube, grad_blocks(cube, normed_low, [values_delta]), [(0, H * NE * DH)])
    score_delta = out_sum.tied(score_delta)
    score_delta = value_sum.tied(score_delta)
    *held, score_delta = tie(*held, score_delta)
    last_held = [moves.over_hi(h) for h in held]
    *outputs_back, score_delta = tie(*[sent_back[s][1] for s in moves.plane[1:]], score_delta)
    out_sum.step()
    value_sum.step()
    query_delta = (
        (
            jnp.einsum("hqk,khd->qhd", score_delta, key_low, preferred_element_type=f32)
            * DH ** (-0.5)
        )
        .astype(bf16)
        .reshape(length, H * DH)
    )
    key_delta = (
        (
            jnp.einsum("hqk,qhd->khd", score_delta, query_low, preferred_element_type=f32)
            * DH ** (-0.5)
        )
        .astype(bf16)
        .reshape(length, H * DH)
    )
    vselect_delta = (
        (
            jnp.sum(value_delta[:, :, None, :] * values_all, axis=3)
            * chosen_mask
            * value_sigmoid
            * (1.0 - value_sigmoid)
        )
        .astype(bf16)
        .reshape(length, H * NE)
    )
    narrow = 128
    margin = ((0, 0), (0, narrow - H * NE))
    select_delta = jnp.concatenate(
        [jnp.pad(vselect_delta, margin), jnp.pad(oselect_delta, margin)], axis=1
    )
    cuts = [(0, H * DH), (H * DH, H * DH)]
    start = 2 * H * DH
    cuts += [(start, H * NE), (start + narrow, H * NE), (start + 2 * narrow, experts)]
    rest_sum = Sum(
        cube,
        grad_blocks(cube, normed_low, [query_delta, key_delta, select_delta], router_sum),
        cuts,
    )
    query_sent = rest_sum.tied(query_delta)
    query_sent = out_sum.tied(query_sent)
    query_sent = value_sum.tied(query_sent)
    last_held[0], last_held[1], query_sent = tie(*last_held, query_sent)
    for each in (rest_sum, out_sum, value_sum):
        each.step()
    normed_delta = (
        input_term(query_sent, query_weight)
        + input_term(key_delta, key_weight)
        + input_term(values_delta, value_weight)
    )
    normed_delta = (
        normed_delta
        + input_term(vselect_delta, value_selector)
        + input_term(oselect_delta, output_selector)
    )
    for each in (rest_sum, out_sum, value_sum):
        normed_delta = each.tied(normed_delta)
    for each in (rest_sum, out_sum, value_sum):
        each.run(each.steps - each.done)
    (grad_output,) = out_sum.out
    (grad_value,) = value_sum.out
    grad_query, grad_key, grad_vselect, grad_oselect, grad_router = rest_sum.out
    input_delta = middle_delta + norm_back(inputs, att_rms, attention_gain, normed_delta)
    grad_attention = jnp.sum(normed_delta * inputs * att_rms, axis=0)
    output_rows = middle_rows + sums[home][0].astype(f32)
    for value in outputs_back:
        output_rows = output_rows + value.astype(f32)
    grad_up, grad_down = (
        h.astype(f32) + a.astype(f32) + b.astype(f32)
        for h, (a, b) in zip(last_held, first_parts)
    )
    small = sum_small(
        moves,
        jnp.stack([grad_attention, grad_mixture, jnp.pad(local_counts, (0, D - experts))]),
    )
    new_counts = expert_counts + small[2, :experts].astype(jnp.int32)
    return (
        output_rows.astype(bf16)[None],
        input_delta[None],
        small[0],
        grad_query,
        grad_key,
        grad_value,
        grad_vselect,
        grad_oselect,
        grad_output,
        small[1],
        grad_router,
        grad_up,
        grad_down,
        new_counts,
    )


def solution(mesh):
    rows3 = P(("dp", "expert"), None, None)
    placed = (
        rows3,
        P(("dp", "expert"), None),
        P(("dp", "expert"), None, None, None),
        rows3,
        *[P()] * 9,
        rows3,
        rows3,
        P(),
        rows3,
    )
    return jax.shard_map(
        on_device,
        mesh=mesh,
        in_specs=placed,
        out_specs=(rows3, rows3, *[P()] * 9, rows3, rows3, P()),
        check_vma=False,
    )
```

```python
import functools

import jax
import jax.numpy as jnp
from jax import lax
from jax.experimental import pallas as pl
from jax.experimental.pallas import tpu as pltpu
from jax.sharding import PartitionSpec as P

D = 1024
H = 4
DH = 128
NE = 5
FF = 128
TOPK = 16
GATE_LANES = 16

epsilon = 1e-06
masked_value = -1e30
bf16 = jnp.bfloat16
f32 = jnp.float32
tanh_scale = 0.7978845608028654
cubic = 0.044715


def inverse_rms(values):
    return lax.rsqrt(jnp.mean(values * values, axis=-1, keepdims=True) + epsilon)


def norm_back(values, scaling, gain, upstream):
    weighted = upstream * gain
    middle = jnp.mean(values * weighted, axis=-1, keepdims=True)
    return scaling * weighted - values * scaling * scaling * scaling * middle


def input_term(delta, weight):
    return jnp.einsum("tc,dc->td", delta, weight, preferred_element_type=f32)


def contract(left, right, left_dim, right_dim):
    return lax.dot_general(
        left, right, (((left_dim,), (right_dim,)), ((), ())), preferred_element_type=f32
    )


def experts_kernel(blocks, pairs, chained, opened, closed, *refs):
    refs = list(refs)

    def take(count):
        taken = refs[:count]
        del refs[:count]
        return taken

    x_hbm, um_hbm = take(blocks), take(blocks)
    select_ref, router_ref = take(2)
    weights = (take(2), take(2))
    y_prev, dx_prev = take(2) if chained else (None, None)
    gu_prev, gd_prev, gr_prev = take(3) if opened else (None, None, None)
    y_ref, dx_ref = take(2)
    grads = take(2)
    (gr_ref,) = take(1)
    (x_buf, u_buf, m_buf, sems, w_up, w_down, w_sems) = take(7)
    (y_acc, dx_acc, gup, gdown, x_turned, u_turned, gate, delta, gr_acc) = take(9)
    gated_buf, hidden_buf = refs
    step = pl.program_id(0)
    pair = pl.program_id(1)
    slot = lax.rem(step, 2)
    local = pairs // 2

    def copies(index, place):
        return (
            pltpu.make_async_copy(x_hbm[index], x_buf.at[place], sems.at[place, 0]),
            pltpu.make_async_copy(
                um_hbm[index].at[:, pl.ds(0, D)], u_buf.at[place], sems.at[place, 1]
            ),
            pltpu.make_async_copy(
                um_hbm[index].at[:, pl.ds(D, m_buf.shape[2])], m_buf.at[place], sems.at[place, 2]
            ),
        )

    def weight_copies(index):
        place = index % 2
        k = index % local
        ways = []
        for side, weight in enumerate(weights[index // local]):
            for part, buffer in enumerate((w_up, w_down)):
                ways.append(
                    pltpu.make_async_copy(
                        weight.at[k, :, pl.ds(part * FF, FF)],
                        buffer.at[place, :, pl.ds(side * FF, FF)],
                        w_sems.at[place, 2 * side + part],
                    )
                )
        return ways

    @pl.when(jnp.logical_and(step == 0, pair == 0))
    def _():
        for copy in (*copies(0, 0), *weight_copies(0)):
            copy.start()

    for index in range(pairs):

        @pl.when(pair == index)
        def _():
            for copy in weight_copies(index):
                copy.wait()
            if index + 1 < pairs:
                for copy in weight_copies(index + 1):
                    copy.start()
            elif blocks > 1:

                @pl.when(step < blocks - 1)
                def _():
                    for copy in weight_copies(0):
                        copy.start()

    @pl.when(pair == 0)
    def _():
        for number in range(blocks):
            place = number % 2

            @pl.when(step == number)
            def _():
                for copy in copies(number, place):
                    copy.wait()
                if number + 1 < blocks:
                    for copy in copies(number + 1, 1 - place):
                        copy.start()

        x = x_buf[slot]
        x_turned[...] = x.T
        u_turned[...] = u_buf[slot].T
        logits = jnp.dot(x, router_ref[...], preferred_element_type=f32)
        chosen = jnp.dot(m_buf[slot], select_ref[...], preferred_element_type=f32)
        gate[...] = jax.nn.sigmoid(logits) * chosen
        delta[...] = jnp.zeros_like(delta)

    @pl.when(pair == 0)
    def _():
        if chained:
            y_acc[...] = y_prev[...].astype(f32)
            dx_acc[...] = dx_prev[...].astype(f32)
        else:
            y_acc[...] = jnp.zeros_like(y_acc)
            dx_acc[...] = jnp.zeros_like(dx_acc)

    tokens = x_buf.shape[1]
    rows = tokens // 2
    which = lax.rem(pair, 2)
    up = w_up[which]
    down = w_down[which]
    lanes = lax.broadcasted_iota(jnp.int32, (rows, GATE_LANES), 1)
    cuts = [pl.ds(c * rows, rows) for c in range(2)]

    def first(cut):
        pre_act = jnp.dot(x_buf[slot, cut], up, preferred_element_type=f32)
        return pre_act, jnp.dot(u_buf[slot, cut], down, preferred_element_type=f32)

    def bend(cut, pre_act, pulled):
        gates = gate[cut]
        gate_a = jnp.sum(jnp.where(lanes == pair, gates, 0.0), axis=1, keepdims=True)
        gate_b = jnp.sum(jnp.where(lanes == pairs + pair, gates, 0.0), axis=1, keepdims=True)
        spread_gate = jnp.concatenate(
            [jnp.broadcast_to(gate_a, (rows, FF)), jnp.broadcast_to(gate_b, (rows, FF))], axis=1
        )
        square = pre_act * pre_act
        bent = jnp.tanh(pre_act * (tanh_scale + tanh_scale * cubic * square))
        half = 0.5 + 0.5 * bent
        hidden = (pre_act * half).astype(bf16).astype(f32)
        slope = half + (0.5 * pre_act) * (1.0 - bent * bent) * (
            tanh_scale + 3.0 * tanh_scale * cubic * square
        )
        felt = hidden * pulled
        felt_a = jnp.sum(felt[:, :FF], axis=1, keepdims=True)
        felt_b = jnp.sum(felt[:, FF:], axis=1, keepdims=True)
        kept = jnp.where(lanes == pair, felt_a, delta[cut])
        delta[cut] = jnp.where(lanes == pairs + pair, felt_b, kept)
        gated_buf[cut] = (spread_gate * hidden).astype(bf16)
        hidden_buf[cut] = (spread_gate * pulled * slope).astype(bf16)

    def second(cut):
        y_acc[cut] += contract(gated_buf[cut], down, 1, 1)
        dx_acc[cut] += contract(hidden_buf[cut], up, 1, 1)

    ready = first(cuts[0])
    for c, cut in enumerate(cuts):
        later = first(cuts[c + 1]) if c + 1 < 2 else None
        bend(cut, *ready)
        second(cut)
        ready = later
    gd_new = jnp.dot(u_turned[...], gated_buf[...], preferred_element_type=f32)
    gu_new = jnp.dot(x_turned[...], hidden_buf[...], preferred_element_type=f32)

    def put(gu_out, gd_out):
        if closed:
            for side in (0, 1):
                grads[side][0, :, :FF] = gu_out[:, side * FF : (side + 1) * FF].astype(bf16)
                grads[side][0, :, FF:] = gd_out[:, side * FF : (side + 1) * FF].astype(bf16)
        else:
            grads[0][0] = gu_out
            grads[1][0] = gd_out

    if blocks == 1:
        if opened:
            gd_new = gd_prev[0] + gd_new
            gu_new = gu_prev[0] + gu_new
        put(gu_new, gd_new)
    else:

        @pl.when(step == 0)
        def _():
            if opened:
                gdown[pair] = gd_prev[0]
                gup[pair] = gu_prev[0]
            else:
                gdown[pair] = jnp.zeros_like(gd_new)
                gup[pair] = jnp.zeros_like(gu_new)

        gdown[pair] += gd_new
        gup[pair] += gu_new

        @pl.when(step == blocks - 1)
        def _():
            put(gup[pair], gdown[pair])

    @pl.when(pair == pairs - 1)
    def _():
        gates_now = gate[...]
        logit_delta = (delta[...] * gates_now * (1.0 - gates_now)).astype(bf16)
        y_ref[...] = y_acc[...].astype(bf16)
        dx_ref[...] = (dx_acc[...] + contract(logit_delta, router_ref[...], 1, 1)).astype(bf16)
        gr_new = jnp.dot(x_turned[...], logit_delta, preferred_element_type=f32)

        @pl.when(step == 0)
        def _():
            if opened:
                gr_acc[...] = gr_prev[...] + gr_new
            else:
                gr_acc[...] = gr_new

        @pl.when(step > 0)
        def _():
            gr_acc[...] += gr_new

        @pl.when(step == blocks - 1)
        def _():
            gr_ref[...] = gr_acc[...]


def run_experts(xs, ums, select, router, first, second, previous, carried, finish):
    blocks = len(xs)
    local = first[0].shape[0]
    pairs = 2 * local
    tokens = xs[0].shape[0]
    experts = select.shape[0]

    def block(i, j):
        return (i, 0)

    def whole(i, j):
        return (0, 0)

    def opening(i, j):
        return (jnp.where(i == 0, j, pairs - 1), 0, 0)

    def closing(i, j):
        return (jnp.where(i == blocks - 1, j, 0), 0, 0)

    anywhere = pl.BlockSpec(memory_space=pl.ANY)
    in_specs = [anywhere] * (2 * blocks) + [
        pl.BlockSpec((experts, GATE_LANES), whole),
        pl.BlockSpec((D, GATE_LANES), whole),
        *[anywhere] * 4,
    ]
    operands = [*xs, *ums, select, router, *first, *second]
    if previous is not None:
        in_specs += [pl.BlockSpec((tokens, D), block)] * 2
        operands += list(previous)
    if carried is not None:
        in_specs += [
            pl.BlockSpec((1, D, 2 * FF), opening),
            pl.BlockSpec((1, D, 2 * FF), opening),
            pl.BlockSpec((D, GATE_LANES), whole),
        ]
        operands += list(carried)
    out_shape = [jax.ShapeDtypeStruct((blocks * tokens, D), bf16)] * 2
    out_specs = [pl.BlockSpec((tokens, D), block)] * 2
    if finish:
        out_shape += [jax.ShapeDtypeStruct((pairs, D, 2 * FF), bf16)] * 2
    else:
        out_shape += [jax.ShapeDtypeStruct((pairs, D, 2 * FF), f32)] * 2
    out_specs += [pl.BlockSpec((1, D, 2 * FF), closing)] * 2
    out_shape.append(jax.ShapeDtypeStruct((D, GATE_LANES), f32))
    out_specs.append(pl.BlockSpec((D, GATE_LANES), whole))
    kept = pairs if blocks > 1 else 1
    return pl.pallas_call(
        functools.partial(
            experts_kernel, blocks, pairs, previous is not None, carried is not None, finish
        ),
        grid=(blocks, pairs),
        in_specs=in_specs,
        out_specs=out_specs,
        out_shape=out_shape,
        scratch_shapes=[
            pltpu.VMEM((2, tokens, D), bf16),
            pltpu.VMEM((2, tokens, D), bf16),
            pltpu.VMEM((2, tokens, experts), bf16),
            pltpu.SemaphoreType.DMA((2, 3)),
            pltpu.VMEM((2, D, 2 * FF), bf16),
            pltpu.VMEM((2, D, 2 * FF), bf16),
            pltpu.SemaphoreType.DMA((2, 4)),
            pltpu.VMEM((tokens, D), f32),
            pltpu.VMEM((tokens, D), f32),
            pltpu.VMEM((kept, D, 2 * FF), f32),
            pltpu.VMEM((kept, D, 2 * FF), f32),
            pltpu.VMEM((D, tokens), bf16),
            pltpu.VMEM((D, tokens), bf16),
            pltpu.VMEM((tokens, GATE_LANES), f32),
            pltpu.VMEM((tokens, GATE_LANES), f32),
            pltpu.VMEM((D, GATE_LANES), f32),
            pltpu.VMEM((tokens, 2 * FF), bf16),
            pltpu.VMEM((tokens, 2 * FF), bf16),
        ],
        compiler_params=pltpu.CompilerParams(
            dimension_semantics=("arbitrary", "arbitrary"),
            vmem_limit_bytes=56 * 1024 * 1024,
        ),
        cost_estimate=pl.CostEstimate(
            flops=12 * blocks * tokens * D * FF * pairs, bytes_accessed=0, transcendentals=0
        ),
        name="experts",
    )(*operands)


def column(values, index):
    lanes = lax.broadcasted_iota(jnp.int32, values.shape, 1)
    return jnp.sum(jnp.where(lanes == index, values, 0.0), axis=1, keepdims=True)


def head_probs(query, key, segment_col, segment_row):
    raw = contract(query, key, 1, 1) * DH ** (-0.5)
    rows = lax.broadcasted_iota(jnp.int32, raw.shape, 0)
    columns = lax.broadcasted_iota(jnp.int32, raw.shape, 1)
    allowed = jnp.logical_and(columns <= rows, segment_col == segment_row)
    scores = jnp.where(allowed, raw, masked_value)
    powers = jnp.exp(scores - jnp.max(scores, axis=1, keepdims=True))
    return powers * (1.0 / jnp.sum(powers, axis=1, keepdims=True))


def head_sigmoids(head, chosen_ref, sigmoids, expert):
    first, second = chosen_ref[0, :, 0:1], chosen_ref[0, :, 1:2]
    chosen = jnp.logical_or(first == expert, second == expert).astype(f32)
    half = sigmoids.shape[1] // 2
    place = head * NE + expert
    return chosen, column(sigmoids[:, :half], place), column(sigmoids[:, half:], place)


def part(expert):
    return slice(expert * DH, (expert + 1) * DH)


def attend_kernel(
    normed_ref,
    query_weight,
    key_weight,
    value_weight,
    selectors,
    chosen_ref,
    segment_col,
    segment_row,
    query_ref,
    key_ref,
    values_ref,
    low_ref,
    mixed_ref,
    spread_ref,
    sigmoids_ref,
):
    head = pl.program_id(0)
    normed = normed_ref[...]

    @pl.when(head == 0)
    def _():
        sigmoids_ref[...] = jax.nn.sigmoid(
            jnp.dot(normed, selectors[...], preferred_element_type=f32)
        )

    query = jnp.dot(normed, query_weight[...], preferred_element_type=f32).astype(bf16)
    key = jnp.dot(normed, key_weight[...], preferred_element_type=f32).astype(bf16)
    query_ref[...] = query
    key_ref[...] = key
    values_ref[...] = jnp.dot(normed, value_weight[...], preferred_element_type=f32)
    sigmoids = sigmoids_ref[...]
    gates = [head_sigmoids(head, chosen_ref, sigmoids, e) for e in range(NE)]
    low = gates[0][0] * gates[0][1] * values_ref[:, part(0)]
    for e in range(1, NE):
        low = low + gates[e][0] * gates[e][1] * values_ref[:, part(e)]
    low = low.astype(bf16)
    low_ref[...] = low
    probs = head_probs(query, key, segment_col[...], segment_row[...]).astype(bf16)
    mixed = jnp.dot(probs, low, preferred_element_type=f32)
    mixed_ref[...] = mixed
    for e in range(NE):
        spread_ref[:, part(e)] = (gates[e][0] * gates[e][2] * mixed).astype(bf16)


def attend_specs(tokens):
    whole = pl.BlockSpec((tokens, D), lambda h: (0, 0))
    narrow = pl.BlockSpec((tokens, DH), lambda h: (0, h))
    wide = pl.BlockSpec((tokens, NE * DH), lambda h: (0, h))
    rest = [
        pl.BlockSpec((1, tokens, 2), lambda h: (h, 0, 0)),
        pl.BlockSpec((tokens, 1), lambda h: (0, 0)),
        pl.BlockSpec((1, tokens), lambda h: (0, 0)),
    ]
    sigmoids = pl.BlockSpec((tokens, 256), lambda h: (0, 0))
    return whole, narrow, wide, rest, sigmoids


def attend(normed, query_weight, key_weight, value_weight, selectors, chosen, segments):
    tokens = normed.shape[0]
    whole, narrow, wide, rest, sigmoids = attend_specs(tokens)
    return pl.pallas_call(
        attend_kernel,
        grid=(H,),
        in_specs=[
            whole,
            pl.BlockSpec((D, DH), lambda h: (0, h)),
            pl.BlockSpec((D, DH), lambda h: (0, h)),
            pl.BlockSpec((D, NE * DH), lambda h: (0, h)),
            pl.BlockSpec((D, 256), lambda h: (0, 0)),
            *rest,
        ],
        out_specs=[narrow, narrow, wide, narrow, narrow, wide, sigmoids],
        out_shape=[
            jax.ShapeDtypeStruct((tokens, H * DH), bf16),
            jax.ShapeDtypeStruct((tokens, H * DH), bf16),
            jax.ShapeDtypeStruct((tokens, H * NE * DH), f32),
            jax.ShapeDtypeStruct((tokens, H * DH), bf16),
            jax.ShapeDtypeStruct((tokens, H * DH), f32),
            jax.ShapeDtypeStruct((tokens, H * NE * DH), bf16),
            jax.ShapeDtypeStruct((tokens, 256), f32),
        ],
        compiler_params=pltpu.CompilerParams(vmem_limit_bytes=48 * 1024 * 1024),
        cost_estimate=pl.CostEstimate(
            flops=2 * tokens * H * DH * (D * (NE + 2) + 2 * tokens),
            bytes_accessed=0,
            transcendentals=0,
        ),
        name="attend",
    )(
        normed,
        query_weight,
        key_weight,
        value_weight,
        selectors,
        chosen,
        segments[:, None],
        segments[None, :],
    )


def attend_back_kernel(
    middle_ref,
    output_weight,
    query_ref,
    key_ref,
    low_ref,
    mixed_ref,
    values_ref,
    sigmoids_ref,
    chosen_ref,
    segment_col,
    segment_row,
    query_delta,
    key_delta,
    values_delta,
    select_delta,
    spread_buf,
    value_acc,
    output_acc,
):
    head = pl.program_id(0)

    @pl.when(head == 0)
    def _():
        value_acc[...] = jnp.zeros_like(value_acc)
        output_acc[...] = jnp.zeros_like(output_acc)

    spread_buf[...] = contract(middle_ref[...], output_weight[...], 1, 1)
    sigmoids = sigmoids_ref[...]
    gates = [head_sigmoids(head, chosen_ref, sigmoids, e) for e in range(NE)]
    query, key, low = query_ref[...], key_ref[...], low_ref[...]
    mixed = mixed_ref[...]
    mixed_delta = gates[0][0] * gates[0][2] * spread_buf[:, part(0)]
    for e in range(1, NE):
        mixed_delta = mixed_delta + gates[e][0] * gates[e][2] * spread_buf[:, part(e)]
    mixed_delta = mixed_delta.astype(bf16)
    probs = head_probs(query, key, segment_col[...], segment_row[...])
    weight_delta = contract(mixed_delta, low, 1, 1)
    pulled = jnp.sum(probs * weight_delta, axis=1, keepdims=True)
    score_delta = (probs * (weight_delta - pulled)).astype(bf16)
    query_delta[...] = (
        jnp.dot(score_delta, key, preferred_element_type=f32) * DH ** (-0.5)
    ).astype(bf16)
    key_delta[...] = (contract(score_delta, query, 0, 0) * DH ** (-0.5)).astype(bf16)
    value_delta = contract(probs.astype(bf16), mixed_delta, 0, 0)
    lanes = lax.broadcasted_iota(jnp.int32, value_acc.shape, 1)
    for e in range(NE):
        chosen, value_sigmoid, output_sigmoid = gates[e]
        values_delta[:, part(e)] = (chosen * value_sigmoid * value_delta).astype(bf16)
        felt = jnp.sum(value_delta * values_ref[:, part(e)], axis=1, keepdims=True)
        felt = felt * chosen * value_sigmoid * (1.0 - value_sigmoid)
        value_acc[...] = jnp.where(lanes == head * NE + e, felt, value_acc[...])
        felt = jnp.sum(spread_buf[:, part(e)] * mixed, axis=1, keepdims=True)
        felt = felt * chosen * output_sigmoid * (1.0 - output_sigmoid)
        output_acc[...] = jnp.where(lanes == head * NE + e, felt, output_acc[...])

    @pl.when(head == H - 1)
    def _():
        half = value_acc.shape[1]
        select_delta[:, :half] = value_acc[...].astype(bf16)
        select_delta[:, half:] = output_acc[...].astype(bf16)


def attend_back(middle_low, output_weight, query, key, low, mixed, values, sigmoids, chosen, segments):
    tokens = middle_low.shape[0]
    whole, narrow, wide, rest, sigmoid_spec = attend_specs(tokens)
    return pl.pallas_call(
        attend_back_kernel,
        grid=(H,),
        in_specs=[
            whole,
            pl.BlockSpec((NE * DH, D), lambda h: (h, 0)),
            narrow,
            narrow,
            narrow,
            narrow,
            wide,
            sigmoid_spec,
            *rest,
        ],
        out_specs=[narrow, narrow, wide, sigmoid_spec],
        out_shape=[
            jax.ShapeDtypeStruct((tokens, H * DH), bf16),
            jax.ShapeDtypeStruct((tokens, H * DH), bf16),
            jax.ShapeDtypeStruct((tokens, H * NE * DH), bf16),
            jax.ShapeDtypeStruct((tokens, 256), bf16),
        ],
        scratch_shapes=[
            pltpu.VMEM((tokens, NE * DH), f32),
            pltpu.VMEM((tokens, 128), f32),
            pltpu.VMEM((tokens, 128), f32),
        ],
        compiler_params=pltpu.CompilerParams(vmem_limit_bytes=48 * 1024 * 1024),
        cost_estimate=pl.CostEstimate(
            flops=2 * tokens * H * DH * (D * NE + 5 * tokens), bytes_accessed=0, transcendentals=0
        ),
        name="attend_back",
    )(
        middle_low,
        output_weight,
        query,
        key,
        low,
        mixed,
        values,
        sigmoids,
        chosen,
        segments[:, None],
        segments[None, :],
    )


class Moves:
    def __init__(self):
        self.dp = lax.axis_size("dp")
        self.ex = lax.axis_size("expert")
        self.nx = self.dp // 2
        self.nh = self.ex // 2
        self.dp_index = lax.axis_index("dp")
        self.ex_index = lax.axis_index("expert")
        self.core = self.dp_index % 2
        self.x = self.dp_index // 2
        self.lo = self.ex_index % 2
        self.hi = self.ex_index // 2
        steps = [(a, b) for a in range(self.nx) for b in range(2)]
        self.plane = sorted(steps, key=lambda s: ((s[0] > 0) + (s[1] > 0), s))

    def over_core(self, value):
        return lax.ppermute(value, "dp", [(i, i ^ 1) for i in range(self.dp)])

    def over_hi(self, value, by=1):
        pairs = [(i, (i // 2 + by) % self.nh * 2 + i % 2) for i in range(self.ex)]
        return lax.ppermute(value, "expert", pairs)

    def over_plane(self, value, offset, back=False):
        a, b = offset
        if back:
            a = (self.nx - a) % self.nx
        if a == 0:
            return lax.ppermute(value, "expert", [(i, i ^ b) for i in range(self.ex)])
        dp_to = [(i // 2 + a) % self.nx * 2 + i % 2 for i in range(self.dp)]
        if b == 0:
            return lax.ppermute(value, "dp", list(enumerate(dp_to)))
        pairs = [
            (i * self.ex + j, dp_to[i] * self.ex + (j ^ 1))
            for i in range(self.dp)
            for j in range(self.ex)
        ]
        return lax.ppermute(value, ("dp", "expert"), pairs)


def add_low(*terms):
    total = terms[0].astype(f32)
    for term in terms[1:]:
        total = total + term.astype(f32)
    return total.astype(bf16)


def tie(*values):
    return lax.optimization_barrier(values)


class Cube:
    def __init__(self, moves):
        self.moves = moves
        ex = moves.ex
        across = [1 << i for i in range(1, moves.dp.bit_length() - 1)]
        along = [1 << i for i in range(ex.bit_length() - 1)]
        across = [mask * ex for mask in across]
        self.flips = (across + along, along[:1] + across + along[1:])
        self.core_flip = ex
        self.count = moves.dp * ex
        self.bits = len(along) + len(across)
        place = moves.dp_index * ex + moves.ex_index
        corners = []
        for flips in self.flips:
            corner = jnp.int32(0)
            for flip in flips:
                corner = corner * 2 + (place // flip) % 2
            corners.append(corner)
        mine = moves.core == 0
        self.corner = jnp.where(mine, corners[0], corners[1])
        self.partner_corner = jnp.where(mine, corners[1], corners[0])

    def exchange(self, value, stage):
        ex = self.moves.ex
        pairs = [
            (i, i ^ self.flips[i // ex % 2][stage]) for i in range(self.count)
        ]
        return lax.ppermute(value, ("dp", "expert"), pairs)

    def over_core(self, value):
        return self.moves.over_core(value)


def small_cost(flops, moved):
    return pl.CostEstimate(flops=flops, bytes_accessed=moved, transcendentals=0)


def grad_blocks_kernel(steps, group, rows, count, order_ref, left_a, left_b, *refs):
    rights, refs = refs[:count], refs[count:]
    out_a, out_b = refs[-2:]
    added = refs[:-2]
    for which, (left, out) in enumerate(((left_a, out_a), (left_b, out_b))):
        low = order_ref[2 * steps + which]
        turned = left[...]
        start = 0
        for right in rights:
            width = right.shape[1]
            product = contract(turned, right[...], 0, 0)
            for h in range(group):
                out[lax.bitwise_xor(low, h), :, start : start + width] = product[
                    h * rows : (h + 1) * rows
                ].astype(bf16)
            start += width
        if added:
            block = added[which][...]
            width = block.shape[1]
            for h in range(group):
                out[lax.bitwise_xor(low, h), :, start : start + width] = block[
                    h * rows : (h + 1) * rows
                ].astype(bf16)


def grad_blocks(cube, left, rights, added=None):
    n = cube.count
    total = left.shape[1]
    tokens = left.shape[0]
    rows = total // n
    group = 1
    while rows * group % 128:
        group *= 2
    wide = rows * group
    steps = n // 2 // group
    core = cube.moves.core
    order = [core * steps + lax.bitwise_xor(cube.corner // group, i) for i in range(steps)]
    order += [
        (1 - core) * steps + lax.bitwise_xor(cube.partner_corner // group, i) for i in range(steps)
    ]
    order += [cube.corner % group, cube.partner_corner % group]
    order = jnp.stack(order).astype(jnp.int32)
    columns = sum(r.shape[1] for r in rights) + (0 if added is None else added.shape[1])
    in_specs = [
        pl.BlockSpec((tokens, wide), lambda i, o: (0, o[i])),
        pl.BlockSpec((tokens, wide), lambda i, o: (0, o[steps + i])),
        *[pl.BlockSpec(r.shape, lambda i, o: (0, 0)) for r in rights],
    ]
    operands = [left, left, *rights]
    if added is not None:
        in_specs += [
            pl.BlockSpec((wide, added.shape[1]), lambda i, o: (o[i], 0)),
            pl.BlockSpec((wide, added.shape[1]), lambda i, o: (o[steps + i], 0)),
        ]
        operands += [added, added]
    shape = jax.ShapeDtypeStruct((n // 2, rows, columns), bf16)
    return pl.pallas_call(
        functools.partial(grad_blocks_kernel, steps, group, rows, len(rights)),
        grid_spec=pltpu.PrefetchScalarGridSpec(
            num_scalar_prefetch=1,
            grid=(steps,),
            in_specs=in_specs,
            out_specs=[pl.BlockSpec((group, rows, columns), lambda i, o: (i, 0, 0))] * 2,
        ),
        out_shape=[shape, shape],
        compiler_params=pltpu.CompilerParams(vmem_limit_bytes=40 * 1024 * 1024),
        cost_estimate=small_cost(tokens * total * columns, total * columns * 2),
        name="grad_blocks",
    )(order, *operands)


def assemble_kernel(count, cuts, order_ref, *refs):
    pieces, outs = refs[:4], refs[4:]
    step = pl.program_id(0)
    for index, piece in enumerate(pieces):

        @pl.when(step // 2 == index)
        def _():
            low = order_ref[8 + index // 2]
            for r in range(count):
                for out, (start, width) in zip(outs, cuts):
                    out[lax.bitwise_xor(low, r)] = piece[r, :, start : start + width].astype(f32)


def assemble(cube, pieces, cuts):
    n = cube.count
    count = n // 8
    rows, columns = pieces[0].shape[1:]
    order = []
    for core, corner in (
        (cube.moves.core, cube.corner),
        (1 - cube.moves.core, cube.partner_corner),
    ):
        order += [core * 4 + lax.bitwise_xor(corner // count, i) for i in range(4)]
    order += [cube.corner % count, cube.partner_corner % count]
    order = jnp.stack(order).astype(jnp.int32)

    def piece(index):
        return pl.BlockSpec(
            (count, rows, columns), lambda i, o: (jnp.clip(i - 2 * index, 0, 1), 0, 0)
        )

    outs = pl.pallas_call(
        functools.partial(assemble_kernel, count, cuts),
        grid_spec=pltpu.PrefetchScalarGridSpec(
            num_scalar_prefetch=1,
            grid=(8,),
            in_specs=[piece(index) for index in range(4)],
            out_specs=[
                pl.BlockSpec((count, rows, width), lambda i, o: (o[i], 0, 0))
                for _, width in cuts
            ],
        ),
        out_shape=[jax.ShapeDtypeStruct((n, rows, width), f32) for _, width in cuts],
        compiler_params=pltpu.CompilerParams(vmem_limit_bytes=40 * 1024 * 1024),
        cost_estimate=small_cost(0, n * rows * columns * 2),
        name="assemble",
    )(order, *pieces)
    return [out.reshape(n * rows, width) for out, (_, width) in zip(outs, cuts)]


def add_halves(kept, got):
    half = kept.shape[0] // 2
    return add_low(kept[:half], got[:half]), add_low(kept[half:], got[half:])


class Sum:
    def __init__(self, cube, blocks, cuts):
        self.cube = cube
        self.cuts = cuts
        self.kept, self.sent = blocks
        self.stage = -1

    def step(self):
        cube = self.cube
        stage = self.stage
        self.stage += 1
        if stage < cube.bits:
            got = cube.over_core(self.sent) if stage < 0 else cube.exchange(self.sent, stage)
            if stage == cube.bits - 1:
                self.total = add_low(self.kept, got)
            else:
                self.kept, self.sent = add_halves(self.kept, got)
            return
        back = 2 * cube.bits - 1 - stage
        if back > 0:
            self.total = jnp.concatenate([self.total, cube.exchange(self.total, back)], axis=0)
        elif back == 0:
            self.halves = [self.total, cube.exchange(self.total, 0)]
        else:
            theirs = [cube.over_core(half) for half in self.halves]
            self.out = assemble(cube, [*self.halves, *theirs], self.cuts)

    def tied(self, value):
        if hasattr(self, "halves"):
            *self.halves, value = tie(*self.halves, value)
        elif hasattr(self, "total"):
            self.total, value = tie(self.total, value)
        else:
            self.kept, self.sent, value = tie(self.kept, self.sent, value)
        return value

    @property
    def done(self):
        return self.stage + 1

    def run(self, steps):
        for _ in range(steps):
            self.step()

    @property
    def steps(self):
        return 2 * self.cube.bits + 2


def small_steps(moves):
    steps = []
    for axis, size in (("dp", moves.dp), ("expert", moves.ex)):
        span = 1
        while span < size:
            steps.append((axis, span))
            span *= 2
    return steps


def sum_step(moves, value, axis, span):
    size = moves.dp if axis == "dp" else moves.ex
    return value + lax.ppermute(value, axis, [(i, i ^ span) for i in range(size)])


def on_device(
    hidden_in,
    segment_ids,
    head_experts,
    token_experts,
    attention_gain,
    query_weight,
    key_weight,
    value_weight,
    value_selector,
    output_selector,
    output_weight,
    mixture_gain,
    router_weight,
    up_weight,
    down_weight,
    expert_counts,
    output_cotangent,
):
    moves = Moves()
    nx, nh = moves.nx, moves.nh
    length = hidden_in.shape[1]
    experts = router_weight.shape[1]
    local = up_weight.shape[0]
    expert_range = jnp.arange(experts, dtype=jnp.int32)

    chosen = token_experts[0]
    routed = jnp.sum((chosen[:, :, None] == expert_range[None, None, :]).astype(f32), axis=1)
    local_counts = jnp.sum(routed, axis=0)
    upstream_low = output_cotangent[0]
    near = [s for s in moves.plane[1:] if 0 in s]
    far = [s for s in moves.plane[1:] if 0 not in s]
    routed_low = routed.astype(bf16)

    weights = [jnp.concatenate([up_weight, jnp.swapaxes(down_weight, 1, 2)], axis=2)]
    weights.append(moves.over_hi(weights[0]))
    core_weights = [moves.over_core(weights[0])]
    masks = jnp.pad(routed_low, ((0, 0), (0, -experts % 128)))
    ums = {moves.plane[0]: jnp.concatenate([upstream_low, masks], axis=1)}
    ums[moves.plane[0]], weights[0] = tie(ums[moves.plane[0]], weights[0])
    for s in near:
        ums[s] = moves.over_plane(ums[moves.plane[0]], s)

    inputs = hidden_in[0].astype(f32)
    att_rms = inverse_rms(inputs)
    normed_low = (inputs * att_rms * attention_gain).astype(bf16)
    narrow = 128
    margin = ((0, 0), (0, narrow - H * NE))
    selectors = jnp.concatenate(
        [jnp.pad(value_selector, margin), jnp.pad(output_selector, margin)], axis=1
    )
    head_chosen = jnp.swapaxes(head_experts[0], 0, 1)
    segments = segment_ids[0]
    query_low, key_low, values_all, value_low, mixed, spread_low, sigmoids = attend(
        normed_low, query_weight, key_weight, value_weight, selectors, head_chosen, segments
    )
    middle_rows = inputs + jnp.dot(spread_low, output_weight, preferred_element_type=f32)
    moe_rms = inverse_rms(middle_rows)
    moe_low = (middle_rows * moe_rms * mixture_gain).astype(bf16)

    home = moves.plane[0]
    moe_low, *values = tie(moe_low, *[ums[s] for s in near])
    xs = {home: moe_low}
    for s, value in zip(near, values):
        ums[s] = value
        xs[s] = moves.over_plane(moe_low, s)
    weights[1], xs[home] = tie(weights[1], moe_low)
    core_weights.append(moves.over_core(weights[1]))
    weights.append(moves.over_hi(weights[1]))

    def slot_weights(s):
        return weights[s], core_weights[s]

    def selection(slots):
        columns = []
        for core in (0, 1):
            for s in slots:
                owner = (moves.dp_index ^ core) * moves.ex + (moves.hi - s) % nh * 2 + moves.lo
                columns += [owner * local + k for k in range(local)]
        columns += [jnp.int32(-1)] * (GATE_LANES - len(columns))
        rows = jnp.arange(experts + -experts % 128, dtype=jnp.int32)
        select = (rows[:, None] == jnp.stack(columns)[None, :]).astype(bf16)
        router = jnp.dot(router_weight, select[:experts], preferred_element_type=f32)
        return select, router.astype(bf16)

    sums = {}
    router_sum = jnp.zeros((D, experts + -experts % 128), f32)

    def visit(offsets, phase, carried, finish):
        slots = (2 * phase, 2 * phase + 1)
        select, router = chosen_by[phase]
        previous = None
        if offsets[0] in sums:
            joined = [sums[s] for s in offsets]
            previous = joined[0] if len(joined) == 1 else tuple(
                jnp.concatenate([j[w] for j in joined], axis=0) for w in (0, 1)
            )
        y, dx, *grads = run_experts(
            [xs[s] for s in offsets],
            [ums[s] for s in offsets],
            select,
            router,
            slot_weights(slots[0]),
            slot_weights(slots[1]),
            previous,
            carried,
            finish,
        )
        for k, s in enumerate(offsets):
            sums[s] = (y[k * length : (k + 1) * length], dx[k * length : (k + 1) * length])
        return grads

    phases = nh // 2
    chosen_by = [selection((2 * p, 2 * p + 1)) for p in range(phases)]
    held = None
    sent_back, later = {}, []
    for phase in range(phases):
        last = phase == phases - 1
        if phase == 0:
            calls = [[home], *[[s] for s in near], far]
        elif last:
            calls = [[s] for s in far] + [[s] for s in near] + [[home]]
        else:
            calls = [[home], *[[s] for s in near], far]
        grads = None
        for turn, offsets in enumerate(calls):
            grads = visit(offsets, phase, grads, turn == len(calls) - 1)
            if phase == 0 and turn == 0:
                values = tie(grads[0], moe_low, ums[home], *[xs[s] for s in near])
                grads[0], far_x, far_um = values[:3]
                for s, value in zip(near, values[3:]):
                    xs[s] = value
                for s in far:
                    xs[s] = moves.over_plane(far_x, s)
                    ums[s] = moves.over_plane(far_um, s)
            if phase == 0 and turn == 1 and nh > 2:
                grads[0], weights[2] = tie(grads[0], weights[2])
                for s in range(3, nh):
                    weights.append(moves.over_hi(weights[-1]))
                core_weights.append(moves.over_core(weights[2]))
            if phase == 0 and turn == len(calls) - 2 and nh > 2:
                grads[0], core_weights[2] = tie(grads[0], core_weights[2])
                core_weights += [moves.over_core(w) for w in weights[3:]]
            if phase > 0 and turn == 0:
                grads[0], held = tie(grads[0], held)
                held = moves.over_hi(held)
            if phase > 0 and turn == len(calls) - 2:
                grads[0], held = tie(grads[0], held)
            if last:
                if later:
                    grads[0], *late = tie(grads[0], *[sums[s][0] for s in later])
                    for s, value in zip(later, late):
                        sent_back[s].append(moves.over_plane(value, s, back=True))
                later = [s for s in offsets if s != home]
                for s in later:
                    sent_back[s] = [moves.over_plane(sums[s][1], s, back=True)]
        router_sum = router_sum + jnp.dot(
            grads[2].astype(bf16),
            chosen_by[phase][0].T,
            preferred_element_type=f32,
        )
        mine, got = grads[0], moves.over_core(grads[1])
        for k in range(2):
            s = 2 * phase + k
            parts = [grad[k * local : (k + 1) * local] for grad in (mine, got)]
            if s == 0:
                first_parts = parts
                continue
            if held is not None:
                parts.append(held if k == 0 else moves.over_hi(held))
            held = add_low(*parts)

    expert_delta = sums[home][1].astype(f32)
    for s in moves.plane[1:]:
        expert_delta = expert_delta + sent_back[s][0].astype(f32)

    upstream = upstream_low.astype(f32)
    middle_delta = upstream + norm_back(middle_rows, moe_rms, mixture_gain, expert_delta)
    grad_mixture = jnp.sum(expert_delta * middle_rows * moe_rms, axis=0)
    middle_low = middle_delta.astype(bf16)
    cube = Cube(moves)
    out_sum = Sum(cube, grad_blocks(cube, spread_low, [middle_low]), [(0, D)])
    middle_sent = out_sum.tied(middle_low)
    out_sum.step()
    query_delta, key_delta, values_delta, select_delta = attend_back(
        middle_sent,
        output_weight,
        query_low,
        key_low,
        value_low,
        mixed,
        values_all,
        sigmoids,
        head_chosen,
        segments,
    )
    values_delta = out_sum.tied(values_delta)
    held, values_delta = tie(held, values_delta)
    *outputs_back, values_delta = tie(*[sent_back[s][1] for s in moves.plane[1:]], values_delta)
    out_sum.step()
    value_sum = Sum(cube, grad_blocks(cube, normed_low, [values_delta]), [(0, H * NE * DH)])
    value_sum.step()
    query_delta = value_sum.tied(query_delta)
    cuts = [(0, H * DH), (H * DH, H * DH)]
    start = 2 * H * DH
    cuts += [(start, H * NE), (start + narrow, H * NE), (start + 2 * narrow, experts)]
    rest_sum = Sum(
        cube,
        grad_blocks(cube, normed_low, [query_delta, key_delta, select_delta], router_sum),
        cuts,
    )
    query_sent = rest_sum.tied(query_delta)
    query_sent = out_sum.tied(query_sent)
    for each in (value_sum, rest_sum, out_sum):
        each.step()
    normed_delta = (
        input_term(query_sent, query_weight)
        + input_term(key_delta, key_weight)
        + input_term(values_delta, value_weight)
        + input_term(select_delta, selectors)
    )
    for each in (rest_sum, out_sum, value_sum):
        normed_delta = each.tied(normed_delta)
    grad_attention = jnp.sum(normed_delta * inputs * att_rms, axis=0)
    small = jnp.stack([grad_attention, grad_mixture, jnp.pad(local_counts, (0, D - experts))])
    for axis, span in small_steps(moves):
        small = out_sum.tied(small)
        small = sum_step(moves, small, axis, span)
        for each in (out_sum, rest_sum, value_sum):
            if each.done < each.steps:
                each.step()
    while value_sum.done < 2 * cube.bits - 2:
        for each in (out_sum, rest_sum, value_sum):
            if each.done < each.steps:
                each.step()
    last_held = moves.over_hi(value_sum.tied(held))
    while value_sum.done < value_sum.steps - 1:
        for each in (out_sum, rest_sum, value_sum):
            if each.done < each.steps:
                each.step()
    out_sum.out[0] = value_sum.tied(out_sum.out[0])
    for each in (out_sum, rest_sum, value_sum):
        each.run(each.steps - each.done)
    (grad_output,) = out_sum.out
    (grad_value,) = value_sum.out
    grad_query, grad_key, grad_vselect, grad_oselect, grad_router = rest_sum.out
    input_delta = middle_delta + norm_back(inputs, att_rms, attention_gain, normed_delta)
    output_rows = middle_rows + sums[home][0].astype(f32)
    for value in outputs_back:
        output_rows = output_rows + value.astype(f32)
    expert_grads = last_held.astype(f32)
    for part in first_parts:
        expert_grads = expert_grads + part.astype(f32)
    grad_up, grad_down = expert_grads[:, :, :FF], jnp.swapaxes(expert_grads[:, :, FF:], 1, 2)
    new_counts = expert_counts + small[2, :experts].astype(jnp.int32)
    return (
        output_rows.astype(bf16)[None],
        input_delta[None],
        small[0],
        grad_query,
        grad_key,
        grad_value,
        grad_vselect,
        grad_oselect,
        grad_output,
        small[1],
        grad_router,
        grad_up,
        grad_down,
        new_counts,
    )


def solution(mesh):
    rows3 = P(("dp", "expert"), None, None)
    placed = (
        rows3,
        P(("dp", "expert"), None),
        P(("dp", "expert"), None, None, None),
        rows3,
        *[P()] * 9,
        rows3,
        rows3,
        P(),
        rows3,
    )
    return jax.shard_map(
        on_device,
        mesh=mesh,
        in_specs=placed,
        out_specs=(rows3, rows3, *[P()] * 9, rows3, rows3, P()),
        check_vma=False,
    )
```

```python
import functools

import jax
import jax.numpy as jnp
from jax import lax
from jax.experimental import pallas as pl
from jax.experimental.pallas import tpu as pltpu
from jax.sharding import PartitionSpec as P

D = 1024
H = 4
DH = 128
NE = 5
FF = 128
TOPK = 16
GATE_LANES = 16

epsilon = 1e-06
masked_value = -1e30
bf16 = jnp.bfloat16
f32 = jnp.float32
tanh_scale = 0.7978845608028654
cubic = 0.044715


def inverse_rms(values):
    return lax.rsqrt(jnp.mean(values * values, axis=-1, keepdims=True) + epsilon)


def norm_back(values, scaling, gain, upstream):
    weighted = upstream * gain
    middle = jnp.mean(values * weighted, axis=-1, keepdims=True)
    return scaling * weighted - values * scaling * scaling * scaling * middle


def input_term(delta, weight):
    return jnp.einsum("tc,dc->td", delta, weight, preferred_element_type=f32)


def contract(left, right, left_dim, right_dim):
    return lax.dot_general(
        left, right, (((left_dim,), (right_dim,)), ((), ())), preferred_element_type=f32
    )


def experts_kernel(blocks, pairs, chained, opened, closed, *refs):
    refs = list(refs)

    def take(count):
        taken = refs[:count]
        del refs[:count]
        return taken

    x_hbm, um_hbm = take(blocks), take(blocks)
    select_ref, router_ref = take(2)
    weights = (take(2), take(2))
    y_prev, dx_prev = take(2) if chained else (None, None)
    gu_prev, gd_prev, gr_prev = take(3) if opened else (None, None, None)
    y_ref, dx_ref = take(2)
    grads = take(2)
    (gr_ref,) = take(1)
    (x_buf, u_buf, m_buf, sems, w_up, w_down, w_sems) = take(7)
    (y_acc, dx_acc, gup, gdown, x_turned, u_turned, gate, delta, gr_acc) = take(9)
    gated_buf, hidden_buf = refs
    step = pl.program_id(0)
    pair = pl.program_id(1)
    slot = lax.rem(step, 2)
    local = pairs // 2

    def copies(index, place):
        return (
            pltpu.make_async_copy(x_hbm[index], x_buf.at[place], sems.at[place, 0]),
            pltpu.make_async_copy(
                um_hbm[index].at[:, pl.ds(0, D)], u_buf.at[place], sems.at[place, 1]
            ),
            pltpu.make_async_copy(
                um_hbm[index].at[:, pl.ds(D, m_buf.shape[2])], m_buf.at[place], sems.at[place, 2]
            ),
        )

    def weight_copies(index):
        place = index % 2
        k = index % local
        ways = []
        for side, weight in enumerate(weights[index // local]):
            for part, buffer in enumerate((w_up, w_down)):
                ways.append(
                    pltpu.make_async_copy(
                        weight.at[k, :, pl.ds(part * FF, FF)],
                        buffer.at[place, :, pl.ds(side * FF, FF)],
                        w_sems.at[place, 2 * side + part],
                    )
                )
        return ways

    @pl.when(jnp.logical_and(step == 0, pair == 0))
    def _():
        for copy in (*copies(0, 0), *weight_copies(0)):
            copy.start()

    for index in range(pairs):

        @pl.when(pair == index)
        def _():
            for copy in weight_copies(index):
                copy.wait()
            if index + 1 < pairs:
                for copy in weight_copies(index + 1):
                    copy.start()
            elif blocks > 1:

                @pl.when(step < blocks - 1)
                def _():
                    for copy in weight_copies(0):
                        copy.start()

    @pl.when(pair == 0)
    def _():
        for number in range(blocks):
            place = number % 2

            @pl.when(step == number)
            def _():
                for copy in copies(number, place):
                    copy.wait()
                if number + 1 < blocks:
                    for copy in copies(number + 1, 1 - place):
                        copy.start()

        x = x_buf[slot]
        x_turned[...] = x.T
        u_turned[...] = u_buf[slot].T
        logits = jnp.dot(x, router_ref[...], preferred_element_type=f32)
        chosen = jnp.dot(m_buf[slot], select_ref[...], preferred_element_type=f32)
        gate[...] = jax.nn.sigmoid(logits) * chosen
        delta[...] = jnp.zeros_like(delta)

    @pl.when(pair == 0)
    def _():
        if chained:
            y_acc[...] = y_prev[...].astype(f32)
            dx_acc[...] = dx_prev[...].astype(f32)
        else:
            y_acc[...] = jnp.zeros_like(y_acc)
            dx_acc[...] = jnp.zeros_like(dx_acc)

    tokens = x_buf.shape[1]
    rows = tokens // 2
    which = lax.rem(pair, 2)
    up = w_up[which]
    down = w_down[which]
    lanes = lax.broadcasted_iota(jnp.int32, (rows, GATE_LANES), 1)
    cuts = [pl.ds(c * rows, rows) for c in range(2)]

    def first(cut):
        pre_act = jnp.dot(x_buf[slot, cut], up, preferred_element_type=f32)
        return pre_act, jnp.dot(u_buf[slot, cut], down, preferred_element_type=f32)

    def bend(cut, pre_act, pulled):
        gates = gate[cut]
        gate_a = jnp.sum(jnp.where(lanes == pair, gates, 0.0), axis=1, keepdims=True)
        gate_b = jnp.sum(jnp.where(lanes == pairs + pair, gates, 0.0), axis=1, keepdims=True)
        spread_gate = jnp.concatenate(
            [jnp.broadcast_to(gate_a, (rows, FF)), jnp.broadcast_to(gate_b, (rows, FF))], axis=1
        )
        square = pre_act * pre_act
        bent = jnp.tanh(pre_act * (tanh_scale + tanh_scale * cubic * square))
        half = 0.5 + 0.5 * bent
        hidden = (pre_act * half).astype(bf16).astype(f32)
        slope = half + (0.5 * pre_act) * (1.0 - bent * bent) * (
            tanh_scale + 3.0 * tanh_scale * cubic * square
        )
        felt = hidden * pulled
        felt_a = jnp.sum(felt[:, :FF], axis=1, keepdims=True)
        felt_b = jnp.sum(felt[:, FF:], axis=1, keepdims=True)
        kept = jnp.where(lanes == pair, felt_a, delta[cut])
        delta[cut] = jnp.where(lanes == pairs + pair, felt_b, kept)
        gated_buf[cut] = (spread_gate * hidden).astype(bf16)
        hidden_buf[cut] = (spread_gate * pulled * slope).astype(bf16)

    def second(cut):
        y_acc[cut] += contract(gated_buf[cut], down, 1, 1)
        dx_acc[cut] += contract(hidden_buf[cut], up, 1, 1)

    ready = first(cuts[0])
    for c, cut in enumerate(cuts):
        later = first(cuts[c + 1]) if c + 1 < 2 else None
        bend(cut, *ready)
        second(cut)
        ready = later
    gd_new = jnp.dot(u_turned[...], gated_buf[...], preferred_element_type=f32)
    gu_new = jnp.dot(x_turned[...], hidden_buf[...], preferred_element_type=f32)

    def put(gu_out, gd_out):
        if closed:
            for side in (0, 1):
                grads[side][0, :, :FF] = gu_out[:, side * FF : (side + 1) * FF].astype(bf16)
                grads[side][0, :, FF:] = gd_out[:, side * FF : (side + 1) * FF].astype(bf16)
        else:
            grads[0][0] = gu_out
            grads[1][0] = gd_out

    if blocks == 1:
        if opened:
            gd_new = gd_prev[0] + gd_new
            gu_new = gu_prev[0] + gu_new
        put(gu_new, gd_new)
    else:

        @pl.when(step == 0)
        def _():
            if opened:
                gdown[pair] = gd_prev[0]
                gup[pair] = gu_prev[0]
            else:
                gdown[pair] = jnp.zeros_like(gd_new)
                gup[pair] = jnp.zeros_like(gu_new)

        gdown[pair] += gd_new
        gup[pair] += gu_new

        @pl.when(step == blocks - 1)
        def _():
            put(gup[pair], gdown[pair])

    @pl.when(pair == pairs - 1)
    def _():
        gates_now = gate[...]
        logit_delta = (delta[...] * gates_now * (1.0 - gates_now)).astype(bf16)
        y_ref[...] = y_acc[...].astype(bf16)
        dx_ref[...] = (dx_acc[...] + contract(logit_delta, router_ref[...], 1, 1)).astype(bf16)
        gr_new = jnp.dot(x_turned[...], logit_delta, preferred_element_type=f32)

        @pl.when(step == 0)
        def _():
            if opened:
                gr_acc[...] = gr_prev[...] + gr_new
            else:
                gr_acc[...] = gr_new

        @pl.when(step > 0)
        def _():
            gr_acc[...] += gr_new

        @pl.when(step == blocks - 1)
        def _():
            gr_ref[...] = gr_acc[...]


def run_experts(xs, ums, select, router, first, second, previous, carried, finish):
    blocks = len(xs)
    local = first[0].shape[0]
    pairs = 2 * local
    tokens = xs[0].shape[0]
    experts = select.shape[0]

    def block(i, j):
        return (i, 0)

    def whole(i, j):
        return (0, 0)

    def opening(i, j):
        return (jnp.where(i == 0, j, pairs - 1), 0, 0)

    def closing(i, j):
        return (jnp.where(i == blocks - 1, j, 0), 0, 0)

    anywhere = pl.BlockSpec(memory_space=pl.ANY)
    in_specs = [anywhere] * (2 * blocks) + [
        pl.BlockSpec((experts, GATE_LANES), whole),
        pl.BlockSpec((D, GATE_LANES), whole),
        *[anywhere] * 4,
    ]
    operands = [*xs, *ums, select, router, *first, *second]
    if previous is not None:
        in_specs += [pl.BlockSpec((tokens, D), block)] * 2
        operands += list(previous)
    if carried is not None:
        in_specs += [
            pl.BlockSpec((1, D, 2 * FF), opening),
            pl.BlockSpec((1, D, 2 * FF), opening),
            pl.BlockSpec((D, GATE_LANES), whole),
        ]
        operands += list(carried)
    out_shape = [jax.ShapeDtypeStruct((blocks * tokens, D), bf16)] * 2
    out_specs = [pl.BlockSpec((tokens, D), block)] * 2
    if finish:
        out_shape += [jax.ShapeDtypeStruct((pairs, D, 2 * FF), bf16)] * 2
    else:
        out_shape += [jax.ShapeDtypeStruct((pairs, D, 2 * FF), f32)] * 2
    out_specs += [pl.BlockSpec((1, D, 2 * FF), closing)] * 2
    out_shape.append(jax.ShapeDtypeStruct((D, GATE_LANES), f32))
    out_specs.append(pl.BlockSpec((D, GATE_LANES), whole))
    kept = pairs if blocks > 1 else 1
    return pl.pallas_call(
        functools.partial(
            experts_kernel, blocks, pairs, previous is not None, carried is not None, finish
        ),
        grid=(blocks, pairs),
        in_specs=in_specs,
        out_specs=out_specs,
        out_shape=out_shape,
        scratch_shapes=[
            pltpu.VMEM((2, tokens, D), bf16),
            pltpu.VMEM((2, tokens, D), bf16),
            pltpu.VMEM((2, tokens, experts), bf16),
            pltpu.SemaphoreType.DMA((2, 3)),
            pltpu.VMEM((2, D, 2 * FF), bf16),
            pltpu.VMEM((2, D, 2 * FF), bf16),
            pltpu.SemaphoreType.DMA((2, 4)),
            pltpu.VMEM((tokens, D), f32),
            pltpu.VMEM((tokens, D), f32),
            pltpu.VMEM((kept, D, 2 * FF), f32),
            pltpu.VMEM((kept, D, 2 * FF), f32),
            pltpu.VMEM((D, tokens), bf16),
            pltpu.VMEM((D, tokens), bf16),
            pltpu.VMEM((tokens, GATE_LANES), f32),
            pltpu.VMEM((tokens, GATE_LANES), f32),
            pltpu.VMEM((D, GATE_LANES), f32),
            pltpu.VMEM((tokens, 2 * FF), bf16),
            pltpu.VMEM((tokens, 2 * FF), bf16),
        ],
        compiler_params=pltpu.CompilerParams(
            dimension_semantics=("arbitrary", "arbitrary"),
            vmem_limit_bytes=56 * 1024 * 1024,
        ),
        cost_estimate=pl.CostEstimate(
            flops=12 * blocks * tokens * D * FF * pairs, bytes_accessed=0, transcendentals=0
        ),
        name="experts",
    )(*operands)


def column(values, index):
    lanes = lax.broadcasted_iota(jnp.int32, values.shape, 1)
    return jnp.sum(jnp.where(lanes == index, values, 0.0), axis=1, keepdims=True)


def head_probs(query, key, segment_col, segment_row):
    raw = contract(query, key, 1, 1) * DH ** (-0.5)
    rows = lax.broadcasted_iota(jnp.int32, raw.shape, 0)
    columns = lax.broadcasted_iota(jnp.int32, raw.shape, 1)
    allowed = jnp.logical_and(columns <= rows, segment_col == segment_row)
    scores = jnp.where(allowed, raw, masked_value)
    powers = jnp.exp(scores - jnp.max(scores, axis=1, keepdims=True))
    return powers * (1.0 / jnp.sum(powers, axis=1, keepdims=True))


def head_sigmoids(head, chosen_ref, sigmoids, expert):
    first, second = chosen_ref[0, :, 0:1], chosen_ref[0, :, 1:2]
    chosen = jnp.logical_or(first == expert, second == expert).astype(f32)
    half = sigmoids.shape[1] // 2
    place = head * NE + expert
    return chosen, column(sigmoids[:, :half], place), column(sigmoids[:, half:], place)


def part(expert):
    return slice(expert * DH, (expert + 1) * DH)


def attend_kernel(
    normed_ref,
    query_weight,
    key_weight,
    value_weight,
    selectors,
    chosen_ref,
    segment_col,
    segment_row,
    query_ref,
    key_ref,
    values_ref,
    low_ref,
    mixed_ref,
    spread_ref,
    sigmoids_ref,
):
    head = pl.program_id(0)
    normed = normed_ref[...]

    @pl.when(head == 0)
    def _():
        sigmoids_ref[...] = jax.nn.sigmoid(
            jnp.dot(normed, selectors[...], preferred_element_type=f32)
        )

    query = jnp.dot(normed, query_weight[...], preferred_element_type=f32).astype(bf16)
    key = jnp.dot(normed, key_weight[...], preferred_element_type=f32).astype(bf16)
    query_ref[...] = query
    key_ref[...] = key
    values_ref[...] = jnp.dot(normed, value_weight[...], preferred_element_type=f32)
    sigmoids = sigmoids_ref[...]
    gates = [head_sigmoids(head, chosen_ref, sigmoids, e) for e in range(NE)]
    low = gates[0][0] * gates[0][1] * values_ref[:, part(0)]
    for e in range(1, NE):
        low = low + gates[e][0] * gates[e][1] * values_ref[:, part(e)]
    low = low.astype(bf16)
    low_ref[...] = low
    probs = head_probs(query, key, segment_col[...], segment_row[...]).astype(bf16)
    mixed = jnp.dot(probs, low, preferred_element_type=f32)
    mixed_ref[...] = mixed
    for e in range(NE):
        spread_ref[:, part(e)] = (gates[e][0] * gates[e][2] * mixed).astype(bf16)


def attend_specs(tokens):
    whole = pl.BlockSpec((tokens, D), lambda h: (0, 0))
    narrow = pl.BlockSpec((tokens, DH), lambda h: (0, h))
    wide = pl.BlockSpec((tokens, NE * DH), lambda h: (0, h))
    rest = [
        pl.BlockSpec((1, tokens, 2), lambda h: (h, 0, 0)),
        pl.BlockSpec((tokens, 1), lambda h: (0, 0)),
        pl.BlockSpec((1, tokens), lambda h: (0, 0)),
    ]
    sigmoids = pl.BlockSpec((tokens, 256), lambda h: (0, 0))
    return whole, narrow, wide, rest, sigmoids


def attend(normed, query_weight, key_weight, value_weight, selectors, chosen, segments):
    tokens = normed.shape[0]
    whole, narrow, wide, rest, sigmoids = attend_specs(tokens)
    return pl.pallas_call(
        attend_kernel,
        grid=(H,),
        in_specs=[
            whole,
            pl.BlockSpec((D, DH), lambda h: (0, h)),
            pl.BlockSpec((D, DH), lambda h: (0, h)),
            pl.BlockSpec((D, NE * DH), lambda h: (0, h)),
            pl.BlockSpec((D, 256), lambda h: (0, 0)),
            *rest,
        ],
        out_specs=[narrow, narrow, wide, narrow, narrow, wide, sigmoids],
        out_shape=[
            jax.ShapeDtypeStruct((tokens, H * DH), bf16),
            jax.ShapeDtypeStruct((tokens, H * DH), bf16),
            jax.ShapeDtypeStruct((tokens, H * NE * DH), f32),
            jax.ShapeDtypeStruct((tokens, H * DH), bf16),
            jax.ShapeDtypeStruct((tokens, H * DH), f32),
            jax.ShapeDtypeStruct((tokens, H * NE * DH), bf16),
            jax.ShapeDtypeStruct((tokens, 256), f32),
        ],
        compiler_params=pltpu.CompilerParams(vmem_limit_bytes=48 * 1024 * 1024),
        cost_estimate=pl.CostEstimate(
            flops=2 * tokens * H * DH * (D * (NE + 2) + 2 * tokens),
            bytes_accessed=0,
            transcendentals=0,
        ),
        name="attend",
    )(
        normed,
        query_weight,
        key_weight,
        value_weight,
        selectors,
        chosen,
        segments[:, None],
        segments[None, :],
    )


def attend_back_kernel(
    middle_ref,
    output_weight,
    query_ref,
    key_ref,
    low_ref,
    mixed_ref,
    values_ref,
    sigmoids_ref,
    chosen_ref,
    segment_col,
    segment_row,
    query_delta,
    key_delta,
    values_delta,
    select_delta,
    spread_buf,
    value_acc,
    output_acc,
):
    head = pl.program_id(0)

    @pl.when(head == 0)
    def _():
        value_acc[...] = jnp.zeros_like(value_acc)
        output_acc[...] = jnp.zeros_like(output_acc)

    spread_buf[...] = contract(middle_ref[...], output_weight[...], 1, 1)
    sigmoids = sigmoids_ref[...]
    gates = [head_sigmoids(head, chosen_ref, sigmoids, e) for e in range(NE)]
    query, key, low = query_ref[...], key_ref[...], low_ref[...]
    mixed = mixed_ref[...]
    mixed_delta = gates[0][0] * gates[0][2] * spread_buf[:, part(0)]
    for e in range(1, NE):
        mixed_delta = mixed_delta + gates[e][0] * gates[e][2] * spread_buf[:, part(e)]
    mixed_delta = mixed_delta.astype(bf16)
    probs = head_probs(query, key, segment_col[...], segment_row[...])
    weight_delta = contract(mixed_delta, low, 1, 1)
    pulled = jnp.sum(probs * weight_delta, axis=1, keepdims=True)
    score_delta = (probs * (weight_delta - pulled)).astype(bf16)
    query_delta[...] = (
        jnp.dot(score_delta, key, preferred_element_type=f32) * DH ** (-0.5)
    ).astype(bf16)
    key_delta[...] = (contract(score_delta, query, 0, 0) * DH ** (-0.5)).astype(bf16)
    value_delta = contract(probs.astype(bf16), mixed_delta, 0, 0)
    lanes = lax.broadcasted_iota(jnp.int32, value_acc.shape, 1)
    for e in range(NE):
        chosen, value_sigmoid, output_sigmoid = gates[e]
        values_delta[:, part(e)] = (chosen * value_sigmoid * value_delta).astype(bf16)
        felt = jnp.sum(value_delta * values_ref[:, part(e)], axis=1, keepdims=True)
        felt = felt * chosen * value_sigmoid * (1.0 - value_sigmoid)
        value_acc[...] = jnp.where(lanes == head * NE + e, felt, value_acc[...])
        felt = jnp.sum(spread_buf[:, part(e)] * mixed, axis=1, keepdims=True)
        felt = felt * chosen * output_sigmoid * (1.0 - output_sigmoid)
        output_acc[...] = jnp.where(lanes == head * NE + e, felt, output_acc[...])

    @pl.when(head == H - 1)
    def _():
        half = value_acc.shape[1]
        select_delta[:, :half] = value_acc[...].astype(bf16)
        select_delta[:, half:] = output_acc[...].astype(bf16)


def attend_back(middle_low, output_weight, query, key, low, mixed, values, sigmoids, chosen, segments):
    tokens = middle_low.shape[0]
    whole, narrow, wide, rest, sigmoid_spec = attend_specs(tokens)
    return pl.pallas_call(
        attend_back_kernel,
        grid=(H,),
        in_specs=[
            whole,
            pl.BlockSpec((NE * DH, D), lambda h: (h, 0)),
            narrow,
            narrow,
            narrow,
            narrow,
            wide,
            sigmoid_spec,
            *rest,
        ],
        out_specs=[narrow, narrow, wide, sigmoid_spec],
        out_shape=[
            jax.ShapeDtypeStruct((tokens, H * DH), bf16),
            jax.ShapeDtypeStruct((tokens, H * DH), bf16),
            jax.ShapeDtypeStruct((tokens, H * NE * DH), bf16),
            jax.ShapeDtypeStruct((tokens, 256), bf16),
        ],
        scratch_shapes=[
            pltpu.VMEM((tokens, NE * DH), f32),
            pltpu.VMEM((tokens, 128), f32),
            pltpu.VMEM((tokens, 128), f32),
        ],
        compiler_params=pltpu.CompilerParams(vmem_limit_bytes=48 * 1024 * 1024),
        cost_estimate=pl.CostEstimate(
            flops=2 * tokens * H * DH * (D * NE + 5 * tokens), bytes_accessed=0, transcendentals=0
        ),
        name="attend_back",
    )(
        middle_low,
        output_weight,
        query,
        key,
        low,
        mixed,
        values,
        sigmoids,
        chosen,
        segments[:, None],
        segments[None, :],
    )


class Moves:
    def __init__(self):
        self.dp = lax.axis_size("dp")
        self.ex = lax.axis_size("expert")
        self.nx = self.dp // 2
        self.nh = self.ex // 2
        self.dp_index = lax.axis_index("dp")
        self.ex_index = lax.axis_index("expert")
        self.core = self.dp_index % 2
        self.x = self.dp_index // 2
        self.lo = self.ex_index % 2
        self.hi = self.ex_index // 2
        steps = [(a, b) for a in range(self.nx) for b in range(2)]
        self.plane = sorted(steps, key=lambda s: ((s[0] > 0) + (s[1] > 0), s))

    def over_core(self, value):
        return lax.ppermute(value, "dp", [(i, i ^ 1) for i in range(self.dp)])

    def over_hi(self, value, by=1):
        pairs = [(i, (i // 2 + by) % self.nh * 2 + i % 2) for i in range(self.ex)]
        return lax.ppermute(value, "expert", pairs)

    def over_plane(self, value, offset, back=False):
        a, b = offset
        if back:
            a = (self.nx - a) % self.nx
        if a == 0:
            return lax.ppermute(value, "expert", [(i, i ^ b) for i in range(self.ex)])
        dp_to = [(i // 2 + a) % self.nx * 2 + i % 2 for i in range(self.dp)]
        if b == 0:
            return lax.ppermute(value, "dp", list(enumerate(dp_to)))
        pairs = [
            (i * self.ex + j, dp_to[i] * self.ex + (j ^ 1))
            for i in range(self.dp)
            for j in range(self.ex)
        ]
        return lax.ppermute(value, ("dp", "expert"), pairs)


def add_low(*terms):
    total = terms[0].astype(f32)
    for term in terms[1:]:
        total = total + term.astype(f32)
    return total.astype(bf16)


def tie(*values):
    return lax.optimization_barrier(values)


class Cube:
    def __init__(self, moves):
        self.moves = moves
        ex = moves.ex
        across = [1 << i for i in range(1, moves.dp.bit_length() - 1)]
        along = [1 << i for i in range(ex.bit_length() - 1)]
        across = [mask * ex for mask in across]
        self.flips = (across + along, along[:1] + across + along[1:])
        self.core_flip = ex
        self.count = moves.dp * ex
        self.bits = len(along) + len(across)
        place = moves.dp_index * ex + moves.ex_index
        corners = []
        for flips in self.flips:
            corner = jnp.int32(0)
            for flip in flips:
                corner = corner * 2 + (place // flip) % 2
            corners.append(corner)
        mine = moves.core == 0
        self.corner = jnp.where(mine, corners[0], corners[1])
        self.partner_corner = jnp.where(mine, corners[1], corners[0])

    def exchange(self, value, stage):
        ex = self.moves.ex
        pairs = [
            (i, i ^ self.flips[i // ex % 2][stage]) for i in range(self.count)
        ]
        return lax.ppermute(value, ("dp", "expert"), pairs)

    def over_core(self, value):
        return self.moves.over_core(value)


def small_cost(flops, moved):
    return pl.CostEstimate(flops=flops, bytes_accessed=moved, transcendentals=0)


def grad_blocks_kernel(steps, group, rows, count, order_ref, left_a, left_b, *refs):
    rights, refs = refs[:count], refs[count:]
    out_a, out_b = refs[-2:]
    added = refs[:-2]
    for which, (left, out) in enumerate(((left_a, out_a), (left_b, out_b))):
        low = order_ref[2 * steps + which]
        turned = left[...]
        start = 0
        for right in rights:
            width = right.shape[1]
            product = contract(turned, right[...], 0, 0)
            for h in range(group):
                out[lax.bitwise_xor(low, h), :, start : start + width] = product[
                    h * rows : (h + 1) * rows
                ].astype(bf16)
            start += width
        if added:
            block = added[which][...]
            width = block.shape[1]
            for h in range(group):
                out[lax.bitwise_xor(low, h), :, start : start + width] = block[
                    h * rows : (h + 1) * rows
                ].astype(bf16)


def grad_blocks(cube, left, rights, added=None):
    n = cube.count
    total = left.shape[1]
    tokens = left.shape[0]
    rows = total // n
    group = 1
    while rows * group % 128:
        group *= 2
    wide = rows * group
    steps = n // 2 // group
    core = cube.moves.core
    order = [core * steps + lax.bitwise_xor(cube.corner // group, i) for i in range(steps)]
    order += [
        (1 - core) * steps + lax.bitwise_xor(cube.partner_corner // group, i) for i in range(steps)
    ]
    order += [cube.corner % group, cube.partner_corner % group]
    order = jnp.stack(order).astype(jnp.int32)
    columns = sum(r.shape[1] for r in rights) + (0 if added is None else added.shape[1])
    in_specs = [
        pl.BlockSpec((tokens, wide), lambda i, o: (0, o[i])),
        pl.BlockSpec((tokens, wide), lambda i, o: (0, o[steps + i])),
        *[pl.BlockSpec(r.shape, lambda i, o: (0, 0)) for r in rights],
    ]
    operands = [left, left, *rights]
    if added is not None:
        in_specs += [
            pl.BlockSpec((wide, added.shape[1]), lambda i, o: (o[i], 0)),
            pl.BlockSpec((wide, added.shape[1]), lambda i, o: (o[steps + i], 0)),
        ]
        operands += [added, added]
    shape = jax.ShapeDtypeStruct((n // 2, rows, columns), bf16)
    return pl.pallas_call(
        functools.partial(grad_blocks_kernel, steps, group, rows, len(rights)),
        grid_spec=pltpu.PrefetchScalarGridSpec(
            num_scalar_prefetch=1,
            grid=(steps,),
            in_specs=in_specs,
            out_specs=[pl.BlockSpec((group, rows, columns), lambda i, o: (i, 0, 0))] * 2,
        ),
        out_shape=[shape, shape],
        compiler_params=pltpu.CompilerParams(vmem_limit_bytes=40 * 1024 * 1024),
        cost_estimate=small_cost(tokens * total * columns, total * columns * 2),
        name="grad_blocks",
    )(order, *operands)


def lanes_of(width):
    return width + -width % 128


def assemble_kernel(count, cuts, order_ref, *refs):
    pieces, outs, buffers = refs[:4], refs[4 : 4 + len(cuts)], refs[4 + len(cuts) :]
    step = pl.program_id(0)
    for index, piece in enumerate(pieces):

        @pl.when(step // 2 == index)
        def _():
            low = order_ref[8 + index // 2]
            rows = piece.shape[1]
            for r in range(count):
                place = lax.bitwise_xor(low, r)
                for out, buffer, (start, width) in zip(outs, buffers, cuts):
                    if width % 128:
                        block = piece[r, :, start : start + lanes_of(width)].astype(f32)
                        buffer[pl.ds(pl.multiple_of(place * rows, rows), rows), :] = block
                    else:
                        out[place] = piece[r, :, start : start + width].astype(f32)
            for out, buffer, (_, width) in zip(outs, buffers, cuts):
                if width % 128:
                    out[...] = buffer[...].T[:width]


def assemble(cube, pieces, cuts):
    n = cube.count
    count = n // 8
    rows, columns = pieces[0].shape[1:]
    order = []
    for core, corner in (
        (cube.moves.core, cube.corner),
        (1 - cube.moves.core, cube.partner_corner),
    ):
        order += [core * 4 + lax.bitwise_xor(corner // count, i) for i in range(4)]
    order += [cube.corner % count, cube.partner_corner % count]
    order = jnp.stack(order).astype(jnp.int32)

    def piece(index):
        return pl.BlockSpec(
            (count, rows, columns), lambda i, o: (jnp.clip(i - 2 * index, 0, 1), 0, 0)
        )

    outs = pl.pallas_call(
        functools.partial(assemble_kernel, count, cuts),
        grid_spec=pltpu.PrefetchScalarGridSpec(
            num_scalar_prefetch=1,
            grid=(8,),
            in_specs=[piece(index) for index in range(4)],
            out_specs=[
                pl.BlockSpec((width, count * rows), lambda i, o: (0, o[i]))
                if width % 128
                else pl.BlockSpec((count, rows, width), lambda i, o: (o[i], 0, 0))
                for _, width in cuts
            ],
            scratch_shapes=[
                pltpu.VMEM((count * rows, lanes_of(width)) if width % 128 else (8, 128), f32)
                for _, width in cuts
            ],
        ),
        out_shape=[
            jax.ShapeDtypeStruct((width, n * rows) if width % 128 else (n, rows, width), f32)
            for _, width in cuts
        ],
        compiler_params=pltpu.CompilerParams(vmem_limit_bytes=40 * 1024 * 1024),
        cost_estimate=small_cost(0, n * rows * columns * 2),
        name="assemble",
    )(order, *pieces)
    return [
        out.T if width % 128 else out.reshape(n * rows, width)
        for out, (_, width) in zip(outs, cuts)
    ]


def add_halves(kept, got):
    half = kept.shape[0] // 2
    return add_low(kept[:half], got[:half]), add_low(kept[half:], got[half:])


class Sum:
    def __init__(self, cube, blocks, cuts):
        self.cube = cube
        self.cuts = cuts
        self.kept, self.sent = blocks
        self.stage = -1

    def step(self):
        cube = self.cube
        stage = self.stage
        self.stage += 1
        if stage < cube.bits:
            got = cube.over_core(self.sent) if stage < 0 else cube.exchange(self.sent, stage)
            if stage == cube.bits - 1:
                self.total = add_low(self.kept, got)
            else:
                self.kept, self.sent = add_halves(self.kept, got)
            return
        back = 2 * cube.bits - 1 - stage
        if back > 0:
            self.total = jnp.concatenate([self.total, cube.exchange(self.total, back)], axis=0)
        elif back == 0:
            self.halves = [self.total, cube.exchange(self.total, 0)]
        else:
            theirs = [cube.over_core(half) for half in self.halves]
            self.out = assemble(cube, [*self.halves, *theirs], self.cuts)

    def tied(self, value):
        if hasattr(self, "halves"):
            *self.halves, value = tie(*self.halves, value)
        elif hasattr(self, "total"):
            self.total, value = tie(self.total, value)
        else:
            self.kept, self.sent, value = tie(self.kept, self.sent, value)
        return value

    @property
    def done(self):
        return self.stage + 1

    def run(self, steps):
        for _ in range(steps):
            self.step()

    @property
    def steps(self):
        return 2 * self.cube.bits + 2


def small_steps(moves):
    steps = []
    for axis, size in (("dp", moves.dp), ("expert", moves.ex)):
        span = 1
        while span < size:
            steps.append((axis, span))
            span *= 2
    return steps


def sum_step(moves, value, axis, span):
    size = moves.dp if axis == "dp" else moves.ex
    return value + lax.ppermute(value, axis, [(i, i ^ span) for i in range(size)])


def on_device(
    hidden_in,
    segment_ids,
    head_experts,
    token_experts,
    attention_gain,
    query_weight,
    key_weight,
    value_weight,
    value_selector,
    output_selector,
    output_weight,
    mixture_gain,
    router_weight,
    up_weight,
    down_weight,
    expert_counts,
    output_cotangent,
):
    moves = Moves()
    nx, nh = moves.nx, moves.nh
    length = hidden_in.shape[1]
    experts = router_weight.shape[1]
    local = up_weight.shape[0]
    expert_range = jnp.arange(experts, dtype=jnp.int32)

    chosen = token_experts[0]
    routed = jnp.sum((chosen[:, :, None] == expert_range[None, None, :]).astype(f32), axis=1)
    local_counts = jnp.sum(routed, axis=0)
    upstream_low = output_cotangent[0]
    near = [s for s in moves.plane[1:] if 0 in s]
    far = [s for s in moves.plane[1:] if 0 not in s]
    routed_low = routed.astype(bf16)

    weights = [jnp.concatenate([up_weight, jnp.swapaxes(down_weight, 1, 2)], axis=2)]
    weights.append(moves.over_hi(weights[0]))
    core_weights = [moves.over_core(weights[0])]
    masks = jnp.pad(routed_low, ((0, 0), (0, -experts % 128)))
    ums = {moves.plane[0]: jnp.concatenate([upstream_low, masks], axis=1)}
    ums[moves.plane[0]], weights[0] = tie(ums[moves.plane[0]], weights[0])
    for s in near:
        ums[s] = moves.over_plane(ums[moves.plane[0]], s)

    inputs = hidden_in[0].astype(f32)
    att_rms = inverse_rms(inputs)
    normed_low = (inputs * att_rms * attention_gain).astype(bf16)
    narrow = 128
    margin = ((0, 0), (0, narrow - H * NE))
    selectors = jnp.concatenate(
        [jnp.pad(value_selector, margin), jnp.pad(output_selector, margin)], axis=1
    )
    head_chosen = jnp.swapaxes(head_experts[0], 0, 1)
    segments = segment_ids[0]
    query_low, key_low, values_all, value_low, mixed, spread_low, sigmoids = attend(
        normed_low, query_weight, key_weight, value_weight, selectors, head_chosen, segments
    )
    middle_rows = inputs + jnp.dot(spread_low, output_weight, preferred_element_type=f32)
    moe_rms = inverse_rms(middle_rows)
    moe_low = (middle_rows * moe_rms * mixture_gain).astype(bf16)

    home = moves.plane[0]
    moe_low, *values = tie(moe_low, *[ums[s] for s in near])
    xs = {home: moe_low}
    for s, value in zip(near, values):
        ums[s] = value
        xs[s] = moves.over_plane(moe_low, s)
    weights[1], xs[home] = tie(weights[1], moe_low)
    core_weights.append(moves.over_core(weights[1]))
    weights.append(moves.over_hi(weights[1]))

    def slot_weights(s):
        return weights[s], core_weights[s]

    def selection(slots):
        columns = []
        for core in (0, 1):
            for s in slots:
                owner = (moves.dp_index ^ core) * moves.ex + (moves.hi - s) % nh * 2 + moves.lo
                columns += [owner * local + k for k in range(local)]
        columns += [jnp.int32(-1)] * (GATE_LANES - len(columns))
        rows = jnp.arange(experts + -experts % 128, dtype=jnp.int32)
        select = (rows[:, None] == jnp.stack(columns)[None, :]).astype(bf16)
        router = jnp.dot(router_weight, select[:experts], preferred_element_type=f32)
        return select, router.astype(bf16)

    sums = {}
    router_sum = jnp.zeros((D, experts + -experts % 128), f32)

    def visit(offsets, phase, carried, finish):
        slots = (2 * phase, 2 * phase + 1)
        select, router = chosen_by[phase]
        previous = None
        if offsets[0] in sums:
            joined = [sums[s] for s in offsets]
            previous = joined[0] if len(joined) == 1 else tuple(
                jnp.concatenate([j[w] for j in joined], axis=0) for w in (0, 1)
            )
        y, dx, *grads = run_experts(
            [xs[s] for s in offsets],
            [ums[s] for s in offsets],
            select,
            router,
            slot_weights(slots[0]),
            slot_weights(slots[1]),
            previous,
            carried,
            finish,
        )
        for k, s in enumerate(offsets):
            sums[s] = (y[k * length : (k + 1) * length], dx[k * length : (k + 1) * length])
        return grads

    phases = nh // 2
    chosen_by = [selection((2 * p, 2 * p + 1)) for p in range(phases)]
    held = None
    sent_back, outputs_back, later = {}, [], []
    for phase in range(phases):
        last = phase == phases - 1
        if phase == 0:
            calls = [[home], *[[s] for s in near], far]
        elif last:
            calls = [[s] for s in far] + [[s] for s in near] + [[home]]
        else:
            calls = [[home], *[[s] for s in near], far]
        grads = None
        for turn, offsets in enumerate(calls):
            grads = visit(offsets, phase, grads, turn == len(calls) - 1)
            if phase == 0 and turn == 0:
                values = tie(grads[0], moe_low, ums[home], *[xs[s] for s in near])
                grads[0], far_x, far_um = values[:3]
                for s, value in zip(near, values[3:]):
                    xs[s] = value
                for s in far:
                    ums[s] = moves.over_plane(far_um, s)
            if phase == 0 and turn == 1:
                grads[0], far_x, *values = tie(grads[0], far_x, *[ums[s] for s in far])
                for s, value in zip(far, values):
                    ums[s] = value
                    xs[s] = moves.over_plane(far_x, s)
            if phase == 0 and turn == 1 and nh > 2:
                grads[0], weights[2] = tie(grads[0], weights[2])
                for s in range(3, nh):
                    weights.append(moves.over_hi(weights[-1]))
                core_weights.append(moves.over_core(weights[2]))
            if phase == 0 and turn == len(calls) - 2 and nh > 2:
                grads[0], core_weights[2] = tie(grads[0], core_weights[2])
                core_weights += [moves.over_core(w) for w in weights[3:]]
            if phase > 0 and turn == 0:
                grads[0], held = tie(grads[0], held)
                held = moves.over_hi(held)
            if phase > 0 and turn == len(calls) - 2:
                grads[0], held = tie(grads[0], held)
            if last:
                if later:
                    grads[0], *late = tie(grads[0], *[sums[s][0] for s in later])
                    for s, value in zip(later, late):
                        if s in far:
                            outputs_back.append(moves.over_plane(value, s, back=True))
                later = [s for s in offsets if s != home]
                for s in later:
                    sent_back[s] = [moves.over_plane(sums[s][1], s, back=True)]
        router_sum = router_sum + jnp.dot(
            grads[2].astype(bf16),
            chosen_by[phase][0].T,
            preferred_element_type=f32,
        )
        mine, got = grads[0], moves.over_core(grads[1])
        if last and phase > 0:
            continue
        for k in range(2):
            s = 2 * phase + k
            parts = [grad[k * local : (k + 1) * local] for grad in (mine, got)]
            if s == 0:
                first_parts = parts
                continue
            if held is not None:
                parts.append(held if k == 0 else moves.over_hi(held))
            held = add_low(*parts)

    expert_delta = sums[home][1].astype(f32)
    for s in moves.plane[1:]:
        expert_delta = expert_delta + sent_back[s][0].astype(f32)

    upstream = upstream_low.astype(f32)
    middle_delta = upstream + norm_back(middle_rows, moe_rms, mixture_gain, expert_delta)
    grad_mixture = jnp.sum(expert_delta * middle_rows * moe_rms, axis=0)
    middle_low = middle_delta.astype(bf16)
    cube = Cube(moves)
    out_sum = Sum(cube, grad_blocks(cube, spread_low, [middle_low]), [(0, D)])
    middle_sent = out_sum.tied(middle_low)
    if phases > 1:
        got, middle_sent = tie(got, middle_sent)
        passed = moves.over_hi(add_low(mine[:local], got[:local], held))
        held = add_low(mine[local:], got[local:], passed)
    out_sum.step()
    query_delta, key_delta, values_delta, select_delta = attend_back(
        middle_sent,
        output_weight,
        query_low,
        key_low,
        value_low,
        mixed,
        values_all,
        sigmoids,
        head_chosen,
        segments,
    )
    out_sum.step()
    held, *outputs_back, values_delta = tie(held, *outputs_back, values_delta)
    values_delta = out_sum.tied(values_delta)
    out_sum.step()
    value_sum = Sum(cube, grad_blocks(cube, normed_low, [values_delta]), [(0, H * NE * DH)])
    value_sum.step()
    query_delta = value_sum.tied(query_delta)
    query_delta = out_sum.tied(query_delta)
    cuts = [(0, H * DH), (H * DH, H * DH)]
    start = 2 * H * DH
    cuts += [(start, H * NE), (start + narrow, H * NE), (start + 2 * narrow, experts)]
    rest_sum = Sum(
        cube,
        grad_blocks(cube, normed_low, [query_delta, key_delta, select_delta], router_sum),
        cuts,
    )
    query_sent = rest_sum.tied(query_delta)
    query_sent = out_sum.tied(query_sent)
    for each in (value_sum, rest_sum, out_sum):
        each.step()
    normed_delta = (
        input_term(query_sent, query_weight)
        + input_term(key_delta, key_weight)
        + input_term(values_delta, value_weight)
        + input_term(select_delta, selectors)
    )
    for each in (rest_sum, out_sum, value_sum):
        normed_delta = each.tied(normed_delta)
    grad_attention = jnp.sum(normed_delta * inputs * att_rms, axis=0)
    small = jnp.stack([grad_attention, grad_mixture, jnp.pad(local_counts, (0, D - experts))])
    for axis, span in small_steps(moves):
        small = rest_sum.tied(out_sum.tied(small))
        small = sum_step(moves, small, axis, span)
        for each in (out_sum, rest_sum, value_sum):
            if each.done < each.steps:
                each.step()
    small = out_sum.tied(small)
    while rest_sum.done < 2 * cube.bits - 1:
        for each in (out_sum, rest_sum, value_sum):
            if each.done < each.steps:
                each.step()
    last_held = moves.over_hi(rest_sum.tied(held))
    while value_sum.done < value_sum.steps - 1:
        for each in (out_sum, rest_sum, value_sum):
            if each.done < each.steps:
                each.step()
    out_sum.out[0] = value_sum.tied(out_sum.out[0])
    for s in near:
        outputs_back.append(moves.over_plane(value_sum.tied(sums[s][0]), s, back=True))
    last_held = value_sum.tied(last_held)
    for each in (out_sum, rest_sum, value_sum):
        each.run(each.steps - each.done)
    (grad_output,) = out_sum.out
    (grad_value,) = value_sum.out
    *outputs_back, grad_value = tie(*outputs_back, grad_value)
    grad_query, grad_key, grad_vselect, grad_oselect, grad_router = rest_sum.out
    input_delta = middle_delta + norm_back(inputs, att_rms, attention_gain, normed_delta)
    output_rows = middle_rows + sums[home][0].astype(f32)
    for value in outputs_back:
        output_rows = output_rows + value.astype(f32)
    expert_grads = last_held.astype(f32)
    for part in first_parts:
        expert_grads = expert_grads + part.astype(f32)
    grad_up, grad_down = expert_grads[:, :, :FF], jnp.swapaxes(expert_grads[:, :, FF:], 1, 2)
    new_counts = expert_counts + small[2, :experts].astype(jnp.int32)
    return (
        output_rows.astype(bf16)[None],
        input_delta[None],
        small[0],
        grad_query,
        grad_key,
        grad_value,
        grad_vselect,
        grad_oselect,
        grad_output,
        small[1],
        grad_router,
        grad_up,
        grad_down,
        new_counts,
    )


def solution(mesh):
    rows3 = P(("dp", "expert"), None, None)
    placed = (
        rows3,
        P(("dp", "expert"), None),
        P(("dp", "expert"), None, None, None),
        rows3,
        *[P()] * 9,
        rows3,
        rows3,
        P(),
        rows3,
    )
    return jax.shard_map(
        on_device,
        mesh=mesh,
        in_specs=placed,
        out_specs=(rows3, rows3, *[P()] * 9, rows3, rows3, P()),
        check_vma=False,
    )
```

```python
import functools

import jax
import jax.numpy as jnp
from jax import lax
from jax.experimental import pallas as pl
from jax.experimental.pallas import tpu as pltpu
from jax.sharding import PartitionSpec as P

D = 1024
H = 4
DH = 128
NE = 5
FF = 128
TOPK = 16
GATE_LANES = 16

epsilon = 1e-06
masked_value = -1e30
bf16 = jnp.bfloat16
f32 = jnp.float32
tanh_scale = 0.7978845608028654
cubic = 0.044715


def inverse_rms(values):
    return lax.rsqrt(jnp.mean(values * values, axis=-1, keepdims=True) + epsilon)


def norm_back(values, scaling, gain, upstream):
    weighted = upstream * gain
    middle = jnp.mean(values * weighted, axis=-1, keepdims=True)
    return scaling * weighted - values * scaling * scaling * scaling * middle


def input_term(delta, weight):
    return jnp.einsum("tc,dc->td", delta, weight, preferred_element_type=f32)


def contract(left, right, left_dim, right_dim):
    return lax.dot_general(
        left, right, (((left_dim,), (right_dim,)), ((), ())), preferred_element_type=f32
    )


def experts_kernel(blocks, pairs, chained, opened, closed, *refs):
    refs = list(refs)

    def take(count):
        taken = refs[:count]
        del refs[:count]
        return taken

    x_hbm, um_hbm = take(blocks), take(blocks)
    select_ref, router_ref = take(2)
    weights = (take(2), take(2))
    y_prev, dx_prev = take(2) if chained else (None, None)
    gu_prev, gd_prev, gr_prev = take(3) if opened else (None, None, None)
    y_ref, dx_ref = take(2)
    grads = take(2)
    (gr_ref,) = take(1)
    (x_buf, u_buf, m_buf, sems, w_up, w_down, w_sems) = take(7)
    (y_acc, dx_acc, gup, gdown, x_turned, u_turned, gate, delta, gr_acc) = take(9)
    gated_buf, hidden_buf = refs
    step = pl.program_id(0)
    pair = pl.program_id(1)
    slot = lax.rem(step, 2)
    local = pairs // 2

    def copies(index, place):
        return (
            pltpu.make_async_copy(x_hbm[index], x_buf.at[place], sems.at[place, 0]),
            pltpu.make_async_copy(
                um_hbm[index].at[:, pl.ds(0, D)], u_buf.at[place], sems.at[place, 1]
            ),
            pltpu.make_async_copy(
                um_hbm[index].at[:, pl.ds(D, m_buf.shape[2])], m_buf.at[place], sems.at[place, 2]
            ),
        )

    def weight_copies(index):
        place = index % 2
        k = index % local
        ways = []
        for side, weight in enumerate(weights[index // local]):
            for part, buffer in enumerate((w_up, w_down)):
                ways.append(
                    pltpu.make_async_copy(
                        weight.at[k, :, pl.ds(part * FF, FF)],
                        buffer.at[place, :, pl.ds(side * FF, FF)],
                        w_sems.at[place, 2 * side + part],
                    )
                )
        return ways

    @pl.when(jnp.logical_and(step == 0, pair == 0))
    def _():
        for copy in (*copies(0, 0), *weight_copies(0)):
            copy.start()

    for index in range(pairs):

        @pl.when(pair == index)
        def _():
            for copy in weight_copies(index):
                copy.wait()
            if index + 1 < pairs:
                for copy in weight_copies(index + 1):
                    copy.start()
            elif blocks > 1:

                @pl.when(step < blocks - 1)
                def _():
                    for copy in weight_copies(0):
                        copy.start()

    @pl.when(pair == 0)
    def _():
        for number in range(blocks):
            place = number % 2

            @pl.when(step == number)
            def _():
                for copy in copies(number, place):
                    copy.wait()
                if number + 1 < blocks:
                    for copy in copies(number + 1, 1 - place):
                        copy.start()

        x = x_buf[slot]
        x_turned[...] = x.T
        u_turned[...] = u_buf[slot].T
        logits = jnp.dot(x, router_ref[...], preferred_element_type=f32)
        chosen = jnp.dot(m_buf[slot], select_ref[...], preferred_element_type=f32)
        gate[...] = jax.nn.sigmoid(logits) * chosen
        delta[...] = jnp.zeros_like(delta)

    @pl.when(pair == 0)
    def _():
        if chained:
            y_acc[...] = y_prev[...].astype(f32)
            dx_acc[...] = dx_prev[...].astype(f32)
        else:
            y_acc[...] = jnp.zeros_like(y_acc)
            dx_acc[...] = jnp.zeros_like(dx_acc)

    tokens = x_buf.shape[1]
    rows = tokens // 2
    which = lax.rem(pair, 2)
    up = w_up[which]
    down = w_down[which]
    lanes = lax.broadcasted_iota(jnp.int32, (rows, GATE_LANES), 1)
    cuts = [pl.ds(c * rows, rows) for c in range(2)]

    def first(cut):
        pre_act = jnp.dot(x_buf[slot, cut], up, preferred_element_type=f32)
        return pre_act, jnp.dot(u_buf[slot, cut], down, preferred_element_type=f32)

    def bend(cut, pre_act, pulled):
        gates = gate[cut]
        gate_a = jnp.sum(jnp.where(lanes == pair, gates, 0.0), axis=1, keepdims=True)
        gate_b = jnp.sum(jnp.where(lanes == pairs + pair, gates, 0.0), axis=1, keepdims=True)
        spread_gate = jnp.concatenate(
            [jnp.broadcast_to(gate_a, (rows, FF)), jnp.broadcast_to(gate_b, (rows, FF))], axis=1
        )
        square = pre_act * pre_act
        bent = jnp.tanh(pre_act * (tanh_scale + tanh_scale * cubic * square))
        half = 0.5 + 0.5 * bent
        hidden = (pre_act * half).astype(bf16).astype(f32)
        slope = half + (0.5 * pre_act) * (1.0 - bent * bent) * (
            tanh_scale + 3.0 * tanh_scale * cubic * square
        )
        felt = hidden * pulled
        felt_a = jnp.sum(felt[:, :FF], axis=1, keepdims=True)
        felt_b = jnp.sum(felt[:, FF:], axis=1, keepdims=True)
        kept = jnp.where(lanes == pair, felt_a, delta[cut])
        delta[cut] = jnp.where(lanes == pairs + pair, felt_b, kept)
        gated_buf[cut] = (spread_gate * hidden).astype(bf16)
        hidden_buf[cut] = (spread_gate * pulled * slope).astype(bf16)

    def second(cut):
        y_acc[cut] += contract(gated_buf[cut], down, 1, 1)
        dx_acc[cut] += contract(hidden_buf[cut], up, 1, 1)

    ready = first(cuts[0])
    for c, cut in enumerate(cuts):
        later = first(cuts[c + 1]) if c + 1 < 2 else None
        bend(cut, *ready)
        second(cut)
        ready = later
    gd_new = jnp.dot(u_turned[...], gated_buf[...], preferred_element_type=f32)
    gu_new = jnp.dot(x_turned[...], hidden_buf[...], preferred_element_type=f32)

    def put(gu_out, gd_out):
        if closed:
            for side in (0, 1):
                grads[side][0, :, :FF] = gu_out[:, side * FF : (side + 1) * FF].astype(bf16)
                grads[side][0, :, FF:] = gd_out[:, side * FF : (side + 1) * FF].astype(bf16)
        else:
            grads[0][0] = gu_out
            grads[1][0] = gd_out

    if blocks == 1:
        if opened:
            gd_new = gd_prev[0] + gd_new
            gu_new = gu_prev[0] + gu_new
        put(gu_new, gd_new)
    else:

        @pl.when(step == 0)
        def _():
            if opened:
                gdown[pair] = gd_prev[0]
                gup[pair] = gu_prev[0]
            else:
                gdown[pair] = jnp.zeros_like(gd_new)
                gup[pair] = jnp.zeros_like(gu_new)

        gdown[pair] += gd_new
        gup[pair] += gu_new

        @pl.when(step == blocks - 1)
        def _():
            put(gup[pair], gdown[pair])

    @pl.when(pair == pairs - 1)
    def _():
        gates_now = gate[...]
        logit_delta = (delta[...] * gates_now * (1.0 - gates_now)).astype(bf16)
        y_ref[...] = y_acc[...].astype(bf16)
        dx_ref[...] = (dx_acc[...] + contract(logit_delta, router_ref[...], 1, 1)).astype(bf16)
        gr_new = jnp.dot(x_turned[...], logit_delta, preferred_element_type=f32)

        @pl.when(step == 0)
        def _():
            if opened:
                gr_acc[...] = gr_prev[...] + gr_new
            else:
                gr_acc[...] = gr_new

        @pl.when(step > 0)
        def _():
            gr_acc[...] += gr_new

        @pl.when(step == blocks - 1)
        def _():
            gr_ref[...] = gr_acc[...]


def run_experts(xs, ums, select, router, first, second, previous, carried, finish):
    blocks = len(xs)
    local = first[0].shape[0]
    pairs = 2 * local
    tokens = xs[0].shape[0]
    experts = select.shape[0]

    def block(i, j):
        return (i, 0)

    def whole(i, j):
        return (0, 0)

    def opening(i, j):
        return (jnp.where(i == 0, j, pairs - 1), 0, 0)

    def closing(i, j):
        return (jnp.where(i == blocks - 1, j, 0), 0, 0)

    anywhere = pl.BlockSpec(memory_space=pl.ANY)
    in_specs = [anywhere] * (2 * blocks) + [
        pl.BlockSpec((experts, GATE_LANES), whole),
        pl.BlockSpec((D, GATE_LANES), whole),
        *[anywhere] * 4,
    ]
    operands = [*xs, *ums, select, router, *first, *second]
    if previous is not None:
        in_specs += [pl.BlockSpec((tokens, D), block)] * 2
        operands += list(previous)
    if carried is not None:
        in_specs += [
            pl.BlockSpec((1, D, 2 * FF), opening),
            pl.BlockSpec((1, D, 2 * FF), opening),
            pl.BlockSpec((D, GATE_LANES), whole),
        ]
        operands += list(carried)
    out_shape = [jax.ShapeDtypeStruct((blocks * tokens, D), bf16)] * 2
    out_specs = [pl.BlockSpec((tokens, D), block)] * 2
    if finish:
        out_shape += [jax.ShapeDtypeStruct((pairs, D, 2 * FF), bf16)] * 2
    else:
        out_shape += [jax.ShapeDtypeStruct((pairs, D, 2 * FF), f32)] * 2
    out_specs += [pl.BlockSpec((1, D, 2 * FF), closing)] * 2
    out_shape.append(jax.ShapeDtypeStruct((D, GATE_LANES), f32))
    out_specs.append(pl.BlockSpec((D, GATE_LANES), whole))
    kept = pairs if blocks > 1 else 1
    return pl.pallas_call(
        functools.partial(
            experts_kernel, blocks, pairs, previous is not None, carried is not None, finish
        ),
        grid=(blocks, pairs),
        in_specs=in_specs,
        out_specs=out_specs,
        out_shape=out_shape,
        scratch_shapes=[
            pltpu.VMEM((2, tokens, D), bf16),
            pltpu.VMEM((2, tokens, D), bf16),
            pltpu.VMEM((2, tokens, experts), bf16),
            pltpu.SemaphoreType.DMA((2, 3)),
            pltpu.VMEM((2, D, 2 * FF), bf16),
            pltpu.VMEM((2, D, 2 * FF), bf16),
            pltpu.SemaphoreType.DMA((2, 4)),
            pltpu.VMEM((tokens, D), f32),
            pltpu.VMEM((tokens, D), f32),
            pltpu.VMEM((kept, D, 2 * FF), f32),
            pltpu.VMEM((kept, D, 2 * FF), f32),
            pltpu.VMEM((D, tokens), bf16),
            pltpu.VMEM((D, tokens), bf16),
            pltpu.VMEM((tokens, GATE_LANES), f32),
            pltpu.VMEM((tokens, GATE_LANES), f32),
            pltpu.VMEM((D, GATE_LANES), f32),
            pltpu.VMEM((tokens, 2 * FF), bf16),
            pltpu.VMEM((tokens, 2 * FF), bf16),
        ],
        compiler_params=pltpu.CompilerParams(
            dimension_semantics=("arbitrary", "arbitrary"),
            vmem_limit_bytes=56 * 1024 * 1024,
        ),
        cost_estimate=pl.CostEstimate(
            flops=12 * blocks * tokens * D * FF * pairs, bytes_accessed=0, transcendentals=0
        ),
        name="experts",
    )(*operands)


def column(values, index):
    lanes = lax.broadcasted_iota(jnp.int32, values.shape, 1)
    return jnp.sum(jnp.where(lanes == index, values, 0.0), axis=1, keepdims=True)


def head_probs(query, key, segment_col, segment_row):
    raw = contract(query, key, 1, 1) * DH ** (-0.5)
    rows = lax.broadcasted_iota(jnp.int32, raw.shape, 0)
    columns = lax.broadcasted_iota(jnp.int32, raw.shape, 1)
    allowed = jnp.logical_and(columns <= rows, segment_col == segment_row)
    scores = jnp.where(allowed, raw, masked_value)
    powers = jnp.exp(scores - jnp.max(scores, axis=1, keepdims=True))
    return powers * (1.0 / jnp.sum(powers, axis=1, keepdims=True))


def head_sigmoids(head, chosen_ref, sigmoids, expert):
    first, second = chosen_ref[0, :, 0:1], chosen_ref[0, :, 1:2]
    chosen = jnp.logical_or(first == expert, second == expert).astype(f32)
    half = sigmoids.shape[1] // 2
    place = head * NE + expert
    return chosen, column(sigmoids[:, :half], place), column(sigmoids[:, half:], place)


def part(expert):
    return slice(expert * DH, (expert + 1) * DH)


def attend_kernel(
    normed_ref,
    query_weight,
    key_weight,
    value_weight,
    selectors,
    chosen_ref,
    segment_col,
    segment_row,
    query_ref,
    key_ref,
    values_ref,
    low_ref,
    mixed_ref,
    spread_ref,
    sigmoids_ref,
):
    head = pl.program_id(0)
    normed = normed_ref[...]

    @pl.when(head == 0)
    def _():
        sigmoids_ref[...] = jax.nn.sigmoid(
            jnp.dot(normed, selectors[...], preferred_element_type=f32)
        )

    query = jnp.dot(normed, query_weight[...], preferred_element_type=f32).astype(bf16)
    key = jnp.dot(normed, key_weight[...], preferred_element_type=f32).astype(bf16)
    query_ref[...] = query
    key_ref[...] = key
    values_ref[...] = jnp.dot(normed, value_weight[...], preferred_element_type=f32)
    sigmoids = sigmoids_ref[...]
    gates = [head_sigmoids(head, chosen_ref, sigmoids, e) for e in range(NE)]
    low = gates[0][0] * gates[0][1] * values_ref[:, part(0)]
    for e in range(1, NE):
        low = low + gates[e][0] * gates[e][1] * values_ref[:, part(e)]
    low = low.astype(bf16)
    low_ref[...] = low
    probs = head_probs(query, key, segment_col[...], segment_row[...]).astype(bf16)
    mixed = jnp.dot(probs, low, preferred_element_type=f32)
    mixed_ref[...] = mixed
    for e in range(NE):
        spread_ref[:, part(e)] = (gates[e][0] * gates[e][2] * mixed).astype(bf16)


def attend_specs(tokens):
    whole = pl.BlockSpec((tokens, D), lambda h: (0, 0))
    narrow = pl.BlockSpec((tokens, DH), lambda h: (0, h))
    wide = pl.BlockSpec((tokens, NE * DH), lambda h: (0, h))
    rest = [
        pl.BlockSpec((1, tokens, 2), lambda h: (h, 0, 0)),
        pl.BlockSpec((tokens, 1), lambda h: (0, 0)),
        pl.BlockSpec((1, tokens), lambda h: (0, 0)),
    ]
    sigmoids = pl.BlockSpec((tokens, 256), lambda h: (0, 0))
    return whole, narrow, wide, rest, sigmoids


def attend(normed, query_weight, key_weight, value_weight, selectors, chosen, segments):
    tokens = normed.shape[0]
    whole, narrow, wide, rest, sigmoids = attend_specs(tokens)
    return pl.pallas_call(
        attend_kernel,
        grid=(H,),
        in_specs=[
            whole,
            pl.BlockSpec((D, DH), lambda h: (0, h)),
            pl.BlockSpec((D, DH), lambda h: (0, h)),
            pl.BlockSpec((D, NE * DH), lambda h: (0, h)),
            pl.BlockSpec((D, 256), lambda h: (0, 0)),
            *rest,
        ],
        out_specs=[narrow, narrow, wide, narrow, narrow, wide, sigmoids],
        out_shape=[
            jax.ShapeDtypeStruct((tokens, H * DH), bf16),
            jax.ShapeDtypeStruct((tokens, H * DH), bf16),
            jax.ShapeDtypeStruct((tokens, H * NE * DH), f32),
            jax.ShapeDtypeStruct((tokens, H * DH), bf16),
            jax.ShapeDtypeStruct((tokens, H * DH), f32),
            jax.ShapeDtypeStruct((tokens, H * NE * DH), bf16),
            jax.ShapeDtypeStruct((tokens, 256), f32),
        ],
        compiler_params=pltpu.CompilerParams(vmem_limit_bytes=32 * 1024 * 1024),
        cost_estimate=pl.CostEstimate(
            flops=2 * tokens * H * DH * (D * (NE + 2) + 2 * tokens),
            bytes_accessed=0,
            transcendentals=0,
        ),
        name="attend",
    )(
        normed,
        query_weight,
        key_weight,
        value_weight,
        selectors,
        chosen,
        segments[:, None],
        segments[None, :],
    )


def attend_back_kernel(
    middle_ref,
    output_weight,
    query_ref,
    key_ref,
    low_ref,
    mixed_ref,
    values_ref,
    sigmoids_ref,
    chosen_ref,
    segment_col,
    segment_row,
    query_delta,
    key_delta,
    values_delta,
    select_delta,
    spread_buf,
    value_acc,
    output_acc,
):
    head = pl.program_id(0)

    @pl.when(head == 0)
    def _():
        value_acc[...] = jnp.zeros_like(value_acc)
        output_acc[...] = jnp.zeros_like(output_acc)

    spread_buf[...] = contract(middle_ref[...], output_weight[...], 1, 1)
    sigmoids = sigmoids_ref[...]
    gates = [head_sigmoids(head, chosen_ref, sigmoids, e) for e in range(NE)]
    query, key, low = query_ref[...], key_ref[...], low_ref[...]
    mixed = mixed_ref[...]
    mixed_delta = gates[0][0] * gates[0][2] * spread_buf[:, part(0)]
    for e in range(1, NE):
        mixed_delta = mixed_delta + gates[e][0] * gates[e][2] * spread_buf[:, part(e)]
    mixed_delta = mixed_delta.astype(bf16)
    probs = head_probs(query, key, segment_col[...], segment_row[...])
    weight_delta = contract(mixed_delta, low, 1, 1)
    pulled = jnp.sum(probs * weight_delta, axis=1, keepdims=True)
    score_delta = (probs * (weight_delta - pulled)).astype(bf16)
    query_delta[...] = (
        jnp.dot(score_delta, key, preferred_element_type=f32) * DH ** (-0.5)
    ).astype(bf16)
    key_delta[...] = (contract(score_delta, query, 0, 0) * DH ** (-0.5)).astype(bf16)
    value_delta = contract(probs.astype(bf16), mixed_delta, 0, 0)
    lanes = lax.broadcasted_iota(jnp.int32, value_acc.shape, 1)
    for e in range(NE):
        chosen, value_sigmoid, output_sigmoid = gates[e]
        values_delta[:, part(e)] = (chosen * value_sigmoid * value_delta).astype(bf16)
        felt = jnp.sum(value_delta * values_ref[:, part(e)], axis=1, keepdims=True)
        felt = felt * chosen * value_sigmoid * (1.0 - value_sigmoid)
        value_acc[...] = jnp.where(lanes == head * NE + e, felt, value_acc[...])
        felt = jnp.sum(spread_buf[:, part(e)] * mixed, axis=1, keepdims=True)
        felt = felt * chosen * output_sigmoid * (1.0 - output_sigmoid)
        output_acc[...] = jnp.where(lanes == head * NE + e, felt, output_acc[...])

    @pl.when(head == H - 1)
    def _():
        half = value_acc.shape[1]
        select_delta[:, :half] = value_acc[...].astype(bf16)
        select_delta[:, half:] = output_acc[...].astype(bf16)


def attend_back(middle_low, output_weight, query, key, low, mixed, values, sigmoids, chosen, segments):
    tokens = middle_low.shape[0]
    whole, narrow, wide, rest, sigmoid_spec = attend_specs(tokens)
    return pl.pallas_call(
        attend_back_kernel,
        grid=(H,),
        in_specs=[
            whole,
            pl.BlockSpec((NE * DH, D), lambda h: (h, 0)),
            narrow,
            narrow,
            narrow,
            narrow,
            wide,
            sigmoid_spec,
            *rest,
        ],
        out_specs=[narrow, narrow, wide, sigmoid_spec],
        out_shape=[
            jax.ShapeDtypeStruct((tokens, H * DH), bf16),
            jax.ShapeDtypeStruct((tokens, H * DH), bf16),
            jax.ShapeDtypeStruct((tokens, H * NE * DH), bf16),
            jax.ShapeDtypeStruct((tokens, 256), bf16),
        ],
        scratch_shapes=[
            pltpu.VMEM((tokens, NE * DH), f32),
            pltpu.VMEM((tokens, 128), f32),
            pltpu.VMEM((tokens, 128), f32),
        ],
        compiler_params=pltpu.CompilerParams(vmem_limit_bytes=32 * 1024 * 1024),
        cost_estimate=pl.CostEstimate(
            flops=2 * tokens * H * DH * (D * NE + 5 * tokens), bytes_accessed=0, transcendentals=0
        ),
        name="attend_back",
    )(
        middle_low,
        output_weight,
        query,
        key,
        low,
        mixed,
        values,
        sigmoids,
        chosen,
        segments[:, None],
        segments[None, :],
    )


class Moves:
    def __init__(self):
        self.dp = lax.axis_size("dp")
        self.ex = lax.axis_size("expert")
        self.nx = self.dp // 2
        self.nh = self.ex // 2
        self.dp_index = lax.axis_index("dp")
        self.ex_index = lax.axis_index("expert")
        self.core = self.dp_index % 2
        self.x = self.dp_index // 2
        self.lo = self.ex_index % 2
        self.hi = self.ex_index // 2
        steps = [(a, b) for a in range(self.nx) for b in range(2)]
        self.plane = sorted(steps, key=lambda s: ((s[0] > 0) + (s[1] > 0), s))

    def over_core(self, value):
        return lax.ppermute(value, "dp", [(i, i ^ 1) for i in range(self.dp)])

    def over_hi(self, value, by=1):
        pairs = [(i, (i // 2 + by) % self.nh * 2 + i % 2) for i in range(self.ex)]
        return lax.ppermute(value, "expert", pairs)

    def over_plane(self, value, offset, back=False):
        a, b = offset
        if back:
            a = (self.nx - a) % self.nx
        if a == 0:
            return lax.ppermute(value, "expert", [(i, i ^ b) for i in range(self.ex)])
        dp_to = [(i // 2 + a) % self.nx * 2 + i % 2 for i in range(self.dp)]
        if b == 0:
            return lax.ppermute(value, "dp", list(enumerate(dp_to)))
        pairs = [
            (i * self.ex + j, dp_to[i] * self.ex + (j ^ 1))
            for i in range(self.dp)
            for j in range(self.ex)
        ]
        return lax.ppermute(value, ("dp", "expert"), pairs)


def add_low(*terms):
    total = terms[0].astype(f32)
    for term in terms[1:]:
        total = total + term.astype(f32)
    return total.astype(bf16)


def tie(*values):
    return lax.optimization_barrier(values)


class Cube:
    def __init__(self, moves):
        self.moves = moves
        ex = moves.ex
        across = [1 << i for i in range(1, moves.dp.bit_length() - 1)]
        along = [1 << i for i in range(ex.bit_length() - 1)]
        across = [mask * ex for mask in across]
        self.flips = (across + along, along[:1] + across + along[1:])
        self.core_flip = ex
        self.count = moves.dp * ex
        self.bits = len(along) + len(across)
        place = moves.dp_index * ex + moves.ex_index
        corners = []
        for flips in self.flips:
            corner = jnp.int32(0)
            for flip in flips:
                corner = corner * 2 + (place // flip) % 2
            corners.append(corner)
        mine = moves.core == 0
        self.corner = jnp.where(mine, corners[0], corners[1])
        self.partner_corner = jnp.where(mine, corners[1], corners[0])

    def exchange(self, value, stage):
        ex = self.moves.ex
        pairs = [
            (i, i ^ self.flips[i // ex % 2][stage]) for i in range(self.count)
        ]
        return lax.ppermute(value, ("dp", "expert"), pairs)

    def over_core(self, value):
        return self.moves.over_core(value)


def small_cost(flops, moved):
    return pl.CostEstimate(flops=flops, bytes_accessed=moved, transcendentals=0)


def grad_blocks_kernel(steps, group, rows, count, order_ref, left_a, left_b, *refs):
    rights, refs = refs[:count], refs[count:]
    out_a, out_b = refs[-2:]
    added = refs[:-2]
    for which, (left, out) in enumerate(((left_a, out_a), (left_b, out_b))):
        low = order_ref[2 * steps + which]
        turned = left[...]
        start = 0
        for right in rights:
            width = right.shape[1]
            product = contract(turned, right[...], 0, 0)
            for h in range(group):
                out[lax.bitwise_xor(low, h), :, start : start + width] = product[
                    h * rows : (h + 1) * rows
                ].astype(bf16)
            start += width
        if added:
            block = added[which][...]
            width = block.shape[1]
            for h in range(group):
                out[lax.bitwise_xor(low, h), :, start : start + width] = block[
                    h * rows : (h + 1) * rows
                ].astype(bf16)


def grad_blocks(cube, left, rights, added=None):
    n = cube.count
    total = left.shape[1]
    tokens = left.shape[0]
    rows = total // n
    group = 1
    while rows * group % 128:
        group *= 2
    wide = rows * group
    steps = n // 2 // group
    core = cube.moves.core
    order = [core * steps + lax.bitwise_xor(cube.corner // group, i) for i in range(steps)]
    order += [
        (1 - core) * steps + lax.bitwise_xor(cube.partner_corner // group, i) for i in range(steps)
    ]
    order += [cube.corner % group, cube.partner_corner % group]
    order = jnp.stack(order).astype(jnp.int32)
    columns = sum(r.shape[1] for r in rights) + (0 if added is None else added.shape[1])
    in_specs = [
        pl.BlockSpec((tokens, wide), lambda i, o: (0, o[i])),
        pl.BlockSpec((tokens, wide), lambda i, o: (0, o[steps + i])),
        *[pl.BlockSpec(r.shape, lambda i, o: (0, 0)) for r in rights],
    ]
    operands = [left, left, *rights]
    if added is not None:
        in_specs += [
            pl.BlockSpec((wide, added.shape[1]), lambda i, o: (o[i], 0)),
            pl.BlockSpec((wide, added.shape[1]), lambda i, o: (o[steps + i], 0)),
        ]
        operands += [added, added]
    shape = jax.ShapeDtypeStruct((n // 2, rows, columns), bf16)
    return pl.pallas_call(
        functools.partial(grad_blocks_kernel, steps, group, rows, len(rights)),
        grid_spec=pltpu.PrefetchScalarGridSpec(
            num_scalar_prefetch=1,
            grid=(steps,),
            in_specs=in_specs,
            out_specs=[pl.BlockSpec((group, rows, columns), lambda i, o: (i, 0, 0))] * 2,
        ),
        out_shape=[shape, shape],
        compiler_params=pltpu.CompilerParams(vmem_limit_bytes=24 * 1024 * 1024),
        cost_estimate=small_cost(tokens * total * columns, total * columns * 2),
        name="grad_blocks",
    )(order, *operands)


def lanes_of(width):
    return width + -width % 128


def assemble_kernel(count, cuts, order_ref, *refs):
    pieces, outs, buffers = refs[:4], refs[4 : 4 + len(cuts)], refs[4 + len(cuts) :]
    step = pl.program_id(0)
    for index, piece in enumerate(pieces):

        @pl.when(step // 2 == index)
        def _():
            low = order_ref[8 + index // 2]
            rows = piece.shape[1]
            for r in range(count):
                place = lax.bitwise_xor(low, r)
                for out, buffer, (start, width) in zip(outs, buffers, cuts):
                    if width % 128:
                        block = piece[r, :, start : start + lanes_of(width)].astype(f32)
                        buffer[pl.ds(pl.multiple_of(place * rows, rows), rows), :] = block
                    else:
                        out[place] = piece[r, :, start : start + width].astype(f32)
            for out, buffer, (_, width) in zip(outs, buffers, cuts):
                if width % 128:
                    out[...] = buffer[...].T[:width]


def assemble(cube, pieces, cuts):
    n = cube.count
    count = n // 8
    rows, columns = pieces[0].shape[1:]
    order = []
    for core, corner in (
        (cube.moves.core, cube.corner),
        (1 - cube.moves.core, cube.partner_corner),
    ):
        order += [core * 4 + lax.bitwise_xor(corner // count, i) for i in range(4)]
    order += [cube.corner % count, cube.partner_corner % count]
    order = jnp.stack(order).astype(jnp.int32)

    def piece(index):
        return pl.BlockSpec(
            (count, rows, columns), lambda i, o: (jnp.clip(i - 2 * index, 0, 1), 0, 0)
        )

    outs = pl.pallas_call(
        functools.partial(assemble_kernel, count, cuts),
        grid_spec=pltpu.PrefetchScalarGridSpec(
            num_scalar_prefetch=1,
            grid=(8,),
            in_specs=[piece(index) for index in range(4)],
            out_specs=[
                pl.BlockSpec((width, count * rows), lambda i, o: (0, o[i]))
                if width % 128
                else pl.BlockSpec((count, rows, width), lambda i, o: (o[i], 0, 0))
                for _, width in cuts
            ],
            scratch_shapes=[
                pltpu.VMEM((count * rows, lanes_of(width)) if width % 128 else (8, 128), f32)
                for _, width in cuts
            ],
        ),
        out_shape=[
            jax.ShapeDtypeStruct((width, n * rows) if width % 128 else (n, rows, width), f32)
            for _, width in cuts
        ],
        compiler_params=pltpu.CompilerParams(vmem_limit_bytes=24 * 1024 * 1024),
        cost_estimate=small_cost(0, n * rows * columns * 2),
        name="assemble",
    )(order, *pieces)
    return [
        out.T if width % 128 else out.reshape(n * rows, width)
        for out, (_, width) in zip(outs, cuts)
    ]


def add_halves(kept, got):
    half = kept.shape[0] // 2
    return add_low(kept[:half], got[:half]), add_low(kept[half:], got[half:])


class Sum:
    def __init__(self, cube, blocks, cuts):
        self.cube = cube
        self.cuts = cuts
        self.kept, self.sent = blocks
        self.stage = -1

    def step(self):
        cube = self.cube
        stage = self.stage
        self.stage += 1
        if stage < cube.bits:
            got = cube.over_core(self.sent) if stage < 0 else cube.exchange(self.sent, stage)
            if stage == cube.bits - 1:
                self.total = add_low(self.kept, got)
            else:
                self.kept, self.sent = add_halves(self.kept, got)
            return
        back = 2 * cube.bits - 1 - stage
        if back > 0:
            self.total = jnp.concatenate([self.total, cube.exchange(self.total, back)], axis=0)
        elif back == 0:
            self.halves = [self.total, cube.exchange(self.total, 0)]
        else:
            theirs = [cube.over_core(half) for half in self.halves]
            self.out = assemble(cube, [*self.halves, *theirs], self.cuts)

    def tied(self, value):
        if hasattr(self, "halves"):
            *self.halves, value = tie(*self.halves, value)
        elif hasattr(self, "total"):
            self.total, value = tie(self.total, value)
        else:
            self.kept, self.sent, value = tie(self.kept, self.sent, value)
        return value

    @property
    def done(self):
        return self.stage + 1

    def run(self, steps):
        for _ in range(steps):
            self.step()

    @property
    def steps(self):
        return 2 * self.cube.bits + 2


def small_steps(moves):
    steps = []
    for axis, size in (("dp", moves.dp), ("expert", moves.ex)):
        span = 1
        while span < size:
            steps.append((axis, span))
            span *= 2
    return steps


def sum_step(moves, value, axis, span):
    size = moves.dp if axis == "dp" else moves.ex
    return value + lax.ppermute(value, axis, [(i, i ^ span) for i in range(size)])


def on_device(
    hidden_in,
    segment_ids,
    head_experts,
    token_experts,
    attention_gain,
    query_weight,
    key_weight,
    value_weight,
    value_selector,
    output_selector,
    output_weight,
    mixture_gain,
    router_weight,
    up_weight,
    down_weight,
    expert_counts,
    output_cotangent,
):
    moves = Moves()
    nx, nh = moves.nx, moves.nh
    length = hidden_in.shape[1]
    experts = router_weight.shape[1]
    local = up_weight.shape[0]
    expert_range = jnp.arange(experts, dtype=jnp.int32)

    chosen = token_experts[0]
    routed = jnp.sum((chosen[:, :, None] == expert_range[None, None, :]).astype(f32), axis=1)
    local_counts = jnp.sum(routed, axis=0)
    upstream_low = output_cotangent[0]
    near = [s for s in moves.plane[1:] if 0 in s]
    far = [s for s in moves.plane[1:] if 0 not in s]
    routed_low = routed.astype(bf16)

    weights = [jnp.concatenate([up_weight, jnp.swapaxes(down_weight, 1, 2)], axis=2)]
    weights.append(moves.over_hi(weights[0]))
    core_weights = [moves.over_core(weights[0])]
    masks = jnp.pad(routed_low, ((0, 0), (0, -experts % 128)))
    ums = {moves.plane[0]: jnp.concatenate([upstream_low, masks], axis=1)}
    ums[moves.plane[0]], weights[0] = tie(ums[moves.plane[0]], weights[0])
    for s in near:
        ums[s] = moves.over_plane(ums[moves.plane[0]], s)

    inputs = hidden_in[0].astype(f32)
    att_rms = inverse_rms(inputs)
    normed_low = (inputs * att_rms * attention_gain).astype(bf16)
    narrow = 128
    margin = ((0, 0), (0, narrow - H * NE))
    selectors = jnp.concatenate(
        [jnp.pad(value_selector, margin), jnp.pad(output_selector, margin)], axis=1
    )
    head_chosen = jnp.swapaxes(head_experts[0], 0, 1)
    segments = segment_ids[0]
    query_low, key_low, values_all, value_low, mixed, spread_low, sigmoids = attend(
        normed_low, query_weight, key_weight, value_weight, selectors, head_chosen, segments
    )
    middle_rows = inputs + jnp.dot(spread_low, output_weight, preferred_element_type=f32)
    moe_rms = inverse_rms(middle_rows)
    moe_low = (middle_rows * moe_rms * mixture_gain).astype(bf16)

    home = moves.plane[0]
    moe_low, *values = tie(moe_low, *[ums[s] for s in near])
    xs = {home: moe_low}
    for s, value in zip(near, values):
        ums[s] = value
        xs[s] = moves.over_plane(moe_low, s)
    weights[1], xs[home] = tie(weights[1], moe_low)
    core_weights.append(moves.over_core(weights[1]))
    weights.append(moves.over_hi(weights[1]))

    def slot_weights(s):
        return weights[s], core_weights[s]

    def selection(slots):
        columns = []
        for core in (0, 1):
            for s in slots:
                owner = (moves.dp_index ^ core) * moves.ex + (moves.hi - s) % nh * 2 + moves.lo
                columns += [owner * local + k for k in range(local)]
        columns += [jnp.int32(-1)] * (GATE_LANES - len(columns))
        rows = jnp.arange(experts + -experts % 128, dtype=jnp.int32)
        select = (rows[:, None] == jnp.stack(columns)[None, :]).astype(bf16)
        router = jnp.dot(router_weight, select[:experts], preferred_element_type=f32)
        return select, router.astype(bf16)

    sums = {}
    router_sum = jnp.zeros((D, experts + -experts % 128), f32)

    def visit(offsets, phase, carried, finish):
        slots = (2 * phase, 2 * phase + 1)
        select, router = chosen_by[phase]
        previous = None
        if offsets[0] in sums:
            joined = [sums[s] for s in offsets]
            previous = joined[0] if len(joined) == 1 else tuple(
                jnp.concatenate([j[w] for j in joined], axis=0) for w in (0, 1)
            )
        y, dx, *grads = run_experts(
            [xs[s] for s in offsets],
            [ums[s] for s in offsets],
            select,
            router,
            slot_weights(slots[0]),
            slot_weights(slots[1]),
            previous,
            carried,
            finish,
        )
        for k, s in enumerate(offsets):
            sums[s] = (y[k * length : (k + 1) * length], dx[k * length : (k + 1) * length])
        return grads

    phases = nh // 2
    chosen_by = [selection((2 * p, 2 * p + 1)) for p in range(phases)]
    held = None
    sent_back, outputs_back, later = {}, [], []
    for phase in range(phases):
        last = phase == phases - 1
        if phase == 0:
            calls = [[home], *[[s] for s in near], far]
        elif last:
            calls = [[s] for s in far] + [[s] for s in near] + [[home]]
        else:
            calls = [[home], *[[s] for s in near], far]
        grads = None
        for turn, offsets in enumerate(calls):
            grads = visit(offsets, phase, grads, turn == len(calls) - 1)
            if phase == 0 and turn == 0:
                values = tie(grads[0], moe_low, ums[home], *[xs[s] for s in near])
                grads[0], far_x, far_um = values[:3]
                for s, value in zip(near, values[3:]):
                    xs[s] = value
                for s in far:
                    ums[s] = moves.over_plane(far_um, s)
            if phase == 0 and turn == 1:
                grads[0], far_x, *values = tie(grads[0], far_x, *[ums[s] for s in far])
                for s, value in zip(far, values):
                    ums[s] = value
                    xs[s] = moves.over_plane(far_x, s)
            if phase == 0 and turn == 1 and nh > 2:
                grads[0], weights[2] = tie(grads[0], weights[2])
                for s in range(3, nh):
                    weights.append(moves.over_hi(weights[-1]))
                core_weights.append(moves.over_core(weights[2]))
            if phase == 0 and turn == len(calls) - 2 and nh > 2:
                grads[0], core_weights[2] = tie(grads[0], core_weights[2])
                core_weights += [moves.over_core(w) for w in weights[3:]]
            if phase > 0 and turn == 0:
                grads[0], held = tie(grads[0], held)
                held = moves.over_hi(held)
            if phase > 0 and turn == len(calls) - 2:
                grads[0], held = tie(grads[0], held)
            if last:
                if later:
                    grads[0], *late = tie(grads[0], *[sums[s][0] for s in later])
                    for s, value in zip(later, late):
                        if s in far:
                            outputs_back.append(moves.over_plane(value, s, back=True))
                later = [s for s in offsets if s != home]
                for s in later:
                    sent_back[s] = [moves.over_plane(sums[s][1], s, back=True)]
        router_sum = router_sum + jnp.dot(
            grads[2].astype(bf16),
            chosen_by[phase][0].T,
            preferred_element_type=f32,
        )
        mine, got = grads[0], moves.over_core(grads[1])
        if last and phase > 0:
            continue
        for k in range(2):
            s = 2 * phase + k
            parts = [grad[k * local : (k + 1) * local] for grad in (mine, got)]
            if s == 0:
                first_parts = parts
                continue
            if held is not None:
                parts.append(held if k == 0 else moves.over_hi(held))
            held = add_low(*parts)

    expert_delta = sums[home][1].astype(f32)
    for s in moves.plane[1:]:
        expert_delta = expert_delta + sent_back[s][0].astype(f32)

    upstream = upstream_low.astype(f32)
    middle_delta = upstream + norm_back(middle_rows, moe_rms, mixture_gain, expert_delta)
    grad_mixture = jnp.sum(expert_delta * middle_rows * moe_rms, axis=0)
    middle_low = middle_delta.astype(bf16)
    cube = Cube(moves)
    out_sum = Sum(cube, grad_blocks(cube, spread_low, [middle_low]), [(0, D)])
    middle_sent = out_sum.tied(middle_low)
    if phases > 1:
        got, middle_sent = tie(got, middle_sent)
        passed = moves.over_hi(add_low(mine[:local], got[:local], held))
        held = add_low(mine[local:], got[local:], passed)
    out_sum.step()
    query_delta, key_delta, values_delta, select_delta = attend_back(
        middle_sent,
        output_weight,
        query_low,
        key_low,
        value_low,
        mixed,
        values_all,
        sigmoids,
        head_chosen,
        segments,
    )
    out_sum.step()
    held, *outputs_back, values_delta = tie(held, *outputs_back, values_delta)
    values_delta = out_sum.tied(values_delta)
    out_sum.step()
    value_sum = Sum(cube, grad_blocks(cube, normed_low, [values_delta]), [(0, H * NE * DH)])
    value_sum.step()
    query_delta = value_sum.tied(query_delta)
    query_delta = out_sum.tied(query_delta)
    cuts = [(0, H * DH), (H * DH, H * DH)]
    start = 2 * H * DH
    cuts += [(start, H * NE), (start + narrow, H * NE), (start + 2 * narrow, experts)]
    rest_sum = Sum(
        cube,
        grad_blocks(cube, normed_low, [query_delta, key_delta, select_delta], router_sum),
        cuts,
    )
    query_sent = rest_sum.tied(query_delta)
    query_sent = out_sum.tied(query_sent)
    for each in (value_sum, rest_sum, out_sum):
        each.step()
    normed_delta = (
        input_term(query_sent, query_weight)
        + input_term(key_delta, key_weight)
        + input_term(values_delta, value_weight)
        + input_term(select_delta, selectors)
    )
    for each in (rest_sum, out_sum, value_sum):
        normed_delta = each.tied(normed_delta)
    grad_attention = jnp.sum(normed_delta * inputs * att_rms, axis=0)
    small = jnp.stack([grad_attention, grad_mixture, jnp.pad(local_counts, (0, D - experts))])
    for axis, span in small_steps(moves):
        small = rest_sum.tied(out_sum.tied(small))
        small = sum_step(moves, small, axis, span)
        for each in (out_sum, rest_sum, value_sum):
            if each.done < each.steps:
                each.step()
    small = out_sum.tied(small)
    while rest_sum.done < 2 * cube.bits - 1:
        for each in (out_sum, rest_sum, value_sum):
            if each.done < each.steps:
                each.step()
    last_held = moves.over_hi(rest_sum.tied(held))
    while value_sum.done < value_sum.steps - 1:
        for each in (out_sum, rest_sum, value_sum):
            if each.done < each.steps:
                each.step()
    out_sum.out[0] = value_sum.tied(out_sum.out[0])
    for s in near:
        outputs_back.append(moves.over_plane(value_sum.tied(sums[s][0]), s, back=True))
    last_held = value_sum.tied(last_held)
    for each in (out_sum, rest_sum, value_sum):
        each.run(each.steps - each.done)
    (grad_output,) = out_sum.out
    (grad_value,) = value_sum.out
    *outputs_back, grad_value = tie(*outputs_back, grad_value)
    grad_query, grad_key, grad_vselect, grad_oselect, grad_router = rest_sum.out
    input_delta = middle_delta + norm_back(inputs, att_rms, attention_gain, normed_delta)
    output_rows = middle_rows + sums[home][0].astype(f32)
    for value in outputs_back:
        output_rows = output_rows + value.astype(f32)
    expert_grads = last_held.astype(f32)
    for part in first_parts:
        expert_grads = expert_grads + part.astype(f32)
    grad_up, grad_down = expert_grads[:, :, :FF], jnp.swapaxes(expert_grads[:, :, FF:], 1, 2)
    new_counts = expert_counts + small[2, :experts].astype(jnp.int32)
    return (
        output_rows.astype(bf16)[None],
        input_delta[None],
        small[0],
        grad_query,
        grad_key,
        grad_value,
        grad_vselect,
        grad_oselect,
        grad_output,
        small[1],
        grad_router,
        grad_up,
        grad_down,
        new_counts,
    )


def solution(mesh):
    rows3 = P(("dp", "expert"), None, None)
    placed = (
        rows3,
        P(("dp", "expert"), None),
        P(("dp", "expert"), None, None, None),
        rows3,
        *[P()] * 9,
        rows3,
        rows3,
        P(),
        rows3,
    )
    return jax.shard_map(
        on_device,
        mesh=mesh,
        in_specs=placed,
        out_specs=(rows3, rows3, *[P()] * 9, rows3, rows3, P()),
        check_vma=False,
    )
```
